256 devices in a mesh: expert: 32 (over y, z_hi, x), dp: 8 (over z_lo, core).
Axes of the slice: x: 4, y: 4, z: 8 (z_hi: 2, z_lo: 4; z = z_hi * 4 + z_lo), core: 2. Of those that a mesh axis runs over, the one named last changes fastest.
Arguments:
- tokens: bfloat16 [8192, 3584], P('expert'), may hold values from -6 to 6
- expert_ids: int32 [8192, 8], P('expert'), may hold values from 0 to 255, all different within a row; in each aligned block of 256 rows (0 to 255, 256 to 511, ...) at most 16 rows name the same one
- gate_values: float32 [8192, 8], P('expert'), may hold values from 0.1 to 1
- tiles: int32 [32], P('expert'), may hold values from 1 to 2
- w_gate: bfloat16 [32, 3584, 2048], P('expert', None, 'dp'), may hold values from -0.09375 to 0.09375
- w_up: bfloat16 [32, 3584, 2048], P('expert', None, 'dp'), may hold values from -0.09375 to 0.09375
- w_down: bfloat16 [32, 2048, 3584], P('expert', 'dp'), may hold values from -0.125 to 0.125
- grad_out: bfloat16 [8192, 3584], P('expert', 'dp'), may hold values from -6 to 6
Outputs:
- mixed: bfloat16 [8192, 3584], P('expert', 'dp')
- grad_tokens: bfloat16 [8192, 3584], P('expert', 'dp')
- grad_gates: float32 [8192, 8], P('expert')
- grad_w_gate: bfloat16 [32, 3584, 2048], P('expert', None, 'dp')
- grad_w_up: bfloat16 [32, 3584, 2048], P('expert', None, 'dp')
- grad_w_down: bfloat16 [32, 2048, 3584], P('expert', 'dp')
The draws below stay inside these ranges and needn't reach their ends.
Inputs may be any that keep to these rules, and one draw needn't show every extreme that they name: `expert_ids`: each row names 8 different experts. Within the rows of one device (aligned blocks of 256 rows) no expert is named by more than 16 rows.
All inputs are finite; a program needn't handle non-finite values.
Results may differ from the reference program's by a relative error of at most 0.015.
Values may be sent and summed in bfloat16 or wider, within the bound.
A program may use at most 128 MiB of HBM per device.

```python
import math
import jax
import jax.numpy as jnp
import numpy as np
from jax import lax

D = 3584
FF = 2048
ALL_EXPERTS = 256
TOP = 8
TILE = 128
TOK_DEV = 256
SLOTS = 16
EXPERTS = 32
TOKENS = 8192
N_EXPERT = 32


def touch_ends(values, key, least, top_value):
    dims = values.shape
    spot = [jax.random.randint(jax.random.fold_in(key, axis), (), 0, dims[axis]) for axis in range(len(dims))]
    values = values.at[tuple(spot)].set(least)
    longest = dims.index(max(dims))
    spot[longest] = (spot[longest] + 1) % dims[longest]
    return values.at[tuple(spot)].set(top_value)


def block_scale(key, shape, shards, least, largest):
    factor_of, own = 1.0, jax.random.fold_in(key, 6)
    for dim, parts in shards:
        heights = jnp.exp(jax.random.uniform(jax.random.fold_in(own, dim), (parts,), jnp.float32, least / len(shards), largest / len(shards)))
        factor_of = factor_of * jnp.repeat(heights, shape[dim] // parts).reshape([-1 if axis == dim else 1 for axis in range(len(shape))])
    return factor_of


def shared_out(own_key, own, number, rows, count, top, bound, skew):
    order = jax.random.permutation(own_key, count)
    packed, common = load_shares(count, rows * top, bound, skew, True), load_shares(count, rows * top, bound, skew, False)
    places = jnp.arange(count)

    def named(tallies, offset_by):
        used = int((tallies > 0).sum())
        fixed = max(1, used // 4)
        shifted = fixed + (places - fixed + offset_by * (used - fixed)) % max(1, count - fixed)
        return jnp.zeros((count,), jnp.int32).at[order[jnp.where(places < fixed, places, shifted)]].set(jnp.asarray(tallies, jnp.int32))

    tallies = jnp.where(number % 4 == 0, named(packed, number // 4), named(common, number - number // 4 - 1))
    mixed = jax.random.permutation(jax.random.fold_in(own, 3), count)
    source_of, receiver = mixed[0:count // 2 * 2:2], mixed[1:count // 2 * 2:2]
    margin = jnp.minimum(tallies[source_of] - 1, bound - tallies[receiver]) // 2
    margin = jnp.where((source_of == order[0]) | (receiver == order[0]) | (tallies[receiver] == 0), 0, jnp.maximum(margin, 0))
    shifted = jax.random.randint(jax.random.fold_in(own, 4), (count // 2,), 0, 1 << 20) % (margin + 1)
    tallies = tallies.at[source_of].add(-shifted).at[receiver].add(shifted)
    members = jnp.searchsorted(jnp.cumsum(tallies), jnp.arange(rows * top), side="right").astype(jnp.int32)
    table = members.reshape(top, rows).T
    table = table[jax.random.permutation(jax.random.fold_in(own, 1), rows)]
    offset_by = jax.random.randint(jax.random.fold_in(own, 2), (rows, 1), 0, top)
    return jnp.take_along_axis(table, (jnp.arange(top)[None, :] + offset_by) % top, axis=1)


def load_shares(number_of, total, most, slope, full):
    weights = [(1 << 20) // math.isqrt(standing ** slope) + 1 for standing in range(1, number_of + 1)]
    largest = most if full else min(most, max(-(-total // number_of), total * weights[0] // sum(weights)))
    least = 1 if total - largest >= number_of - 1 else 0
    counts, surplus = [largest] + [least] * (number_of - 1), total - largest - least * (number_of - 1)
    while surplus > 0:
        movable = [i for i in range(1, number_of) if counts[i] < largest] or [i for i in range(1, number_of) if counts[i] < most]
        pool, budget = sum([weights[i] for i in movable]), surplus
        for i in movable:
            addition = min(most - counts[i], max(1, budget * weights[i] // pool), surplus)
            counts[i] = counts[i] + addition
            surplus = surplus - addition
    return np.array(counts)


def noise(rng, shape, spread, most, cuts=(), kind=jnp.bfloat16):
    result = jax.random.normal(rng, shape, jnp.float32) * spread
    if len(cuts) > 0:
        result = block_scale(rng, shape, cuts, -0.22, 0.18) * result
    return jnp.clip(result, min=-most, max=most).astype(kind)


def setup_inputs(seed: int = 0) -> dict:
    key_of = jax.random.split(jax.random.key(seed), 9)
    tokens = noise(key_of[0], (TOKENS, D), 1.0, 6.0, ((0, 32),))
    expert_ids_keys = jax.random.split(jax.random.fold_in(key_of[1], 1), TOKENS // TOK_DEV)
    expert_ids_turns = jax.random.permutation(jax.random.fold_in(key_of[1], 3), TOKENS // TOK_DEV)
    expert_ids = jax.vmap(lambda own, number: shared_out(jax.random.fold_in(key_of[1], 2), own, number, TOK_DEV, ALL_EXPERTS, TOP, SLOTS, 2))(expert_ids_keys, expert_ids_turns).reshape((TOKENS, TOP))
    gate_values = jnp.clip(0.1 + 0.9 * jax.random.uniform(key_of[2], (TOKENS, TOP), jnp.float32) ** block_scale(key_of[2], (TOKENS, TOP), ((0, 32),), -0.2, 0.2), 0.1, 1.0)
    tiles = touch_ends(jax.random.randint(key_of[3], (N_EXPERT,), 1, TOK_DEV // TILE + 1), jax.random.fold_in(key_of[3], 1), 1, (TOK_DEV // TILE + 1) - 1).astype(jnp.int32)
    w_gate = noise(key_of[4], (EXPERTS, D, FF), D ** -0.5, 0.09375, ((0, 32), (2, 8)))
    w_up = noise(key_of[5], (EXPERTS, D, FF), D ** -0.5, 0.09375, ((0, 32), (2, 8)))
    w_down = noise(key_of[6], (EXPERTS, FF, D), FF ** -0.5, 0.125, ((0, 32), (1, 8)))
    grad_out = noise(key_of[7], (TOKENS, D), 1.0, 6.0, ((0, 32), (1, 8)))
    return dict(tokens=tokens, expert_ids=expert_ids, gate_values=gate_values, tiles=tiles, w_gate=w_gate, w_up=w_up, w_down=w_down, grad_out=grad_out)


def route_tables(ids, gates, count, experts, slots, tile):
    tok, top = ids.shape
    queue = experts * slots
    live = jnp.arange(tok, dtype=jnp.int32) < count * tile
    valid = (ids < experts) & live[:, None]
    flat_ids = ids.reshape(-1)
    flat_valid = valid.reshape(-1)
    onehot = ((flat_ids[:, None] == jnp.arange(experts, dtype=jnp.int32)[None, :]) & flat_valid[:, None]).astype(jnp.int32)
    ranks = jnp.sum((jnp.cumsum(onehot, axis=0).astype(jnp.int32) - 1) * onehot, axis=1).astype(jnp.int32)
    target = jnp.where(flat_valid, flat_ids * slots + ranks, -1).astype(jnp.int32)
    match = (target[None, :] == jnp.arange(queue, dtype=jnp.int32)[:, None]).astype(jnp.float32)
    picker = jnp.sum(match.reshape(queue, tok, top), axis=2)
    slot_gate = jnp.dot(match, gates.reshape(-1), precision=lax.Precision.HIGHEST)
    return match, picker, slot_gate


def reference(tokens, expert_ids, gate_values, tiles, w_gate, w_up, w_down, grad_out):
    experts = N_EXPERT
    queue = experts * SLOTS
    ids_b = expert_ids.reshape(experts, TOK_DEV, TOP)
    gates_b = gate_values.reshape(experts, TOK_DEV, TOP)
    tok_b = tokens.reshape(experts, TOK_DEV, D)
    dy_b = grad_out.reshape(experts, TOK_DEV, D)

    def gather_source(args):
        ids, gates, count, xs, dys = args
        match, picker, slot_gate = route_tables(ids, gates, count, experts, SLOTS, TILE)
        pick_b = picker.astype(jnp.bfloat16)
        xrows = jnp.dot(pick_b, xs, preferred_element_type=jnp.float32).astype(jnp.bfloat16)
        dy_rows = jnp.dot(pick_b, dys, preferred_element_type=jnp.float32)
        dyrow = (dy_rows * slot_gate[:, None]).astype(jnp.bfloat16)
        return xrows, dyrow

    xrows, dyrows = lax.map(gather_source, (ids_b, gates_b, tiles, tok_b, dy_b))

    def by_expert(a):
        return a.reshape(experts, experts, SLOTS, D).transpose(1, 0, 2, 3).reshape(experts, experts * SLOTS, D)

    def by_source(a):
        return a.reshape(experts, experts, SLOTS, D).transpose(1, 0, 2, 3).reshape(experts, queue, D)

    def one_expert(args):
        rows, dyr, wg, wu, wd = args
        gate_pre = jnp.dot(rows, wg, preferred_element_type=jnp.float32)
        up_pre = jnp.dot(rows, wu, preferred_element_type=jnp.float32)
        sig = jax.nn.sigmoid(gate_pre)
        hidden = (gate_pre * sig * up_pre).astype(jnp.bfloat16)
        yrow = jnp.dot(hidden, wd, preferred_element_type=jnp.float32)
        dh = jnp.dot(dyr, wd.T, preferred_element_type=jnp.float32)
        d_gate = (dh * up_pre * sig * (1.0 + gate_pre * (1.0 - sig))).astype(jnp.bfloat16)
        d_up = (dh * gate_pre * sig).astype(jnp.bfloat16)
        grad_down = jnp.dot(hidden.T, dyr, preferred_element_type=jnp.float32).astype(jnp.bfloat16)
        grad_gate = jnp.dot(rows.T, d_gate, preferred_element_type=jnp.float32).astype(jnp.bfloat16)
        grad_up = jnp.dot(rows.T, d_up, preferred_element_type=jnp.float32).astype(jnp.bfloat16)
        dxrow = jnp.dot(d_gate, wg.T, preferred_element_type=jnp.float32) + jnp.dot(d_up, wu.T, preferred_element_type=jnp.float32)
        return yrow, dxrow, grad_gate, grad_up, grad_down

    yrow, dxrow, grad_w_gate, grad_w_up, grad_w_down = lax.map(one_expert, (by_expert(xrows), by_expert(dyrows), w_gate, w_up, w_down))
    yrow = by_source(yrow)
    dxrow = by_source(dxrow)

    def combine(args):
        ids, gates, count, dys, ys, dxs = args
        match, picker, slot_gate = route_tables(ids, gates, count, experts, SLOTS, TILE)
        weighted = (picker * slot_gate[:, None]).T
        mixed = jnp.dot(weighted, ys, precision=lax.Precision.HIGHEST).astype(jnp.bfloat16)
        dy_rows = jnp.dot(picker.astype(jnp.bfloat16), dys, preferred_element_type=jnp.float32)
        score = jnp.sum(dy_rows * ys, axis=1)
        grad_gates = jnp.dot(score, match, precision=lax.Precision.HIGHEST).reshape(TOK_DEV, TOP)
        grad_tokens = jnp.dot(picker.T, dxs, precision=lax.Precision.HIGHEST).astype(jnp.bfloat16)
        return mixed, grad_tokens, grad_gates

    mixed, grad_tokens, grad_gates = lax.map(combine, (ids_b, gates_b, tiles, dy_b, yrow, dxrow))
    return (mixed.reshape(TOKENS, D), grad_tokens.reshape(TOKENS, D), grad_gates.reshape(TOKENS, TOP),
            grad_w_gate, grad_w_up, grad_w_down)
```

```python
import functools

import jax
import jax.numpy as jnp
from jax import lax
from jax.experimental import pallas as pl
from jax.experimental.pallas import tpu as pltpu
from jax.sharding import PartitionSpec as P

TILE = 128
SL = 16
MESH = pl.DeviceIdType.MESH
VMEM_LIMIT = 60 * 1024 * 1024
BF = jnp.bfloat16
F32 = jnp.float32
ROWBLOCKS = 4


def place(nx):
    e = lax.axis_index("expert")
    d = lax.axis_index("dp")
    x = lax.rem(e, nx)
    zh = lax.rem(lax.div(e, nx), 2)
    y = lax.div(e, 2 * nx)
    return y * nx + x, zh, lax.div(d, 2), lax.rem(d, 2)


def device(nx, q, z, core):
    e = (lax.div(q, nx) * 2 + lax.div(z, 4)) * nx + lax.rem(q, nx)
    return {"expert": e, "dp": lax.rem(z, 4) * 2 + core}


def signal(sem, who):
    pl.semaphore_signal(sem, inc=1, device_id=who, device_id_type=MESH)


def remote(src, dst, send, recv, who):
    return pltpu.make_async_remote_copy(
        src_ref=src, dst_ref=dst, send_sem=send, recv_sem=recv, device_id=who, device_id_type=MESH
    )


def dispatch_kernel(
    nx, nq, tok_ref, gout_ref, tabs_ref, x_ref, dy_ref, tab_ref,
    tok, tabr, dyt, rows, pick, sg,
    tok_l, tab_l, gout_l, row_l, tab_s, tab_r, gout_s, gout_r, x_s, x_r, up_s, down_s, ring_r,
    plane_s, plane_r, sib_s, sib_r,
):
    me, zh, zl, c = place(nx)
    z = zh * 4 + zl
    own = zh == c
    r = lax.rem(z - 4 * c + 8, 8)
    ntok = tok_ref.shape[0]
    ch = gout_ref.shape[1]
    pair = 2 * ch
    ns = nq * SL
    up = device(nx, me, lax.rem(z + 1, 8), c)
    down = device(nx, me, lax.rem(z + 7, 8), c)
    across = device(nx, me, lax.rem(z + 4, 8), c)
    sibling = device(nx, me, z, 1 - c)
    outs = (x_ref, dy_ref)

    barrier = pltpu.get_barrier_semaphore()
    for who in (up, down, across, sibling):
        signal(barrier, who)

    @pl.loop(1, nq)
    def _(i):
        signal(barrier, device(nx, lax.rem(me + i, nq), z, c))

    pl.semaphore_wait(barrier, 4 + nq - 1)

    def tok_in(g):
        return pltpu.make_async_copy(tok_ref.at[:, pl.ds(g * pair, pair)], tok.at[g], tok_l.at[g])

    tab_in = pltpu.make_async_copy(tabs_ref.at[zh], tabr, tab_l)
    tab_out = remote(tabs_ref.at[1 - zh], tabr, tab_s, tab_r, across)
    mine = 2 * zl + c
    gout_in = pltpu.make_async_copy(gout_ref, dyt.at[mine], gout_l)
    gout_out = remote(gout_ref, dyt.at[mine], gout_s, gout_r, sibling)

    def piece(h, i, who):
        step = ntok // ROWBLOCKS
        part = tok.at[2 * h + i // ROWBLOCKS, pl.ds((i % ROWBLOCKS) * step, step)]
        return remote(part, part, x_s.at[h, i], x_r.at[h, i], who)

    def ring(j, who, sems):
        part = dyt.at[pl.ds(2 * j, 2)]
        return remote(part, part, sems.at[j], ring_r.at[j], who)

    pieces = 2 * ROWBLOCKS

    @pl.when(own)
    def _():
        tab_out.start()
        tab_in.start()
        gout_in.start()
        for g in (0, 2, 1, 3):
            tok_in(g).start()
        gout_in.wait()
        gout_out.wait_recv()
        ring(zl, up, up_s).start()
        ring(zl, down, down_s).start()
        for g in (0, 2, 1, 3):
            tok_in(g).wait()
            for i in range(ROWBLOCKS):
                n = (g % 2) * ROWBLOCKS + i
                if g < 2:

                    @pl.when(r == 3)
                    def _():
                        piece(0, n, up).start()
                else:

                    @pl.when(r == 0)
                    def _():
                        piece(1, n, down).start()

        tab_in.wait()

    @pl.when(jnp.logical_not(own))
    def _():
        gout_out.start()
        tab_out.wait_recv()

    rt = tabr[0:nq, :]
    gt = tabr[nq : 2 * nq, :]
    slot = lax.broadcasted_iota(jnp.int32, (nq, SL, ntok), 1).astype(F32)
    hit = jnp.where(jnp.broadcast_to(rt[:, None, :], (nq, SL, ntok)) == slot, 1.0, 0.0)
    pick[...] = hit.reshape(ns, ntok).astype(BF)
    weighted = hit * jnp.broadcast_to(gt[:, None, :], (nq, SL, ntok))
    sg[...] = jnp.broadcast_to(jnp.sum(weighted.reshape(ns, ntok), axis=1, keepdims=True), sg.shape)
    tab_ref[...] = tabr[...]

    def send_rows(t, g):
        @pl.loop(1, nq)
        def _(i):
            q = lax.rem(me + i, nq)
            remote(
                rows.at[t, g, pl.ds(pl.multiple_of(q * SL, SL), SL)],
                outs[t].at[g, pl.ds(pl.multiple_of(c * ns + me * SL, SL), SL)],
                plane_s.at[t, g], plane_r.at[t, g], device(nx, q, z, c),
            ).start()

        row_local(t, g).start()

    def row_local(t, g):
        return pltpu.make_async_copy(
            rows.at[t, g, pl.ds(pl.multiple_of(me * SL, SL), SL)],
            outs[t].at[g, pl.ds(pl.multiple_of(c * ns + me * SL, SL), SL)],
            row_l.at[t, g],
        )

    def x_group(g):
        rows[0, g] = jnp.dot(pick[...], tok[g], preferred_element_type=F32).astype(BF)
        send_rows(0, g)

    def dy_group(g):
        a = jnp.dot(pick[...], dyt[2 * g], preferred_element_type=F32)
        b = jnp.dot(pick[...], dyt[2 * g + 1], preferred_element_type=F32)
        both = jnp.concatenate([a, b], axis=1)
        rows[1, g] = (both * sg[:, 0:1]).astype(BF)
        send_rows(1, g)

    @pl.when(own)
    def _():
        @pl.loop(0, 4)
        def _(g):
            x_group(g)

        dy_group(zl)

    @pl.when(jnp.logical_not(own))
    def _():
        for i in range(pieces):
            piece(0, i, up).wait_recv()

            @pl.when(r < 7)
            def _():
                piece(0, i, up).start()

            piece(1, i, down).wait_recv()

            @pl.when(r > 4)
            def _():
                piece(1, i, down).start()

            if i % ROWBLOCKS == ROWBLOCKS - 1:
                x_group(i // ROWBLOCKS)
                x_group(2 + i // ROWBLOCKS)

    @pl.loop(1, 5)
    def _(k):
        ju = lax.rem(r - k + 8, 8)
        jd = lax.rem(r + k, 8)
        from_below = ju < 4
        from_above = jnp.logical_and(jd < 4, k < 4)

        @pl.when(from_below)
        def _():
            ring(ju, up, up_s).wait_recv()

            @pl.when(k < 4)
            def _():
                ring(ju, up, up_s).start()

        @pl.when(from_above)
        def _():
            ring(jd, down, down_s).wait_recv()

            @pl.when(k < 3)
            def _():
                ring(jd, down, down_s).start()

        @pl.when(from_below)
        def _():
            dy_group(ju)

        @pl.when(from_above)
        def _():
            dy_group(jd)

    def share(t, g):
        part = outs[t].at[g, pl.ds(pl.multiple_of(c * ns, SL), ns)]
        return remote(part, part, sib_s.at[t, g], sib_r.at[t, g], sibling)

    def arrived(t, g):
        part = rows.at[t, g, pl.ds(0, ns - SL)]
        return remote(part, outs[t].at[g, pl.ds(0, ns - SL)], plane_s.at[t, g], plane_r.at[t, g], sibling)

    for t in range(2):

        @pl.loop(0, 4)
        def _(g):
            arrived(t, g).wait_recv()
            row_local(t, g).wait()
            share(t, g).start()

    for t in range(2):

        @pl.loop(0, 4)
        def _(g):
            share(t, g).wait_recv()
            share(t, g).wait_send()
            arrived(t, g).wait_send()

    @pl.when(own)
    def _():
        tab_out.wait_send()

    @pl.when(jnp.logical_not(own))
    def _():
        gout_out.wait_send()

    for i in range(pieces):

        @pl.when(jnp.logical_and(r >= 3, r < 7))
        def _():
            piece(0, i, up).wait_send()

        @pl.when(jnp.logical_or(r == 0, r > 4))
        def _():
            piece(1, i, down).wait_send()

    @pl.loop(0, 4)
    def _(j):
        @pl.when(lax.rem(r - j + 8, 8) < 4)
        def _():
            ring(j, up, up_s).wait_send()

        @pl.when(lax.rem(j - r + 8, 8) < 3)
        def _():
            ring(j, down, down_s).wait_send()


def dispatch(nx, nq, tokens, gout, tabs):
    ntok, width = tokens.shape
    ch = gout.shape[1]
    ns = nq * SL
    hbm = pl.BlockSpec(memory_space=pl.ANY)
    dma = pltpu.SemaphoreType.DMA
    big = jax.ShapeDtypeStruct((4, 2 * ns, 2 * ch), BF)
    return pl.pallas_call(
        functools.partial(dispatch_kernel, nx, nq),
        out_shape=(big, big, jax.ShapeDtypeStruct((2 * nq, ntok), F32)),
        in_specs=[hbm, hbm, hbm],
        out_specs=(hbm, hbm, pl.BlockSpec(memory_space=pltpu.VMEM)),
        scratch_shapes=[
            pltpu.VMEM((4, ntok, 2 * ch), BF),
            pltpu.VMEM((2 * nq, ntok), F32),
            pltpu.VMEM((8, ntok, ch), BF),
            pltpu.VMEM((2, 4, ns, 2 * ch), BF),
            pltpu.VMEM((ns, ntok), BF),
            pltpu.VMEM((ns, 128), F32),
            dma((4,)), dma, dma, dma((2, 4)), dma, dma, dma, dma,
            dma((2, 2 * ROWBLOCKS)), dma((2, 2 * ROWBLOCKS)), dma((4,)), dma((4,)), dma((4,)),
            dma((2, 4)), dma((2, 4)), dma((2, 4)), dma((2, 4)),
        ],
        compiler_params=pltpu.CompilerParams(
            collective_id=1, has_side_effects=True, vmem_limit_bytes=VMEM_LIMIT
        ),
        name="dispatch",
    )(tokens, gout, tabs)


def tdot(a, b):
    return lax.dot_general(a, b, (((0,), (0,)), ((), ())), preferred_element_type=F32)


def dot_t(a, b):
    return lax.dot_general(a, b, (((1,), (1,)), ((), ())), preferred_element_type=F32)


def expert_kernel(x, dy, wg, wu, wd, y, dx, sc, gwg, gwu, gwd):
    groups, _, pair = x.shape

    def total(f):
        acc = f(0)
        for k in range(1, groups):
            acc = acc + f(k)
        return acc

    g = total(lambda k: jnp.dot(x[k], wg[k], preferred_element_type=F32))
    u = total(lambda k: jnp.dot(x[k], wu[k], preferred_element_type=F32))
    sig = jax.nn.sigmoid(g)
    gs = g * sig
    h = (gs * u).astype(BF)
    dh = total(lambda k: dot_t(dy[k], wd[:, k * pair : (k + 1) * pair]))
    dg = (dh * u * sig * (1.0 + g * (1.0 - sig))).astype(BF)
    du = (dh * gs).astype(BF)
    part = h.astype(F32) * dh
    hi = part.astype(BF)
    lo = (part - hi.astype(F32)).astype(BF)
    ones = jnp.ones((8, part.shape[1]), BF)
    sc[...] = (dot_t(ones, hi) + dot_t(ones, lo))[0:1, :]
    for k in range(groups):
        lanes = slice(k * pair, (k + 1) * pair)
        y[k] = jnp.dot(h, wd[:, lanes], preferred_element_type=F32).astype(BF)
        dx[k] = (dot_t(dg, wg[k]) + dot_t(du, wu[k])).astype(BF)
        gwd[:, lanes] = tdot(h, dy[k]).astype(BF)
        gwg[k] = tdot(x[k], dg).astype(BF)
        gwu[k] = tdot(x[k], du).astype(BF)


def expert(x, dy, wg, wu, wd):
    s = jax.ShapeDtypeStruct
    return pl.pallas_call(
        expert_kernel,
        out_shape=(
            s(x.shape, BF), s(x.shape, BF), s((1, x.shape[1]), F32),
            s(wg.shape, BF), s(wu.shape, BF), s(wd.shape, BF),
        ),
        in_specs=[pl.BlockSpec(memory_space=pltpu.VMEM)] * 5,
        out_specs=(pl.BlockSpec(memory_space=pltpu.VMEM),) * 6,
        compiler_params=pltpu.CompilerParams(vmem_limit_bytes=VMEM_LIMIT),
        name="expert",
    )(x, dy, wg, wu, wd)


def combine_kernel(
    nx, nq, y_ref, dx_ref, sc_ref, tab_ref, mixed_ref, gtok_ref, rsc_ref,
    ob, rb, sb, rv, tp, rsd, rsu, fin, fo, wt, scr, st, rsc,
    ob_l, sib_s, sib_r, row_l, plane_s, plane_r, ring_s, down_r, up_r, fin_s, fin_r,
    dp_s, dp_r, ex_s, ex_r,
):
    me, zh, zl, c = place(nx)
    z = zh * 4 + zl
    own = zh == c
    r = lax.rem(z - 4 * c + 8, 8)
    ns = nq * SL
    ntok = tab_ref.shape[1]
    pair = y_ref.shape[2]
    ch = pair // 2
    d = 2 * zl + c
    e = lax.axis_index("expert")
    ne = 2 * nq
    up = device(nx, me, lax.rem(z + 1, 8), c)
    down = device(nx, me, lax.rem(z + 7, 8), c)
    sibling = device(nx, me, z, 1 - c)
    srcs = (y_ref, dx_ref)
    outs = (mixed_ref, gtok_ref)

    barrier = pltpu.get_barrier_semaphore()
    signal(barrier, up)
    signal(barrier, down)

    @pl.loop(1, 8)
    def _(i):
        signal(barrier, {"expert": e, "dp": lax.rem(d + i, 8)})

    @pl.loop(1, ne)
    def _(i):
        signal(barrier, {"expert": lax.rem(e + i, ne), "dp": d})

    pl.semaphore_wait(barrier, 2 + 7 + ne - 1)

    def own_rows(t, g):
        return pltpu.make_async_copy(
            srcs[t].at[g, pl.ds(pl.multiple_of(c * ns, SL), ns)], ob.at[t, g], ob_l.at[t, g]
        )

    def to_sibling(t, g):
        return remote(
            srcs[t].at[g, pl.ds(pl.multiple_of((1 - c) * ns, SL), ns)], rb.at[t, g],
            sib_s.at[t, g], sib_r.at[t, g], sibling,
        )

    scr[pl.ds(d, 1)] = sc_ref[...][None]

    @pl.loop(1, 8)
    def _(i):
        remote(sc_ref, scr.at[d], dp_s, dp_r, {"expert": e, "dp": lax.rem(d + i, 8)}).start()

    for t in range(2):

        @pl.loop(0, 4)
        def _(g):
            own_rows(t, g).start()
            to_sibling(t, g).start()

    rt = tab_ref[0:nq, :]
    gt = tab_ref[nq : 2 * nq, :]
    slot = lax.broadcasted_iota(jnp.int32, (nq, SL, ntok), 1).astype(F32)
    hit = jnp.where(jnp.broadcast_to(rt[:, None, :], (nq, SL, ntok)) == slot, 1.0, 0.0)
    heavy = (hit * jnp.broadcast_to(gt[:, None, :], (nq, SL, ntok))).reshape(ns, ntok).T
    top = heavy.astype(BF)
    wt[0] = top
    wt[1] = (heavy - top.astype(F32)).astype(BF)
    wt[2] = hit.reshape(ns, ntok).T.astype(BF)

    def row_local(t, g):
        rows = pl.ds(pl.multiple_of(me * SL, SL), SL)
        return pltpu.make_async_copy(sb.at[t, g, rows], rv.at[t, g, rows], row_l.at[t, g])

    def arrived(t, g):
        some = pl.ds(0, ns - SL)
        return remote(sb.at[t, g, some], rv.at[t, g, some], plane_s.at[t, g], plane_r.at[t, g], sibling)

    def plane(t, g):
        own_rows(t, g).wait()
        to_sibling(t, g).wait_recv()
        sb[t, g] = (ob[t, g].astype(F32) + rb[t, g].astype(F32)).astype(BF)

        @pl.loop(1, nq)
        def _(i):
            q = lax.rem(me + i, nq)
            remote(
                sb.at[t, g, pl.ds(pl.multiple_of(q * SL, SL), SL)],
                rv.at[t, g, pl.ds(pl.multiple_of(me * SL, SL), SL)],
                plane_s.at[t, g], plane_r.at[t, g], device(nx, q, z, c),
            ).start()

        row_local(t, g).start()

    @pl.loop(0, 4)
    def _(g):
        plane(0, g)

    def all_but_one(a):
        return a.at[pl.ds(0, 7)]

    dp_all = remote(all_but_one(scr), all_but_one(scr), dp_s, dp_r, sibling)
    dp_all.wait_recv()
    st[...] = jnp.sum(scr[...], axis=0)
    rsc[pl.ds(e, 1)] = st[...][None]

    @pl.loop(1, ne)
    def _(i):
        remote(st, rsc.at[e], ex_s, ex_r, {"expert": lax.rem(e + i, ne), "dp": d}).start()

    @pl.loop(0, 4)
    def _(g):
        plane(1, g)

    def send_down(t, j):
        return remote(tp.at[t, j], rsd.at[t, j], ring_s.at[t, j], down_r.at[t, j], down)

    def send_up(t, j):
        return remote(tp.at[t, j], rsu.at[t, j], ring_s.at[t, j], up_r.at[t, j], up)

    for t in range(2):

        @pl.loop(0, 4)
        def _(g):
            arrived(t, g).wait_recv()
            row_local(t, g).wait()
            if t == 0:
                part = jnp.dot(wt[0], rv[t, g], preferred_element_type=F32)
                part = part + jnp.dot(wt[1], rv[t, g], preferred_element_type=F32)
            else:
                part = jnp.dot(wt[2], rv[t, g], preferred_element_type=F32)
            tp[t, g] = part.astype(BF)

            @pl.when(lax.rem(r - g + 8, 8) == 4)
            def _():
                send_down(t, g).start()

            @pl.when(lax.rem(g - r + 8, 8) == 3)
            def _():
                send_up(t, g).start()

        @pl.loop(1, 4)
        def _(n):
            k = 4 - n
            ju = lax.rem(r - k + 8, 8)
            jd = lax.rem(r + k, 8)

            @pl.when(ju < 4)
            def _():
                send_down(t, ju).wait_recv()
                tp[t, ju] = (tp[t, ju].astype(F32) + rsd[t, ju].astype(F32)).astype(BF)
                send_down(t, ju).start()

            @pl.when(jnp.logical_and(jd < 4, k < 3))
            def _():
                send_up(t, jd).wait_recv()
                tp[t, jd] = (tp[t, jd].astype(F32) + rsu[t, jd].astype(F32)).astype(BF)
                send_up(t, jd).start()

        final = remote(fin.at[t], fo.at[t], fin_s.at[t], fin_r.at[t], sibling)

        @pl.when(own)
        def _():
            send_down(t, zl).wait_recv()
            send_up(t, zl).wait_recv()
            whole = tp[t, zl].astype(F32) + rsd[t, zl].astype(F32) + rsu[t, zl].astype(F32)
            low = whole[:, :ch]
            high = pltpu.roll(whole, ch, 1)[:, :ch]
            first = c == 0
            outs[t][...] = jnp.where(first, low, high).astype(BF)
            fin[t] = jnp.where(first, high, low).astype(BF)
            final.start()

    for t in range(2):
        final = remote(fin.at[t], fo.at[t], fin_s.at[t], fin_r.at[t], sibling)

        @pl.when(own)
        def _():
            final.wait_send()

        @pl.when(jnp.logical_not(own))
        def _():
            final.wait_recv()
            outs[t][...] = fo[t]

    some = pl.ds(0, ne - 1)
    ex_all = remote(rsc.at[some], rsc.at[some], ex_s, ex_r, sibling)
    ex_all.wait_recv()
    rsc_ref[...] = rsc[...]
    ex_all.wait_send()
    dp_all.wait_send()
    for t in range(2):

        @pl.loop(0, 4)
        def _(g):
            to_sibling(t, g).wait_send()
            arrived(t, g).wait_send()

            @pl.when(g != r)
            def _():
                send_down(t, g).wait_send()


def combine(nx, nq, ch, ntok, y, dx, sc, tab):
    ns = nq * SL
    pair = 2 * ch
    hbm = pl.BlockSpec(memory_space=pl.ANY)
    vm = pl.BlockSpec(memory_space=pltpu.VMEM)
    dma = pltpu.SemaphoreType.DMA
    s = jax.ShapeDtypeStruct
    wide = pltpu.VMEM((2, 4, ns, pair), BF)
    tall = pltpu.VMEM((2, 4, ntok, pair), BF)
    return pl.pallas_call(
        functools.partial(combine_kernel, nx, nq),
        out_shape=(s((ntok, ch), BF), s((ntok, ch), BF), s((2 * nq, 1, 2 * ns), F32)),
        in_specs=[hbm, hbm, vm, vm],
        out_specs=(vm, vm, vm),
        scratch_shapes=[
            wide, wide, wide, wide, tall, tall, tall,
            pltpu.VMEM((2, ntok, ch), BF), pltpu.VMEM((2, ntok, ch), BF),
            pltpu.VMEM((3, ntok, ns), BF),
            pltpu.VMEM((8, 1, 2 * ns), F32), pltpu.VMEM((1, 2 * ns), F32), pltpu.VMEM((2 * nq, 1, 2 * ns), F32),
            dma((2, 4)), dma((2, 4)), dma((2, 4)), dma((2, 4)), dma((2, 4)), dma((2, 4)),
            dma((2, 4)), dma((2, 4)), dma((2, 4)), dma((2,)), dma((2,)),
            dma, dma, dma, dma,
        ],
        compiler_params=pltpu.CompilerParams(
            collective_id=2, has_side_effects=True, vmem_limit_bytes=VMEM_LIMIT
        ),
        name="combine",
    )(y, dx, sc, tab)


def on_device(nx, tokens, expert_ids, gate_values, tiles, w_gate, w_up, w_down, grad_out):
    ne = lax.axis_size("expert")
    nq = ne // 2
    ntok, width = tokens.shape
    ch = grad_out.shape[1]
    pair = 2 * ch
    live = jnp.arange(ntok, dtype=jnp.int32) < tiles[0] * TILE
    names = jnp.arange(ne, dtype=jnp.int32)[:, None, None]
    chosen = (expert_ids.T[None] == names) & live[None, None, :]
    named = jnp.any(chosen, axis=1)
    earlier = jnp.arange(ntok)[:, None] < jnp.arange(ntok)[None, :]
    rank = jnp.dot(named.astype(BF), earlier.astype(BF), preferred_element_type=F32)
    rank = jnp.where(named, rank, -1.0)
    gate = jnp.sum(jnp.where(chosen, gate_values.T[None], 0.0), axis=1)

    def halves(a):
        return a.reshape(nq // nx, 2, nx, ntok).transpose(1, 0, 2, 3).reshape(2, nq, ntok)

    tabs = jnp.concatenate([halves(rank), halves(gate)], axis=1)
    x, dy, tab = dispatch(nx, nq, tokens, grad_out, tabs)
    fh = w_gate.shape[2]
    wg = w_gate.reshape(4, pair, fh)
    wu = w_up.reshape(4, pair, fh)
    y, dx, sc, gwg, gwu, gwd = expert(x, dy, wg, wu, w_down[0])
    mixed, gtok, rsc = combine(nx, nq, ch, ntok, y, dx, sc, tab)
    e = lax.axis_index("expert")
    zh = (e // nx) % 2
    me = (e // (2 * nx)) * nx + e % nx
    mine = lax.dynamic_slice(rsc[:, 0, :], (0, zh * nq * SL + me * SL), (ne, SL))
    slots = jnp.arange(SL, dtype=F32)
    at = jnp.sum(jnp.where(rank[:, None, :] == slots[None, :, None], mine[:, :, None], 0.0), axis=1)
    at = jnp.where(named, at / jnp.where(named, gate, 1.0), 0.0)
    grad_gates = jnp.sum(jnp.where(chosen, at[:, None, :], 0.0), axis=0).T
    return (
        mixed, gtok, grad_gates,
        gwg.reshape(1, width, fh), gwu.reshape(1, width, fh), gwd[None],
    )


def build(mesh, nx):
    placed = (
        P("expert", None),
        P("expert", None),
        P("expert", None),
        P("expert"),
        P("expert", None, "dp"),
        P("expert", None, "dp"),
        P("expert", "dp", None),
        P("expert", "dp"),
    )
    return jax.shard_map(
        functools.partial(on_device, nx),
        mesh=mesh,
        in_specs=placed,
        out_specs=(
            P("expert", "dp"),
            P("expert", "dp"),
            P("expert", None),
            P("expert", None, "dp"),
            P("expert", None, "dp"),
            P("expert", "dp", None),
        ),
        check_vma=False,
    )


def solution(mesh):
    return build(mesh, 4)
```

```python
import functools

import jax
import jax.numpy as jnp
from jax import lax
from jax.experimental import pallas as pl
from jax.experimental.pallas import tpu as pltpu
from jax.sharding import PartitionSpec as P

TILE = 128
SL = 16
MESH = pl.DeviceIdType.MESH
VMEM_LIMIT = 60 * 1024 * 1024
BF = jnp.bfloat16
F32 = jnp.float32
ROWBLOCKS = 4


def place(nx):
    e = lax.axis_index("expert")
    d = lax.axis_index("dp")
    x = lax.rem(e, nx)
    zh = lax.rem(lax.div(e, nx), 2)
    y = lax.div(e, 2 * nx)
    return y * nx + x, zh, lax.div(d, 2), lax.rem(d, 2)


def device(nx, q, z, core):
    e = (lax.div(q, nx) * 2 + lax.div(z, 4)) * nx + lax.rem(q, nx)
    return {"expert": e, "dp": lax.rem(z, 4) * 2 + core}


def signal(sem, who):
    pl.semaphore_signal(sem, inc=1, device_id=who, device_id_type=MESH)


def remote(src, dst, send, recv, who):
    return pltpu.make_async_remote_copy(
        src_ref=src, dst_ref=dst, send_sem=send, recv_sem=recv, device_id=who, device_id_type=MESH
    )


def dispatch_kernel(
    nx, nq, tok_ref, gout_ref, tabs_ref, x_ref, dy_ref, tab_ref,
    tok, tabr, dyt, rows, pick, sg,
    tok_l, tab_l, gout_l, row_l, tab_s, tab_r, gout_s, gout_r, x_s, x_r, up_s, down_s, ring_r,
    plane_s, plane_r, sib_s, sib_r,
):
    me, zh, zl, c = place(nx)
    z = zh * 4 + zl
    own = zh == c
    r = lax.rem(z - 4 * c + 8, 8)
    ntok = tok_ref.shape[0]
    ch = gout_ref.shape[0]
    pair = 2 * ch
    ns = nq * SL
    up = device(nx, me, lax.rem(z + 1, 8), c)
    down = device(nx, me, lax.rem(z + 7, 8), c)
    across = device(nx, me, lax.rem(z + 4, 8), c)
    sibling = device(nx, me, z, 1 - c)
    outs = (x_ref, dy_ref)

    barrier = pltpu.get_barrier_semaphore()
    for who in (up, down, across, sibling):
        signal(barrier, who)

    @pl.loop(1, nq)
    def _(i):
        signal(barrier, device(nx, lax.rem(me + i, nq), z, c))

    pl.semaphore_wait(barrier, 4 + nq - 1)

    def tok_in(g):
        return pltpu.make_async_copy(tok_ref.at[:, pl.ds(g * pair, pair)], tok.at[g], tok_l.at[g])

    tab_in = pltpu.make_async_copy(tabs_ref.at[zh], tabr, tab_l)
    tab_out = remote(tabs_ref.at[1 - zh], tabr, tab_s, tab_r, across)
    mine = dyt.at[zl, pl.ds(pl.multiple_of(c * ch, SL), ch)]
    gout_in = pltpu.make_async_copy(gout_ref, mine, gout_l)
    gout_out = remote(gout_ref, mine, gout_s, gout_r, sibling)

    def piece(h, i, who):
        step = ntok // ROWBLOCKS
        first = pl.multiple_of(lax.rem(i, ROWBLOCKS) * step, step)
        part = tok.at[2 * h + lax.div(i, ROWBLOCKS), pl.ds(first, step)]
        return remote(part, part, x_s.at[h, i], x_r.at[h, i], who)

    def ring(j, who, sems):
        part = dyt.at[j]
        return remote(part, part, sems.at[j], ring_r.at[j], who)

    pieces = 2 * ROWBLOCKS

    @pl.when(own)
    def _():
        tab_out.start()
        tab_in.start()
        gout_in.start()
        for g in (0, 2, 1, 3):
            tok_in(g).start()
        gout_in.wait()
        gout_out.wait_recv()
        ring(zl, up, up_s).start()
        ring(zl, down, down_s).start()
        for g in (0, 2, 1, 3):
            tok_in(g).wait()
            for i in range(ROWBLOCKS):
                n = (g % 2) * ROWBLOCKS + i
                if g < 2:

                    @pl.when(r == 3)
                    def _():
                        piece(0, n, up).start()
                else:

                    @pl.when(r == 0)
                    def _():
                        piece(1, n, down).start()

        tab_in.wait()

    @pl.when(jnp.logical_not(own))
    def _():
        gout_out.start()
        tab_out.wait_recv()

    rt = tabr[0:nq, :]
    gt = tabr[nq : 2 * nq, :]
    slot = lax.broadcasted_iota(jnp.int32, (nq, SL, ntok), 1).astype(F32)
    hit = jnp.where(jnp.broadcast_to(rt[:, None, :], (nq, SL, ntok)) == slot, 1.0, 0.0)
    pick[...] = hit.reshape(ns, ntok).astype(BF)
    weighted = hit * jnp.broadcast_to(gt[:, None, :], (nq, SL, ntok))
    sg[...] = jnp.broadcast_to(jnp.sum(weighted.reshape(ns, ntok), axis=1, keepdims=True), sg.shape)
    tab_ref[...] = tabr[...]

    def send_rows(t, g):
        @pl.loop(1, nq)
        def _(i):
            q = lax.rem(me + i, nq)
            remote(
                rows.at[t, g, pl.ds(pl.multiple_of(q * SL, SL), SL)],
                outs[t].at[g, pl.ds(pl.multiple_of(c * ns + me * SL, SL), SL)],
                plane_s.at[t, g], plane_r.at[t, g], device(nx, q, z, c),
            ).start()

        row_local(t, g).start()

    def row_local(t, g):
        return pltpu.make_async_copy(
            rows.at[t, g, pl.ds(pl.multiple_of(me * SL, SL), SL)],
            outs[t].at[g, pl.ds(pl.multiple_of(c * ns + me * SL, SL), SL)],
            row_l.at[t, g],
        )

    def x_group(g):
        rows[0, g] = jnp.dot(pick[...], tok[g], preferred_element_type=F32).astype(BF)
        send_rows(0, g)

    def dy_group(g):
        rows[1, g] = (dot_t(pick[...], dyt[g]) * sg[:, 0:1]).astype(BF)
        send_rows(1, g)

    @pl.when(own)
    def _():
        @pl.loop(0, 4)
        def _(g):
            x_group(g)

        dy_group(zl)

    @pl.when(jnp.logical_not(own))
    def _():
        @pl.loop(1, pieces + 4)
        def _(n):
            for h, far, who in ((0, r - 3, up), (1, 8 - r, down)):
                i = n - far

                @pl.when(jnp.logical_and(i >= 0, i < pieces))
                def _():
                    piece(h, i, who).wait_recv()

                    @pl.when(far < 4)
                    def _():
                        piece(h, i, who).start()

            for h, far in ((0, r - 3), (1, 8 - r)):
                i = n - far
                whole = lax.rem(i + ROWBLOCKS, ROWBLOCKS) == ROWBLOCKS - 1

                @pl.when(jnp.logical_and(jnp.logical_and(i >= 0, i < pieces), whole))
                def _():
                    x_group(2 * h + lax.div(i, ROWBLOCKS))

    @pl.loop(1, 5)
    def _(k):
        ju = lax.rem(r - k + 8, 8)
        jd = lax.rem(r + k, 8)
        from_below = ju < 4
        from_above = jnp.logical_and(jd < 4, k < 4)

        @pl.when(from_below)
        def _():
            ring(ju, up, up_s).wait_recv()

            @pl.when(k < 4)
            def _():
                ring(ju, up, up_s).start()

        @pl.when(from_above)
        def _():
            ring(jd, down, down_s).wait_recv()

            @pl.when(k < 3)
            def _():
                ring(jd, down, down_s).start()

        @pl.when(from_below)
        def _():
            dy_group(ju)

        @pl.when(from_above)
        def _():
            dy_group(jd)

    def share(t, g):
        part = outs[t].at[g, pl.ds(pl.multiple_of(c * ns, SL), ns)]
        return remote(part, part, sib_s.at[t, g], sib_r.at[t, g], sibling)

    def arrived(t, g):
        part = rows.at[t, g, pl.ds(0, ns - SL)]
        return remote(part, outs[t].at[g, pl.ds(0, ns - SL)], plane_s.at[t, g], plane_r.at[t, g], sibling)

    for t in range(2):

        @pl.loop(0, 4)
        def _(g):
            arrived(t, g).wait_recv()
            row_local(t, g).wait()
            share(t, g).start()

    for t in range(2):

        @pl.loop(0, 4)
        def _(g):
            share(t, g).wait_recv()
            share(t, g).wait_send()
            arrived(t, g).wait_send()

    @pl.when(own)
    def _():
        tab_out.wait_send()

    @pl.when(jnp.logical_not(own))
    def _():
        gout_out.wait_send()

    for i in range(pieces):

        @pl.when(jnp.logical_and(r >= 3, r < 7))
        def _():
            piece(0, i, up).wait_send()

        @pl.when(jnp.logical_or(r == 0, r > 4))
        def _():
            piece(1, i, down).wait_send()

    @pl.loop(0, 4)
    def _(j):
        @pl.when(lax.rem(r - j + 8, 8) < 4)
        def _():
            ring(j, up, up_s).wait_send()

        @pl.when(lax.rem(j - r + 8, 8) < 3)
        def _():
            ring(j, down, down_s).wait_send()


def dispatch(nx, nq, tokens, gout, tabs):
    ntok, width = tokens.shape
    ch = gout.shape[0]
    ns = nq * SL
    hbm = pl.BlockSpec(memory_space=pl.ANY)
    dma = pltpu.SemaphoreType.DMA
    big = jax.ShapeDtypeStruct((4, 2 * ns, 2 * ch), BF)
    return pl.pallas_call(
        functools.partial(dispatch_kernel, nx, nq),
        out_shape=(big, big, jax.ShapeDtypeStruct((2 * nq, ntok), F32)),
        in_specs=[hbm, hbm, hbm],
        out_specs=(hbm, hbm, pl.BlockSpec(memory_space=pltpu.VMEM)),
        scratch_shapes=[
            pltpu.VMEM((4, ntok, 2 * ch), BF),
            pltpu.VMEM((2 * nq, ntok), F32),
            pltpu.VMEM((4, 2 * ch, ntok), BF),
            pltpu.VMEM((2, 4, ns, 2 * ch), BF),
            pltpu.VMEM((ns, ntok), BF),
            pltpu.VMEM((ns, 128), F32),
            dma((4,)), dma, dma, dma((2, 4)), dma, dma, dma, dma,
            dma((2, 2 * ROWBLOCKS)), dma((2, 2 * ROWBLOCKS)), dma((4,)), dma((4,)), dma((4,)),
            dma((2, 4)), dma((2, 4)), dma((2, 4)), dma((2, 4)),
        ],
        compiler_params=pltpu.CompilerParams(
            collective_id=1, has_side_effects=True, vmem_limit_bytes=VMEM_LIMIT
        ),
        name="dispatch",
    )(tokens, gout, tabs)


def tdot(a, b):
    return lax.dot_general(a, b, (((0,), (0,)), ((), ())), preferred_element_type=F32)


def dot_t(a, b):
    return lax.dot_general(a, b, (((1,), (1,)), ((), ())), preferred_element_type=F32)


def expert_kernel(x, dy, wg, wu, wd, y, dx, sc, gwg, gwu, gwd):
    groups, _, pair = x.shape

    def total(f):
        acc = f(0)
        for k in range(1, groups):
            acc = acc + f(k)
        return acc

    g = total(lambda k: jnp.dot(x[k], wg[k], preferred_element_type=F32))
    u = total(lambda k: jnp.dot(x[k], wu[k], preferred_element_type=F32))
    sig = jax.nn.sigmoid(g)
    gs = g * sig
    h = (gs * u).astype(BF)
    dh = total(lambda k: dot_t(dy[k], wd[:, k * pair : (k + 1) * pair]))
    dg = (dh * u * sig * (1.0 + g * (1.0 - sig))).astype(BF)
    du = (dh * gs).astype(BF)
    part = h.astype(F32) * dh
    hi = part.astype(BF)
    lo = (part - hi.astype(F32)).astype(BF)
    ones = jnp.ones((8, part.shape[1]), BF)
    sc[...] = (dot_t(ones, hi) + dot_t(ones, lo))[0:1, :]
    for k in range(groups):
        lanes = slice(k * pair, (k + 1) * pair)
        y[k] = jnp.dot(h, wd[:, lanes], preferred_element_type=F32).astype(BF)
        dx[k] = (dot_t(dg, wg[k]) + dot_t(du, wu[k])).astype(BF)
        gwd[:, lanes] = tdot(h, dy[k]).astype(BF)
        gwg[k] = tdot(x[k], dg).astype(BF)
        gwu[k] = tdot(x[k], du).astype(BF)


def expert(x, dy, wg, wu, wd):
    s = jax.ShapeDtypeStruct
    return pl.pallas_call(
        expert_kernel,
        out_shape=(
            s(x.shape, BF), s(x.shape, BF), s((1, x.shape[1]), F32),
            s(wg.shape, BF), s(wu.shape, BF), s(wd.shape, BF),
        ),
        in_specs=[pl.BlockSpec(memory_space=pltpu.VMEM)] * 5,
        out_specs=(pl.BlockSpec(memory_space=pltpu.VMEM),) * 6,
        compiler_params=pltpu.CompilerParams(vmem_limit_bytes=VMEM_LIMIT),
        name="expert",
    )(x, dy, wg, wu, wd)


def combine_kernel(
    nx, nq, y_ref, dx_ref, sc_ref, tab_ref, mixed_ref, gtok_ref, rsc_ref,
    ob, rb, sb, rv, tp, rsd, rsu, fin, fo, wt, scr, st, rsc,
    ob_l, sib_s, sib_r, row_l, plane_s, plane_r, ring_s, down_r, up_r, fin_s, fin_r,
    dp_s, dp_r, ex_s, ex_r,
):
    me, zh, zl, c = place(nx)
    z = zh * 4 + zl
    own = zh == c
    r = lax.rem(z - 4 * c + 8, 8)
    ns = nq * SL
    ntok = tab_ref.shape[1]
    pair = y_ref.shape[2]
    ch = pair // 2
    d = 2 * zl + c
    e = lax.axis_index("expert")
    ne = 2 * nq
    up = device(nx, me, lax.rem(z + 1, 8), c)
    down = device(nx, me, lax.rem(z + 7, 8), c)
    sibling = device(nx, me, z, 1 - c)
    srcs = (y_ref, dx_ref)
    outs = (mixed_ref, gtok_ref)

    barrier = pltpu.get_barrier_semaphore()
    signal(barrier, up)
    signal(barrier, down)

    @pl.loop(1, 8)
    def _(i):
        signal(barrier, {"expert": e, "dp": lax.rem(d + i, 8)})

    @pl.loop(1, ne)
    def _(i):
        signal(barrier, {"expert": lax.rem(e + i, ne), "dp": d})

    pl.semaphore_wait(barrier, 2 + 7 + ne - 1)

    def own_rows(t, g):
        return pltpu.make_async_copy(
            srcs[t].at[g, pl.ds(pl.multiple_of(c * ns, SL), ns)], ob.at[t, g], ob_l.at[t, g]
        )

    def to_sibling(t, g):
        return remote(
            srcs[t].at[g, pl.ds(pl.multiple_of((1 - c) * ns, SL), ns)], rb.at[t, g],
            sib_s.at[t, g], sib_r.at[t, g], sibling,
        )

    scr[pl.ds(d, 1)] = sc_ref[...][None]

    @pl.loop(1, 8)
    def _(i):
        remote(sc_ref, scr.at[d], dp_s, dp_r, {"expert": e, "dp": lax.rem(d + i, 8)}).start()

    for t in range(2):

        @pl.loop(0, 4)
        def _(g):
            own_rows(t, g).start()
            to_sibling(t, g).start()

    rt = tab_ref[0:nq, :]
    gt = tab_ref[nq : 2 * nq, :]
    slot = lax.broadcasted_iota(jnp.int32, (nq, SL, ntok), 1).astype(F32)
    hit = jnp.where(jnp.broadcast_to(rt[:, None, :], (nq, SL, ntok)) == slot, 1.0, 0.0)
    heavy = (hit * jnp.broadcast_to(gt[:, None, :], (nq, SL, ntok))).reshape(ns, ntok)
    top = heavy.astype(BF)
    wt[0] = top
    wt[1] = (heavy - top.astype(F32)).astype(BF)
    wt[2] = hit.reshape(ns, ntok).astype(BF)

    def row_local(t, g):
        rows = pl.ds(pl.multiple_of(me * SL, SL), SL)
        return pltpu.make_async_copy(sb.at[t, g, rows], rv.at[t, g, rows], row_l.at[t, g])

    def arrived(t, g):
        some = pl.ds(0, ns - SL)
        return remote(sb.at[t, g, some], rv.at[t, g, some], plane_s.at[t, g], plane_r.at[t, g], sibling)

    def plane(t, g):
        own_rows(t, g).wait()
        to_sibling(t, g).wait_recv()
        sb[t, g] = (ob[t, g].astype(F32) + rb[t, g].astype(F32)).astype(BF)

        @pl.loop(1, nq)
        def _(i):
            q = lax.rem(me + i, nq)
            remote(
                sb.at[t, g, pl.ds(pl.multiple_of(q * SL, SL), SL)],
                rv.at[t, g, pl.ds(pl.multiple_of(me * SL, SL), SL)],
                plane_s.at[t, g], plane_r.at[t, g], device(nx, q, z, c),
            ).start()

        row_local(t, g).start()

    @pl.loop(0, 4)
    def _(g):
        plane(0, g)

    def all_but_one(a):
        return a.at[pl.ds(0, 7)]

    dp_all = remote(all_but_one(scr), all_but_one(scr), dp_s, dp_r, sibling)
    dp_all.wait_recv()
    st[...] = jnp.sum(scr[...], axis=0)
    rsc[pl.ds(e, 1)] = st[...][None]

    @pl.loop(1, ne)
    def _(i):
        remote(st, rsc.at[e], ex_s, ex_r, {"expert": lax.rem(e + i, ne), "dp": d}).start()

    @pl.loop(0, 4)
    def _(g):
        plane(1, g)

    def half(t, j, n, a):
        return a.at[t, j, pl.ds(n * ch, ch)]

    def send_down(t, j, n):
        return remote(half(t, j, n, tp), half(t, j, n, rsd), ring_s.at[t, j, n], down_r.at[t, j, n], down)

    def send_up(t, j, n):
        return remote(half(t, j, n, tp), half(t, j, n, rsu), ring_s.at[t, j, n], up_r.at[t, j, n], up)

    def add_in(t, j, n, a):
        both = half(t, j, n, tp)[...].astype(F32) + half(t, j, n, a)[...].astype(F32)
        half(t, j, n, tp)[...] = both.astype(BF)

    for t in range(2):

        @pl.loop(0, 4)
        def _(g):
            arrived(t, g).wait_recv()
            row_local(t, g).wait()
            if t == 0:
                part = tdot(rv[t, g], wt[0]) + tdot(rv[t, g], wt[1])
            else:
                part = tdot(rv[t, g], wt[2])
            tp[t, g] = part.astype(BF)

            @pl.when(lax.rem(r - g + 8, 8) == 4)
            def _():
                for n in range(2):
                    send_down(t, g, n).start()

            @pl.when(lax.rem(g - r + 8, 8) == 3)
            def _():
                for n in range(2):
                    send_up(t, g, n).start()

        @pl.loop(1, 4)
        def _(m):
            k = 4 - m
            ju = lax.rem(r - k + 8, 8)
            jd = lax.rem(r + k, 8)
            for n in range(2):

                @pl.when(ju < 4)
                def _():
                    send_down(t, ju, n).wait_recv()
                    add_in(t, ju, n, rsd)
                    send_down(t, ju, n).start()

                @pl.when(jnp.logical_and(jd < 4, k < 3))
                def _():
                    send_up(t, jd, n).wait_recv()
                    add_in(t, jd, n, rsu)
                    send_up(t, jd, n).start()

        final = remote(fin.at[t], fo.at[t], fin_s.at[t], fin_r.at[t], sibling)

        @pl.when(own)
        def _():
            for n in range(2):
                send_down(t, zl, n).wait_recv()
                send_up(t, zl, n).wait_recv()

            def summed(core):
                rows = pl.ds(pl.multiple_of(core * ch, SL), ch)
                total = tp[t, zl, rows].astype(F32) + rsd[t, zl, rows].astype(F32)
                return (total + rsu[t, zl, rows].astype(F32)).astype(BF)

            fin[t] = summed(1 - c)
            final.start()
            outs[t][...] = summed(c)

    for t in range(2):
        final = remote(fin.at[t], fo.at[t], fin_s.at[t], fin_r.at[t], sibling)

        @pl.when(own)
        def _():
            final.wait_send()

        @pl.when(jnp.logical_not(own))
        def _():
            final.wait_recv()
            outs[t][...] = fo[t]

    some = pl.ds(0, ne - 1)
    ex_all = remote(rsc.at[some], rsc.at[some], ex_s, ex_r, sibling)
    ex_all.wait_recv()
    rsc_ref[...] = rsc[...]
    ex_all.wait_send()
    dp_all.wait_send()
    for t in range(2):

        @pl.loop(0, 4)
        def _(g):
            to_sibling(t, g).wait_send()
            arrived(t, g).wait_send()

            @pl.when(g != r)
            def _():
                for n in range(2):
                    send_down(t, g, n).wait_send()


def combine(nx, nq, ch, ntok, y, dx, sc, tab):
    ns = nq * SL
    pair = 2 * ch
    hbm = pl.BlockSpec(memory_space=pl.ANY)
    vm = pl.BlockSpec(memory_space=pltpu.VMEM)
    dma = pltpu.SemaphoreType.DMA
    s = jax.ShapeDtypeStruct
    wide = pltpu.VMEM((2, 4, ns, pair), BF)
    tall = pltpu.VMEM((2, 4, pair, ntok), BF)
    return pl.pallas_call(
        functools.partial(combine_kernel, nx, nq),
        out_shape=(s((ch, ntok), BF), s((ch, ntok), BF), s((2 * nq, 1, 2 * ns), F32)),
        in_specs=[hbm, hbm, vm, vm],
        out_specs=(vm, vm, vm),
        scratch_shapes=[
            wide, wide, wide, wide, tall, tall, tall,
            pltpu.VMEM((2, ch, ntok), BF), pltpu.VMEM((2, ch, ntok), BF),
            pltpu.VMEM((3, ns, ntok), BF),
            pltpu.VMEM((8, 1, 2 * ns), F32), pltpu.VMEM((1, 2 * ns), F32), pltpu.VMEM((2 * nq, 1, 2 * ns), F32),
            dma((2, 4)), dma((2, 4)), dma((2, 4)), dma((2, 4)), dma((2, 4)), dma((2, 4)),
            dma((2, 4, 2)), dma((2, 4, 2)), dma((2, 4, 2)), dma((2,)), dma((2,)),
            dma, dma, dma, dma,
        ],
        compiler_params=pltpu.CompilerParams(
            collective_id=2, has_side_effects=True, vmem_limit_bytes=VMEM_LIMIT
        ),
        name="combine",
    )(y, dx, sc, tab)


def on_device(nx, tokens, expert_ids, gate_values, tiles, w_gate, w_up, w_down, grad_out):
    ne = lax.axis_size("expert")
    nq = ne // 2
    ntok, width = tokens.shape
    ch = grad_out.shape[1]
    pair = 2 * ch
    live = jnp.arange(ntok, dtype=jnp.int32) < tiles[0] * TILE
    names = jnp.arange(ne, dtype=jnp.int32)[:, None, None]
    chosen = (expert_ids.T[None] == names) & live[None, None, :]
    named = jnp.any(chosen, axis=1)
    earlier = jnp.arange(ntok)[:, None] < jnp.arange(ntok)[None, :]
    rank = jnp.dot(named.astype(BF), earlier.astype(BF), preferred_element_type=F32)
    rank = jnp.where(named, rank, -1.0)
    gate = jnp.sum(jnp.where(chosen, gate_values.T[None], 0.0), axis=1)

    def halves(a):
        return a.reshape(nq // nx, 2, nx, ntok).transpose(1, 0, 2, 3).reshape(2, nq, ntok)

    tabs = jnp.concatenate([halves(rank), halves(gate)], axis=1)
    x, dy, tab = dispatch(nx, nq, tokens, grad_out.T, tabs)
    fh = w_gate.shape[2]
    wg = w_gate.reshape(4, pair, fh)
    wu = w_up.reshape(4, pair, fh)
    y, dx, sc, gwg, gwu, gwd = expert(x, dy, wg, wu, w_down[0])
    mixed, gtok, rsc = combine(nx, nq, ch, ntok, y, dx, sc, tab)
    e = lax.axis_index("expert")
    zh = (e // nx) % 2
    me = (e // (2 * nx)) * nx + e % nx
    mine = lax.dynamic_slice(rsc[:, 0, :], (0, zh * nq * SL + me * SL), (ne, SL))
    slots = jnp.arange(SL, dtype=F32)
    at = jnp.sum(jnp.where(rank[:, None, :] == slots[None, :, None], mine[:, :, None], 0.0), axis=1)
    at = jnp.where(named, at / jnp.where(named, gate, 1.0), 0.0)
    grad_gates = jnp.sum(jnp.where(chosen, at[:, None, :], 0.0), axis=0).T
    return (
        mixed.T, gtok.T, grad_gates,
        gwg.reshape(1, width, fh), gwu.reshape(1, width, fh), gwd[None],
    )


def build(mesh, nx):
    placed = (
        P("expert", None),
        P("expert", None),
        P("expert", None),
        P("expert"),
        P("expert", None, "dp"),
        P("expert", None, "dp"),
        P("expert", "dp", None),
        P("expert", "dp"),
    )
    return jax.shard_map(
        functools.partial(on_device, nx),
        mesh=mesh,
        in_specs=placed,
        out_specs=(
            P("expert", "dp"),
            P("expert", "dp"),
            P("expert", None),
            P("expert", None, "dp"),
            P("expert", None, "dp"),
            P("expert", "dp", None),
        ),
        check_vma=False,
    )


def solution(mesh):
    return build(mesh, 4)
```

```python
import functools

import jax
import jax.numpy as jnp
from jax import lax
from jax.experimental import pallas as pl
from jax.experimental.pallas import tpu as pltpu
from jax.sharding import PartitionSpec as P

TILE = 128
SL = 16
MESH = pl.DeviceIdType.MESH
VMEM_LIMIT = 60 * 1024 * 1024
BF = jnp.bfloat16
F32 = jnp.float32
ROWBLOCKS = 4
PARTS = 4


def place(nx):
    e = lax.axis_index("expert")
    d = lax.axis_index("dp")
    x = lax.rem(e, nx)
    zh = lax.rem(lax.div(e, nx), 2)
    y = lax.div(e, 2 * nx)
    return y * nx + x, zh, lax.div(d, 2), lax.rem(d, 2)


def device(nx, q, z, core):
    e = (lax.div(q, nx) * 2 + lax.div(z, 4)) * nx + lax.rem(q, nx)
    return {"expert": e, "dp": lax.rem(z, 4) * 2 + core}


def signal(sem, who):
    pl.semaphore_signal(sem, inc=1, device_id=who, device_id_type=MESH)


def remote(src, dst, send, recv, who):
    return pltpu.make_async_remote_copy(
        src_ref=src, dst_ref=dst, send_sem=send, recv_sem=recv, device_id=who, device_id_type=MESH
    )


def tdot(a, b):
    return lax.dot_general(a, b, (((0,), (0,)), ((), ())), preferred_element_type=F32)


def dot_t(a, b):
    return lax.dot_general(a, b, (((1,), (1,)), ((), ())), preferred_element_type=F32)


def moe_kernel(
    nx, nq, tok_ref, gout_ref, tabs_ref, wg_ref, wu_ref, wd_ref,
    mixed_ref, gtok_ref, rsc_ref, gwg_ref, gwu_ref, gwd_ref,
    tok, tabr, dyt, rows, xdy, pick, sg, wt, wg, wu, wd,
    gacc, uacc, dacc, hb, dgb, dub, scb,
    so, ob, rb, rv, tp, rsd, rsu, fin, fo, scr, st, rsc,
    tok_l, tab_l, gout_l, w_l, row_l, back_l, out_l,
    tab_s, tab_r, gout_s, gout_r, x_s, x_r, up_s, down_s, ring_r,
    plane_s, plane_r, share_s, share_r, sib_s, sib_r, back_s, back_r,
    ring_s, down_r, up_r, fin_s, fin_r, dp_s, dp_r, ex_s, ex_r,
):
    me, zh, zl, c = place(nx)
    z = zh * 4 + zl
    e = lax.axis_index("expert")
    d = 2 * zl + c
    own = zh == c
    other = jnp.logical_not(own)
    r = lax.rem(z - 4 * c + 8, 8)
    ntok = tok_ref.shape[0]
    ch = gout_ref.shape[0]
    pair = 2 * ch
    ns = nq * SL
    ne = 2 * nq
    part = pair // PARTS
    up = device(nx, me, lax.rem(z + 1, 8), c)
    down = device(nx, me, lax.rem(z + 7, 8), c)
    across = device(nx, me, lax.rem(z + 4, 8), c)
    sibling = device(nx, me, z, 1 - c)
    outs = (mixed_ref, gtok_ref)
    mine = pl.ds(pl.multiple_of(c * ns, SL), ns)
    theirs = pl.ds(pl.multiple_of((1 - c) * ns, SL), ns)

    def slots(q):
        return pl.ds(pl.multiple_of(q * SL, SL), SL)

    weights = [
        pltpu.make_async_copy(a, b, w_l.at[i])
        for i, (a, b) in enumerate(((wg_ref, wg), (wu_ref, wu), (wd_ref, wd)))
    ]

    def tok_in(g):
        return pltpu.make_async_copy(tok_ref.at[:, pl.ds(g * pair, pair)], tok.at[g], tok_l.at[g])

    tab_in = pltpu.make_async_copy(tabs_ref.at[zh], tabr, tab_l)
    tab_out = remote(tabs_ref.at[1 - zh], tabr, tab_s, tab_r, across)
    chunk = dyt.at[zl, pl.ds(pl.multiple_of(c * ch, SL), ch)]
    gout_in = pltpu.make_async_copy(gout_ref, chunk, gout_l)
    gout_out = remote(gout_ref, chunk, gout_s, gout_r, sibling)

    @pl.when(own)
    def _():
        tab_in.start()
        for g in (0, 2, 1, 3):
            tok_in(g).start()
        gout_in.start()

    for w in weights:
        w.start()

    barrier = pltpu.get_barrier_semaphore()
    signal(barrier, up)
    signal(barrier, down)

    @pl.loop(1, 8)
    def _(i):
        signal(barrier, {"expert": e, "dp": lax.rem(d + i, 8)})

    @pl.loop(1, ne)
    def _(i):
        signal(barrier, {"expert": lax.rem(e + i, ne), "dp": d})

    pl.semaphore_wait(barrier, 2 + 7 + ne - 1)

    def piece(h, i, who):
        step = ntok // ROWBLOCKS
        first = pl.multiple_of(lax.rem(i, ROWBLOCKS) * step, step)
        some = tok.at[2 * h + lax.div(i, ROWBLOCKS), pl.ds(first, step)]
        return remote(some, some, x_s.at[h, i], x_r.at[h, i], who)

    def ring(j, who, sems):
        return remote(dyt.at[j], dyt.at[j], sems.at[j], ring_r.at[j], who)

    pieces = 2 * ROWBLOCKS

    @pl.when(own)
    def _():
        tab_out.start()
        for g in (0, 2, 1, 3):
            tok_in(g).wait()
            for i in range(ROWBLOCKS):
                n = (g % 2) * ROWBLOCKS + i
                if g < 2:

                    @pl.when(r == 3)
                    def _():
                        piece(0, n, up).start()
                else:

                    @pl.when(r == 0)
                    def _():
                        piece(1, n, down).start()

        gout_in.wait()
        gout_out.wait_recv()
        ring(zl, up, up_s).start()
        ring(zl, down, down_s).start()
        tab_in.wait()

    @pl.when(other)
    def _():
        gout_out.start()
        tab_out.wait_recv()

    rt = tabr[0:nq, :]
    gt = tabr[nq : 2 * nq, :]
    slot = lax.broadcasted_iota(jnp.int32, (nq, SL, ntok), 1).astype(F32)
    hit = jnp.where(jnp.broadcast_to(rt[:, None, :], (nq, SL, ntok)) == slot, 1.0, 0.0)
    heavy = (hit * jnp.broadcast_to(gt[:, None, :], (nq, SL, ntok))).reshape(ns, ntok)
    top = heavy.astype(BF)
    pick[...] = hit.reshape(ns, ntok).astype(BF)
    wt[0] = top
    wt[1] = (heavy - top.astype(F32)).astype(BF)
    sg[...] = jnp.broadcast_to(jnp.sum(heavy, axis=1, keepdims=True), sg.shape)

    def row_local(t, g):
        return pltpu.make_async_copy(
            rows.at[t, g, slots(me)], xdy.at[t, g, slots(c * nq + me)], row_l.at[t, g]
        )

    def send_rows(t, g):
        @pl.loop(1, nq)
        def _(i):
            q = lax.rem(me + i, nq)
            remote(
                rows.at[t, g, slots(q)], xdy.at[t, g, slots(c * nq + me)],
                plane_s.at[t, g], plane_r.at[t, g], device(nx, q, z, c),
            ).start()

        row_local(t, g).start()

    def x_group(g):
        rows[0, g] = jnp.dot(pick[...], tok[g], preferred_element_type=F32).astype(BF)
        send_rows(0, g)

    def dy_group(g):
        rows[1, g] = (dot_t(pick[...], dyt[g]) * sg[:, 0:1]).astype(BF)
        send_rows(1, g)

    @pl.when(own)
    def _():
        @pl.loop(0, 4)
        def _(g):
            x_group(g)

        dy_group(zl)

    @pl.when(other)
    def _():
        @pl.loop(1, pieces + 4)
        def _(n):
            for h, far, who in ((0, r - 3, up), (1, 8 - r, down)):
                i = n - far

                @pl.when(jnp.logical_and(i >= 0, i < pieces))
                def _():
                    piece(h, i, who).wait_recv()

                    @pl.when(far < 4)
                    def _():
                        piece(h, i, who).start()

            for h, far in ((0, r - 3), (1, 8 - r)):
                i = n - far
                whole = lax.rem(i + ROWBLOCKS, ROWBLOCKS) == ROWBLOCKS - 1

                @pl.when(jnp.logical_and(jnp.logical_and(i >= 0, i < pieces), whole))
                def _():
                    x_group(2 * h + lax.div(i, ROWBLOCKS))

    @pl.loop(1, 5)
    def _(k):
        ju = lax.rem(r - k + 8, 8)
        jd = lax.rem(r + k, 8)
        from_below = ju < 4
        from_above = jnp.logical_and(jd < 4, k < 4)

        @pl.when(from_below)
        def _():
            ring(ju, up, up_s).wait_recv()

            @pl.when(k < 4)
            def _():
                ring(ju, up, up_s).start()

        @pl.when(from_above)
        def _():
            ring(jd, down, down_s).wait_recv()

            @pl.when(k < 3)
            def _():
                ring(jd, down, down_s).start()

        @pl.when(from_below)
        def _():
            dy_group(ju)

        @pl.when(from_above)
        def _():
            dy_group(jd)

    def share(t, g):
        return remote(xdy.at[t, g, mine], xdy.at[t, g, mine], share_s.at[t, g], share_r.at[t, g], sibling)

    def arrived(t, g):
        some = pl.ds(0, ns - SL)
        return remote(rows.at[t, g, some], xdy.at[t, g, some], plane_s.at[t, g], plane_r.at[t, g], sibling)

    def take_in(t):
        @pl.loop(0, 4)
        def _(g):
            arrived(t, g).wait_recv()
            row_local(t, g).wait()
            share(t, g).start()

    def to_sibling(t, f):
        return remote(so.at[t, f], rb.at[t, f], sib_s.at[t, f], sib_r.at[t, f], sibling)

    def back_local(t, g):
        return pltpu.make_async_copy(ob.at[t, g, slots(me)], rv.at[t, g, slots(me)], back_l.at[t, g])

    def back_arrived(t, g):
        some = pl.ds(0, ns - SL)
        return remote(ob.at[t, g, some], rv.at[t, g, some], back_s.at[t, g], back_r.at[t, g], sibling)

    def send_back(t):
        @pl.loop(0, 4)
        def _(g):
            to_sibling(t, g).wait_recv()
            ob[t, g] = (ob[t, g].astype(F32) + rb[t, g].astype(F32)).astype(BF)

            @pl.loop(1, nq)
            def _(i):
                q = lax.rem(me + i, nq)
                remote(
                    ob.at[t, g, slots(q)], rv.at[t, g, slots(me)],
                    back_s.at[t, g], back_r.at[t, g], device(nx, q, z, c),
                ).start()

            back_local(t, g).start()

    def lanes(f):
        return slice(f * pair, (f + 1) * pair)

    take_in(0)
    weights[0].wait()
    weights[1].wait()
    gacc[...] = jnp.zeros_like(gacc)
    uacc[...] = jnp.zeros_like(uacc)

    @pl.loop(0, 4)
    def _(f):
        share(0, f).wait_recv()
        gacc[...] += jnp.dot(xdy[0, f], wg[f], preferred_element_type=F32)
        uacc[...] += jnp.dot(xdy[0, f], wu[f], preferred_element_type=F32)

    g = gacc[...]
    hb[...] = (g * jax.nn.sigmoid(g) * uacc[...]).astype(BF)
    weights[2].wait()
    for f in range(4):
        so[0, f] = jnp.dot(hb[theirs, :], wd[:, lanes(f)], preferred_element_type=F32).astype(BF)
        to_sibling(0, f).start()
        ob[0, f] = jnp.dot(hb[mine, :], wd[:, lanes(f)], preferred_element_type=F32).astype(BF)

    send_back(0)

    take_in(1)
    dacc[...] = jnp.zeros_like(dacc)
    for f in range(4):
        share(1, f).wait_recv()
        dacc[...] += dot_t(xdy[1, f], wd[:, lanes(f)])

    g = gacc[...]
    u = uacc[...]
    dh = dacc[...]
    sig = jax.nn.sigmoid(g)
    dgb[...] = (dh * u * sig * (1.0 + g * (1.0 - sig))).astype(BF)
    dub[...] = (dh * g * sig).astype(BF)
    prod = hb[...].astype(F32) * dh
    hi = prod.astype(BF)
    lo = (prod - hi.astype(F32)).astype(BF)
    ones = jnp.ones((8, prod.shape[1]), BF)
    scb[...] = (dot_t(ones, hi) + dot_t(ones, lo))[0:1, :]
    scr[pl.ds(d, 1)] = scb[...][None]

    @pl.loop(1, 8)
    def _(i):
        remote(scb, scr.at[d], dp_s, dp_r, {"expert": e, "dp": lax.rem(d + i, 8)}).start()

    @pl.loop(0, 4)
    def _(f):
        so[1, f] = (dot_t(dgb[theirs, :], wg[f]) + dot_t(dub[theirs, :], wu[f])).astype(BF)
        to_sibling(1, f).start()
        ob[1, f] = (dot_t(dgb[mine, :], wg[f]) + dot_t(dub[mine, :], wu[f])).astype(BF)

    send_back(1)

    seven = scr.at[pl.ds(0, 7)]
    dp_all = remote(seven, seven, dp_s, dp_r, sibling)
    dp_all.wait_recv()
    st[...] = jnp.sum(scr[...], axis=0)
    rsc[pl.ds(e, 1)] = st[...][None]

    @pl.loop(1, ne)
    def _(i):
        remote(st, rsc.at[e], ex_s, ex_r, {"expert": lax.rem(e + i, ne), "dp": d}).start()

    @pl.loop(0, 4)
    def _(f):
        wg[f] = tdot(xdy[0, f], dgb[...]).astype(BF)
        wu[f] = tdot(xdy[0, f], dub[...]).astype(BF)

    for f in range(4):
        wd[:, lanes(f)] = tdot(hb[...], xdy[1, f]).astype(BF)

    results = [
        pltpu.make_async_copy(a, b, out_l.at[i])
        for i, (a, b) in enumerate(((wg, gwg_ref), (wu, gwu_ref), (wd, gwd_ref)))
    ]
    for o in results:
        o.start()

    def rows_of(n):
        return pl.ds(pl.multiple_of(n * part, SL), part)

    def send_down(t, j, n):
        return remote(
            tp.at[t, j, rows_of(n)], rsd.at[t, j, rows_of(n)], ring_s.at[t, j, n], down_r.at[t, j, n], down
        )

    def send_up(t, j, n):
        return remote(
            tp.at[t, j, rows_of(n)], rsu.at[t, j, rows_of(n)], ring_s.at[t, j, n], up_r.at[t, j, n], up
        )

    def add_in(t, j, n, a):
        tp[t, j, rows_of(n)] = (
            tp[t, j, rows_of(n)].astype(F32) + a[t, j, rows_of(n)].astype(F32)
        ).astype(BF)

    for t in range(2):

        @pl.loop(0, 4)
        def _(g):
            back_arrived(t, g).wait_recv()
            back_local(t, g).wait()
            if t == 0:
                made = tdot(rv[t, g], wt[0]) + tdot(rv[t, g], wt[1])
            else:
                made = tdot(rv[t, g], pick[...])
            tp[t, g] = made.astype(BF)
            above = lax.rem(r - g + 8, 8)
            below = lax.rem(g - r + 8, 8)

            @pl.when(jnp.logical_and(above > 0, above < 5))
            def _():
                @pl.loop(0, PARTS)
                def _(n):
                    @pl.when(above < 4)
                    def _():
                        send_down(t, g, n).wait_recv()
                        add_in(t, g, n, rsd)

                    send_down(t, g, n).start()

            @pl.when(jnp.logical_and(below > 0, below < 4))
            def _():
                @pl.loop(0, PARTS)
                def _(n):
                    @pl.when(below < 3)
                    def _():
                        send_up(t, g, n).wait_recv()
                        add_in(t, g, n, rsu)

                    send_up(t, g, n).start()

    def final(t):
        return remote(fin.at[t], fo.at[t], fin_s.at[t], fin_r.at[t], sibling)

    @pl.when(own)
    def _():
        for t in range(2):

            @pl.loop(0, PARTS)
            def _(n):
                send_down(t, zl, n).wait_recv()
                send_up(t, zl, n).wait_recv()

            def summed(core):
                some = pl.ds(pl.multiple_of(core * ch, SL), ch)
                total = tp[t, zl, some].astype(F32) + rsd[t, zl, some].astype(F32)
                return (total + rsu[t, zl, some].astype(F32)).astype(BF)

            fin[t] = summed(1 - c)
            final(t).start()
            outs[t][...] = summed(c)

        for t in range(2):
            final(t).wait_send()

        tab_out.wait_send()

    @pl.when(other)
    def _():
        for t in range(2):
            final(t).wait_recv()
            outs[t][...] = fo[t]

        gout_out.wait_send()

    some = pl.ds(0, ne - 1)
    ex_all = remote(rsc.at[some], rsc.at[some], ex_s, ex_r, sibling)
    ex_all.wait_recv()
    rsc_ref[...] = rsc[...]
    ex_all.wait_send()
    dp_all.wait_send()
    for o in results:
        o.wait()

    @pl.loop(0, pieces)
    def _(i):
        @pl.when(jnp.logical_and(r >= 3, r < 7))
        def _():
            piece(0, i, up).wait_send()

        @pl.when(jnp.logical_or(r == 0, r > 4))
        def _():
            piece(1, i, down).wait_send()

    for t in range(2):

        @pl.loop(0, 4)
        def _(g):
            arrived(t, g).wait_send()
            share(t, g).wait_send()
            to_sibling(t, g).wait_send()
            back_arrived(t, g).wait_send()

            @pl.when(g != r)
            def _():
                @pl.loop(0, PARTS)
                def _(n):
                    send_down(t, g, n).wait_send()

    @pl.loop(0, 4)
    def _(j):
        @pl.when(lax.rem(r - j + 8, 8) < 4)
        def _():
            ring(j, up, up_s).wait_send()

        @pl.when(lax.rem(j - r + 8, 8) < 3)
        def _():
            ring(j, down, down_s).wait_send()


def moe(nx, nq, tokens, gout, tabs, wg, wu, wd):
    ntok = tokens.shape[0]
    ch = gout.shape[0]
    pair = 2 * ch
    ns = nq * SL
    fh = wg.shape[2]
    hbm = pl.BlockSpec(memory_space=pl.ANY)
    vm = pl.BlockSpec(memory_space=pltpu.VMEM)
    dma = pltpu.SemaphoreType.DMA
    s = jax.ShapeDtypeStruct
    v = pltpu.VMEM
    wide = v((2, 4, ns, pair), BF)
    tall = v((2, 4, pair, ntok), BF)
    each = dma((2, 4))
    parts = dma((2, 4, PARTS))
    return pl.pallas_call(
        functools.partial(moe_kernel, nx, nq),
        out_shape=(
            s((ch, ntok), BF), s((ch, ntok), BF), s((2 * nq, 1, 2 * ns), F32),
            s(wg.shape, BF), s(wu.shape, BF), s(wd.shape, BF),
        ),
        in_specs=[hbm] * 6,
        out_specs=(vm, vm, vm, hbm, hbm, hbm),
        scratch_shapes=[
            v((4, ntok, pair), BF), v((2 * nq, ntok), F32), v((4, pair, ntok), BF), wide,
            v((2, 4, 2 * ns, pair), BF), v((ns, ntok), BF), v((ns, 128), F32), v((2, ns, ntok), BF),
            v(wg.shape, BF), v(wu.shape, BF), v(wd.shape, BF),
            v((2 * ns, fh), F32), v((2 * ns, fh), F32), v((2 * ns, fh), F32),
            v((2 * ns, fh), BF), v((2 * ns, fh), BF), v((2 * ns, fh), BF), v((1, 2 * ns), F32),
            wide, wide, wide, wide, tall, tall, tall, v((2, ch, ntok), BF), v((2, ch, ntok), BF),
            v((8, 1, 2 * ns), F32), v((1, 2 * ns), F32), v((2 * nq, 1, 2 * ns), F32),
            dma((4,)), dma, dma, dma((3,)), each, each, dma((3,)),
            dma, dma, dma, dma, dma((2, 2 * ROWBLOCKS)), dma((2, 2 * ROWBLOCKS)), dma((4,)), dma((4,)), dma((4,)),
            each, each, each, each, each, each, each, each,
            parts, parts, parts, dma((2,)), dma((2,)), dma, dma, dma, dma,
        ],
        compiler_params=pltpu.CompilerParams(
            collective_id=1, has_side_effects=True, vmem_limit_bytes=VMEM_LIMIT
        ),
        name="moe",
    )(tokens, gout, tabs, wg, wu, wd)


def on_device(nx, tokens, expert_ids, gate_values, tiles, w_gate, w_up, w_down, grad_out):
    ne = lax.axis_size("expert")
    nq = ne // 2
    ntok, width = tokens.shape
    ch = grad_out.shape[1]
    pair = 2 * ch
    live = jnp.arange(ntok, dtype=jnp.int32) < tiles[0] * TILE
    names = jnp.arange(ne, dtype=jnp.int32)[:, None, None]
    chosen = (expert_ids.T[None] == names) & live[None, None, :]
    named = jnp.any(chosen, axis=1)
    earlier = jnp.arange(ntok)[:, None] < jnp.arange(ntok)[None, :]
    rank = jnp.dot(named.astype(BF), earlier.astype(BF), preferred_element_type=F32)
    rank = jnp.where(named, rank, -1.0)
    gate = jnp.sum(jnp.where(chosen, gate_values.T[None], 0.0), axis=1)

    def halves(a):
        return a.reshape(nq // nx, 2, nx, ntok).transpose(1, 0, 2, 3).reshape(2, nq, ntok)

    tabs = jnp.concatenate([halves(rank), halves(gate)], axis=1)
    fh = w_gate.shape[2]
    wg = w_gate.reshape(4, pair, fh)
    wu = w_up.reshape(4, pair, fh)
    mixed, gtok, rsc, gwg, gwu, gwd = moe(nx, nq, tokens, grad_out.T, tabs, wg, wu, w_down[0])
    e = lax.axis_index("expert")
    zh = (e // nx) % 2
    me = (e // (2 * nx)) * nx + e % nx
    mine = lax.dynamic_slice(rsc[:, 0, :], (0, zh * nq * SL + me * SL), (ne, SL))
    slots = jnp.arange(SL, dtype=F32)
    at = jnp.sum(jnp.where(rank[:, None, :] == slots[None, :, None], mine[:, :, None], 0.0), axis=1)
    at = jnp.where(named, at / jnp.where(named, gate, 1.0), 0.0)
    grad_gates = jnp.sum(jnp.where(chosen, at[:, None, :], 0.0), axis=0).T
    return (
        mixed.T, gtok.T, grad_gates,
        gwg.reshape(1, width, fh), gwu.reshape(1, width, fh), gwd[None],
    )


def build(mesh, nx):
    placed = (
        P("expert", None),
        P("expert", None),
        P("expert", None),
        P("expert"),
        P("expert", None, "dp"),
        P("expert", None, "dp"),
        P("expert", "dp", None),
        P("expert", "dp"),
    )
    return jax.shard_map(
        functools.partial(on_device, nx),
        mesh=mesh,
        in_specs=placed,
        out_specs=(
            P("expert", "dp"),
            P("expert", "dp"),
            P("expert", None),
            P("expert", None, "dp"),
            P("expert", None, "dp"),
            P("expert", "dp", None),
        ),
        check_vma=False,
    )


def solution(mesh):
    return build(mesh, 4)
```

```python
import functools

import jax
import jax.numpy as jnp
from jax import lax
from jax.experimental import pallas as pl
from jax.experimental.pallas import tpu as pltpu
from jax.sharding import PartitionSpec as P

TILE = 128
SL = 16
MESH = pl.DeviceIdType.MESH
VMEM_LIMIT = 60 * 1024 * 1024
BF = jnp.bfloat16
F32 = jnp.float32
ROWBLOCKS = 4
PARTS = 4
SKEW = 2
RING_FIRST = 9
RING_STEP = 4
RING_INSIDE = 2


def place(nx):
    e = lax.axis_index("expert")
    d = lax.axis_index("dp")
    x = lax.rem(e, nx)
    zh = lax.rem(lax.div(e, nx), 2)
    y = lax.div(e, 2 * nx)
    return y * nx + x, zh, lax.div(d, 2), lax.rem(d, 2)


def device(nx, q, z, core):
    e = (lax.div(q, nx) * 2 + lax.div(z, 4)) * nx + lax.rem(q, nx)
    return {"expert": e, "dp": lax.rem(z, 4) * 2 + core}


def signal(sem, who):
    pl.semaphore_signal(sem, inc=1, device_id=who, device_id_type=MESH)


def remote(src, dst, send, recv, who):
    return pltpu.make_async_remote_copy(
        src_ref=src, dst_ref=dst, send_sem=send, recv_sem=recv, device_id=who, device_id_type=MESH
    )


def tdot(a, b):
    return lax.dot_general(a, b, (((0,), (0,)), ((), ())), preferred_element_type=F32)


def dot_t(a, b):
    return lax.dot_general(a, b, (((1,), (1,)), ((), ())), preferred_element_type=F32)


def moe_kernel(
    nx, nq, tok_ref, gout_ref, tabs_ref, wg_ref, wu_ref, wd_ref,
    mixed_ref, gtok_ref, rsc_ref, gwg_ref, gwu_ref, gwd_ref,
    tok, tabr, dyt, rows, xdy, pick, sg, wt, wg, wu, wd,
    gacc, uacc, dacc, hb, dgb, dub, scb,
    so, ob, rb, rv, tp, rsd, rsu, fin, fo, scr, st, rsc,
    tok_l, tab_l, gout_l, w_l, row_l, back_l, out_l,
    tab_s, tab_r, gout_s, gout_r, x_s, x_r, up_s, down_s, ring_r,
    plane_s, plane_r, share_s, share_r, sib_s, sib_r, back_s, back_r,
    ring_s, down_r, up_r, fin_s, fin_r, dp_s, dp_r, ex_s, ex_r,
):
    me, zh, zl, c = place(nx)
    z = zh * 4 + zl
    e = lax.axis_index("expert")
    d = 2 * zl + c
    own = zh == c
    other = jnp.logical_not(own)
    r = lax.rem(z - 4 * c + 8, 8)
    ntok = tok_ref.shape[0]
    ch = gout_ref.shape[0]
    pair = 2 * ch
    ns = nq * SL
    ne = 2 * nq
    part = pair // PARTS
    up = device(nx, me, lax.rem(z + 1, 8), c)
    down = device(nx, me, lax.rem(z + 7, 8), c)
    across = device(nx, me, lax.rem(z + 4, 8), c)
    sibling = device(nx, me, z, 1 - c)
    outs = (mixed_ref, gtok_ref)
    mine = pl.ds(pl.multiple_of(c * ns, SL), ns)
    theirs = pl.ds(pl.multiple_of((1 - c) * ns, SL), ns)

    def slots(q):
        return pl.ds(pl.multiple_of(q * SL, SL), SL)

    weights = [
        pltpu.make_async_copy(a, b, w_l.at[i])
        for i, (a, b) in enumerate(((wg_ref, wg), (wu_ref, wu), (wd_ref, wd)))
    ]

    def tok_in(g):
        return pltpu.make_async_copy(tok_ref.at[:, pl.ds(g * pair, pair)], tok.at[g], tok_l.at[g])

    tab_in = pltpu.make_async_copy(tabs_ref.at[zh], tabr, tab_l)
    tab_out = remote(tabs_ref.at[1 - zh], tabr, tab_s, tab_r, across)
    chunk = dyt.at[zl, pl.ds(pl.multiple_of(c * ch, SL), ch)]
    gout_in = pltpu.make_async_copy(gout_ref, chunk, gout_l)
    gout_out = remote(gout_ref, chunk, gout_s, gout_r, sibling)

    @pl.when(own)
    def _():
        tab_in.start()
        for g in (0, 2, 1, 3):
            tok_in(g).start()
        gout_in.start()

    for w in weights:
        w.start()

    barrier = pltpu.get_barrier_semaphore()
    signal(barrier, up)
    signal(barrier, down)

    @pl.loop(1, 8)
    def _(i):
        signal(barrier, {"expert": e, "dp": lax.rem(d + i, 8)})

    @pl.loop(1, ne)
    def _(i):
        signal(barrier, {"expert": lax.rem(e + i, ne), "dp": d})

    pl.semaphore_wait(barrier, 2 + 7 + ne - 1)

    def piece(h, i, who):
        step = ntok // ROWBLOCKS
        first = pl.multiple_of(lax.rem(i, ROWBLOCKS) * step, step)
        some = tok.at[2 * h + lax.div(i, ROWBLOCKS), pl.ds(first, step)]
        return remote(some, some, x_s.at[h, i], x_r.at[h, i], who)

    def ring(j, who, sems):
        return remote(dyt.at[j], dyt.at[j], sems.at[j], ring_r.at[j], who)

    pieces = 2 * ROWBLOCKS

    @pl.when(own)
    def _():
        tab_out.start()
        for g in (0, 2, 1, 3):
            tok_in(g).wait()
            for i in range(ROWBLOCKS):
                n = (g % 2) * ROWBLOCKS + i
                if g < 2:

                    @pl.when(r == 3)
                    def _():
                        piece(0, n, up).start()
                else:

                    @pl.when(r == 0)
                    def _():
                        piece(1, n, down).start()

        gout_in.wait()
        gout_out.wait_recv()
        ring(zl, up, up_s).start()
        ring(zl, down, down_s).start()
        tab_in.wait()

    @pl.when(other)
    def _():
        gout_out.start()
        tab_out.wait_recv()

    rt = tabr[0:nq, :]
    gt = tabr[nq : 2 * nq, :]
    slot = lax.broadcasted_iota(jnp.int32, (nq, SL, ntok), 1).astype(F32)
    hit = jnp.where(jnp.broadcast_to(rt[:, None, :], (nq, SL, ntok)) == slot, 1.0, 0.0)
    heavy = (hit * jnp.broadcast_to(gt[:, None, :], (nq, SL, ntok))).reshape(ns, ntok)
    top = heavy.astype(BF)
    pick[...] = hit.reshape(ns, ntok).astype(BF)
    wt[0] = top
    wt[1] = (heavy - top.astype(F32)).astype(BF)
    sg[...] = jnp.broadcast_to(jnp.sum(heavy, axis=1, keepdims=True), sg.shape)

    def row_local(t, g):
        return pltpu.make_async_copy(
            rows.at[t, g, slots(me)], xdy.at[t, g, slots(c * nq + me)], row_l.at[t, g]
        )

    def send_rows(t, g):
        @pl.loop(1, nq)
        def _(i):
            q = lax.rem(me + i, nq)
            remote(
                rows.at[t, g, slots(q)], xdy.at[t, g, slots(c * nq + me)],
                plane_s.at[t, g], plane_r.at[t, g], device(nx, q, z, c),
            ).start()

        row_local(t, g).start()

    def x_group(g):
        rows[0, g] = jnp.dot(pick[...], tok[g], preferred_element_type=F32).astype(BF)
        send_rows(0, g)

    def dy_group(g):
        rows[1, g] = (dot_t(pick[...], dyt[g]) * sg[:, 0:1]).astype(BF)
        send_rows(1, g)

    def ring_step(k):
        ju = lax.rem(r - k + 8, 8)
        jd = lax.rem(r + k, 8)
        from_below = ju < 4
        from_above = jnp.logical_and(jd < 4, k < 4)

        @pl.when(from_below)
        def _():
            ring(ju, up, up_s).wait_recv()

            @pl.when(k < 4)
            def _():
                ring(ju, up, up_s).start()

        @pl.when(from_above)
        def _():
            ring(jd, down, down_s).wait_recv()

            @pl.when(k < 3)
            def _():
                ring(jd, down, down_s).start()

        @pl.when(from_below)
        def _():
            dy_group(ju)

        @pl.when(from_above)
        def _():
            dy_group(jd)

    @pl.when(own)
    def _():
        @pl.loop(0, 4)
        def _(g):
            x_group(g)

        dy_group(zl)

    @pl.when(other)
    def _():
        @pl.loop(SKEW, pieces + 4 * SKEW)
        def _(n):
            for h, far, who in ((0, r - 3, up), (1, 8 - r, down)):
                i = n - far * SKEW

                @pl.when(jnp.logical_and(i >= 0, i < pieces))
                def _():
                    piece(h, i, who).wait_recv()

                    @pl.when(far < 4)
                    def _():
                        piece(h, i, who).start()

            for h, far in ((0, r - 3), (1, 8 - r)):
                i = n - far * SKEW
                whole = lax.rem(i + 4 * ROWBLOCKS, ROWBLOCKS) == ROWBLOCKS - 1

                @pl.when(jnp.logical_and(jnp.logical_and(i >= 0, i < pieces), whole))
                def _():
                    x_group(2 * h + lax.div(i, ROWBLOCKS))

            k = lax.div(n - RING_FIRST, RING_STEP) + 1
            turn = lax.rem(n - RING_FIRST + RING_STEP * 8, RING_STEP) == 0

            @pl.when(jnp.logical_and(jnp.logical_and(n >= RING_FIRST, k <= RING_INSIDE), turn))
            def _():
                ring_step(k)

        @pl.loop(RING_INSIDE + 1, 5)
        def _(k):
            ring_step(k)

    @pl.when(own)
    def _():
        @pl.loop(1, 4)
        def _(k):
            ring_step(k)

    def share(t, g):
        return remote(xdy.at[t, g, mine], xdy.at[t, g, mine], share_s.at[t, g], share_r.at[t, g], sibling)

    def arrived(t, g):
        some = pl.ds(0, ns - SL)
        return remote(rows.at[t, g, some], xdy.at[t, g, some], plane_s.at[t, g], plane_r.at[t, g], sibling)

    def take_in(t):
        @pl.loop(0, 4)
        def _(g):
            arrived(t, g).wait_recv()
            row_local(t, g).wait()
            share(t, g).start()

    def to_sibling(t, f):
        return remote(so.at[t, f], rb.at[t, f], sib_s.at[t, f], sib_r.at[t, f], sibling)

    def back_local(t, g):
        return pltpu.make_async_copy(ob.at[t, g, slots(me)], rv.at[t, g, slots(me)], back_l.at[t, g])

    def back_arrived(t, g):
        some = pl.ds(0, ns - SL)
        return remote(ob.at[t, g, some], rv.at[t, g, some], back_s.at[t, g], back_r.at[t, g], sibling)

    def send_back(t):
        @pl.loop(0, 4)
        def _(g):
            to_sibling(t, g).wait_recv()
            ob[t, g] = (ob[t, g].astype(F32) + rb[t, g].astype(F32)).astype(BF)

            @pl.loop(1, nq)
            def _(i):
                q = lax.rem(me + i, nq)
                remote(
                    ob.at[t, g, slots(q)], rv.at[t, g, slots(me)],
                    back_s.at[t, g], back_r.at[t, g], device(nx, q, z, c),
                ).start()

            back_local(t, g).start()

    def lanes(f):
        return slice(f * pair, (f + 1) * pair)

    take_in(0)
    weights[0].wait()
    weights[1].wait()
    gacc[...] = jnp.zeros_like(gacc)
    uacc[...] = jnp.zeros_like(uacc)

    @pl.loop(0, 4)
    def _(f):
        share(0, f).wait_recv()
        gacc[...] += jnp.dot(xdy[0, f], wg[f], preferred_element_type=F32)
        uacc[...] += jnp.dot(xdy[0, f], wu[f], preferred_element_type=F32)

    g = gacc[...]
    hb[...] = (g * jax.nn.sigmoid(g) * uacc[...]).astype(BF)
    weights[2].wait()
    for f in range(4):
        so[0, f] = jnp.dot(hb[theirs, :], wd[:, lanes(f)], preferred_element_type=F32).astype(BF)
        to_sibling(0, f).start()
        ob[0, f] = jnp.dot(hb[mine, :], wd[:, lanes(f)], preferred_element_type=F32).astype(BF)

    send_back(0)

    take_in(1)
    dacc[...] = jnp.zeros_like(dacc)
    for f in range(4):
        share(1, f).wait_recv()
        dacc[...] += dot_t(xdy[1, f], wd[:, lanes(f)])

    g = gacc[...]
    u = uacc[...]
    dh = dacc[...]
    sig = jax.nn.sigmoid(g)
    dgb[...] = (dh * u * sig * (1.0 + g * (1.0 - sig))).astype(BF)
    dub[...] = (dh * g * sig).astype(BF)
    prod = hb[...].astype(F32) * dh
    hi = prod.astype(BF)
    lo = (prod - hi.astype(F32)).astype(BF)
    ones = jnp.ones((8, prod.shape[1]), BF)
    scb[...] = (dot_t(ones, hi) + dot_t(ones, lo))[0:1, :]
    scr[pl.ds(d, 1)] = scb[...][None]

    @pl.loop(1, 8)
    def _(i):
        remote(scb, scr.at[d], dp_s, dp_r, {"expert": e, "dp": lax.rem(d + i, 8)}).start()

    @pl.loop(0, 4)
    def _(f):
        so[1, f] = (dot_t(dgb[theirs, :], wg[f]) + dot_t(dub[theirs, :], wu[f])).astype(BF)
        to_sibling(1, f).start()
        ob[1, f] = (dot_t(dgb[mine, :], wg[f]) + dot_t(dub[mine, :], wu[f])).astype(BF)

    send_back(1)

    seven = scr.at[pl.ds(0, 7)]
    dp_all = remote(seven, seven, dp_s, dp_r, sibling)
    dp_all.wait_recv()
    st[...] = jnp.sum(scr[...], axis=0)
    rsc[pl.ds(e, 1)] = st[...][None]

    @pl.loop(1, ne)
    def _(i):
        remote(st, rsc.at[e], ex_s, ex_r, {"expert": lax.rem(e + i, ne), "dp": d}).start()

    @pl.loop(0, 4)
    def _(f):
        wg[f] = tdot(xdy[0, f], dgb[...]).astype(BF)
        wu[f] = tdot(xdy[0, f], dub[...]).astype(BF)

    for f in range(4):
        wd[:, lanes(f)] = tdot(hb[...], xdy[1, f]).astype(BF)

    results = [
        pltpu.make_async_copy(a, b, out_l.at[i])
        for i, (a, b) in enumerate(((wg, gwg_ref), (wu, gwu_ref), (wd, gwd_ref)))
    ]
    for o in results:
        o.start()

    def rows_of(n):
        return pl.ds(pl.multiple_of(n * part, SL), part)

    def send_down(t, j, n):
        return remote(
            tp.at[t, j, rows_of(n)], rsd.at[t, j, rows_of(n)], ring_s.at[t, j, n], down_r.at[t, j, n], down
        )

    def send_up(t, j, n):
        return remote(
            tp.at[t, j, rows_of(n)], rsu.at[t, j, rows_of(n)], ring_s.at[t, j, n], up_r.at[t, j, n], up
        )

    def add_in(t, j, n, a):
        tp[t, j, rows_of(n)] = (
            tp[t, j, rows_of(n)].astype(F32) + a[t, j, rows_of(n)].astype(F32)
        ).astype(BF)

    def pass_on(t, g, m):
        above = lax.rem(r - g + 8, 8)
        below = lax.rem(g - r + 8, 8)

        @pl.when(above == 4 - m)
        def _():
            @pl.loop(0, PARTS)
            def _(n):
                if m > 0:
                    send_down(t, g, n).wait_recv()
                    add_in(t, g, n, rsd)
                send_down(t, g, n).start()

        if m < 3:

            @pl.when(below == 3 - m)
            def _():
                @pl.loop(0, PARTS)
                def _(n):
                    if m > 0:
                        send_up(t, g, n).wait_recv()
                        add_in(t, g, n, rsu)
                    send_up(t, g, n).start()

    @pl.loop(0, 11)
    def _(n):
        for m in (3, 2, 1):
            at = n - m

            @pl.when(jnp.logical_and(at >= 0, at < 8))
            def _():
                pass_on(lax.div(at, 4), lax.rem(at, 4), m)

        @pl.when(n < 8)
        def _():
            t = lax.div(n, 4)
            g = lax.rem(n, 4)
            back_arrived(t, g).wait_recv()
            back_local(t, g).wait()

            @pl.when(t == 0)
            def _():
                tp[0, g] = (tdot(rv[0, g], wt[0]) + tdot(rv[0, g], wt[1])).astype(BF)

            @pl.when(t == 1)
            def _():
                tp[1, g] = tdot(rv[1, g], pick[...]).astype(BF)

            pass_on(t, g, 0)

    def final(t):
        return remote(fin.at[t], fo.at[t], fin_s.at[t], fin_r.at[t], sibling)

    @pl.when(own)
    def _():
        for t in range(2):

            @pl.loop(0, PARTS)
            def _(n):
                send_down(t, zl, n).wait_recv()
                send_up(t, zl, n).wait_recv()

            def summed(core):
                some = pl.ds(pl.multiple_of(core * ch, SL), ch)
                total = tp[t, zl, some].astype(F32) + rsd[t, zl, some].astype(F32)
                return (total + rsu[t, zl, some].astype(F32)).astype(BF)

            fin[t] = summed(1 - c)
            final(t).start()
            outs[t][...] = summed(c)

        for t in range(2):
            final(t).wait_send()

        tab_out.wait_send()

    @pl.when(other)
    def _():
        for t in range(2):
            final(t).wait_recv()
            outs[t][...] = fo[t]

        gout_out.wait_send()

    some = pl.ds(0, ne - 1)
    ex_all = remote(rsc.at[some], rsc.at[some], ex_s, ex_r, sibling)
    ex_all.wait_recv()
    rsc_ref[...] = rsc[...]
    ex_all.wait_send()
    dp_all.wait_send()
    for o in results:
        o.wait()

    @pl.loop(0, pieces)
    def _(i):
        @pl.when(jnp.logical_and(r >= 3, r < 7))
        def _():
            piece(0, i, up).wait_send()

        @pl.when(jnp.logical_or(r == 0, r > 4))
        def _():
            piece(1, i, down).wait_send()

    for t in range(2):

        @pl.loop(0, 4)
        def _(g):
            arrived(t, g).wait_send()
            share(t, g).wait_send()
            to_sibling(t, g).wait_send()
            back_arrived(t, g).wait_send()

            @pl.when(g != r)
            def _():
                @pl.loop(0, PARTS)
                def _(n):
                    send_down(t, g, n).wait_send()

    @pl.loop(0, 4)
    def _(j):
        @pl.when(lax.rem(r - j + 8, 8) < 4)
        def _():
            ring(j, up, up_s).wait_send()

        @pl.when(lax.rem(j - r + 8, 8) < 3)
        def _():
            ring(j, down, down_s).wait_send()


def moe(nx, nq, tokens, gout, tabs, wg, wu, wd):
    ntok = tokens.shape[0]
    ch = gout.shape[0]
    pair = 2 * ch
    ns = nq * SL
    fh = wg.shape[2]
    hbm = pl.BlockSpec(memory_space=pl.ANY)
    vm = pl.BlockSpec(memory_space=pltpu.VMEM)
    dma = pltpu.SemaphoreType.DMA
    s = jax.ShapeDtypeStruct
    v = pltpu.VMEM
    wide = v((2, 4, ns, pair), BF)
    tall = v((2, 4, pair, ntok), BF)
    each = dma((2, 4))
    parts = dma((2, 4, PARTS))
    return pl.pallas_call(
        functools.partial(moe_kernel, nx, nq),
        out_shape=(
            s((ch, ntok), BF), s((ch, ntok), BF), s((2 * nq, 1, 2 * ns), F32),
            s(wg.shape, BF), s(wu.shape, BF), s(wd.shape, BF),
        ),
        in_specs=[hbm] * 6,
        out_specs=(vm, vm, vm, hbm, hbm, hbm),
        scratch_shapes=[
            v((4, ntok, pair), BF), v((2 * nq, ntok), F32), v((4, pair, ntok), BF), wide,
            v((2, 4, 2 * ns, pair), BF), v((ns, ntok), BF), v((ns, 128), F32), v((2, ns, ntok), BF),
            v(wg.shape, BF), v(wu.shape, BF), v(wd.shape, BF),
            v((2 * ns, fh), F32), v((2 * ns, fh), F32), v((2 * ns, fh), F32),
            v((2 * ns, fh), BF), v((2 * ns, fh), BF), v((2 * ns, fh), BF), v((1, 2 * ns), F32),
            wide, wide, wide, wide, tall, tall, tall, v((2, ch, ntok), BF), v((2, ch, ntok), BF),
            v((8, 1, 2 * ns), F32), v((1, 2 * ns), F32), v((2 * nq, 1, 2 * ns), F32),
            dma((4,)), dma, dma, dma((3,)), each, each, dma((3,)),
            dma, dma, dma, dma, dma((2, 2 * ROWBLOCKS)), dma((2, 2 * ROWBLOCKS)), dma((4,)), dma((4,)), dma((4,)),
            each, each, each, each, each, each, each, each,
            parts, parts, parts, dma((2,)), dma((2,)), dma, dma, dma, dma,
        ],
        compiler_params=pltpu.CompilerParams(
            collective_id=1, has_side_effects=True, vmem_limit_bytes=VMEM_LIMIT
        ),
        name="moe",
    )(tokens, gout, tabs, wg, wu, wd)


def on_device(nx, tokens, expert_ids, gate_values, tiles, w_gate, w_up, w_down, grad_out):
    ne = lax.axis_size("expert")
    nq = ne // 2
    ntok, width = tokens.shape
    ch = grad_out.shape[1]
    pair = 2 * ch
    live = jnp.arange(ntok, dtype=jnp.int32) < tiles[0] * TILE
    names = jnp.arange(ne, dtype=jnp.int32)[:, None, None]
    chosen = (expert_ids.T[None] == names) & live[None, None, :]
    named = jnp.any(chosen, axis=1)
    earlier = jnp.arange(ntok)[:, None] < jnp.arange(ntok)[None, :]
    rank = jnp.dot(named.astype(BF), earlier.astype(BF), preferred_element_type=F32)
    rank = jnp.where(named, rank, -1.0)
    gate = jnp.sum(jnp.where(chosen, gate_values.T[None], 0.0), axis=1)

    def halves(a):
        return a.reshape(nq // nx, 2, nx, ntok).transpose(1, 0, 2, 3).reshape(2, nq, ntok)

    tabs = jnp.concatenate([halves(rank), halves(gate)], axis=1)
    fh = w_gate.shape[2]
    wg = w_gate.reshape(4, pair, fh)
    wu = w_up.reshape(4, pair, fh)
    mixed, gtok, rsc, gwg, gwu, gwd = moe(nx, nq, tokens, grad_out.T, tabs, wg, wu, w_down[0])
    e = lax.axis_index("expert")
    zh = (e // nx) % 2
    me = (e // (2 * nx)) * nx + e % nx
    mine = lax.dynamic_slice(rsc[:, 0, :], (0, zh * nq * SL + me * SL), (ne, SL))
    slots = jnp.arange(SL, dtype=F32)
    at = jnp.sum(jnp.where(rank[:, None, :] == slots[None, :, None], mine[:, :, None], 0.0), axis=1)
    at = jnp.where(named, at / jnp.where(named, gate, 1.0), 0.0)
    grad_gates = jnp.sum(jnp.where(chosen, at[:, None, :], 0.0), axis=0).T
    return (
        mixed.T, gtok.T, grad_gates,
        gwg.reshape(1, width, fh), gwu.reshape(1, width, fh), gwd[None],
    )


def build(mesh, nx):
    placed = (
        P("expert", None),
        P("expert", None),
        P("expert", None),
        P("expert"),
        P("expert", None, "dp"),
        P("expert", None, "dp"),
        P("expert", "dp", None),
        P("expert", "dp"),
    )
    return jax.shard_map(
        functools.partial(on_device, nx),
        mesh=mesh,
        in_specs=placed,
        out_specs=(
            P("expert", "dp"),
            P("expert", "dp"),
            P("expert", None),
            P("expert", None, "dp"),
            P("expert", None, "dp"),
            P("expert", "dp", None),
        ),
        check_vma=False,
    )


def solution(mesh):
    return build(mesh, 4)
```

```python
import functools

import jax
import jax.numpy as jnp
from jax import lax
from jax.experimental import pallas as pl
from jax.experimental.pallas import tpu as pltpu
from jax.sharding import PartitionSpec as P

TILE = 128
SL = 16
MESH = pl.DeviceIdType.MESH
VMEM_LIMIT = 60 * 1024 * 1024
BF = jnp.bfloat16
F32 = jnp.float32
ROWBLOCKS = 4
PARTS = 4
SKEW = 3
RING_FIRST = 6


def place(nx):
    e = lax.axis_index("expert")
    d = lax.axis_index("dp")
    x = lax.rem(e, nx)
    zh = lax.rem(lax.div(e, nx), 2)
    y = lax.div(e, 2 * nx)
    return y * nx + x, zh, lax.div(d, 2), lax.rem(d, 2)


def device(nx, q, z, core):
    e = (lax.div(q, nx) * 2 + lax.div(z, 4)) * nx + lax.rem(q, nx)
    return {"expert": e, "dp": lax.rem(z, 4) * 2 + core}


def signal(sem, who):
    pl.semaphore_signal(sem, inc=1, device_id=who, device_id_type=MESH)


def remote(src, dst, send, recv, who):
    return pltpu.make_async_remote_copy(
        src_ref=src, dst_ref=dst, send_sem=send, recv_sem=recv, device_id=who, device_id_type=MESH
    )


def tdot(a, b):
    return lax.dot_general(a, b, (((0,), (0,)), ((), ())), preferred_element_type=F32)


def dot_t(a, b):
    return lax.dot_general(a, b, (((1,), (1,)), ((), ())), preferred_element_type=F32)


def routing(ids, gates, tiles, names):
    top, ntok = ids.shape
    named = names < 0
    gate = jnp.zeros((names.shape[0], ntok), F32)
    named = jnp.broadcast_to(named, gate.shape)
    for k in range(top):
        chosen = ids[k : k + 1, :] == names
        named = jnp.logical_or(named, chosen)
        gate = gate + jnp.where(chosen, gates[k : k + 1, :], 0.0)
    live = lax.broadcasted_iota(jnp.int32, gate.shape, 1) < tiles * TILE
    named = jnp.logical_and(named, live)
    square = (ntok, ntok)
    earlier = lax.broadcasted_iota(jnp.int32, square, 0) < lax.broadcasted_iota(jnp.int32, square, 1)
    ones = jnp.where(named, 1.0, 0.0).astype(BF)
    before = jnp.dot(ones, jnp.where(earlier, 1.0, 0.0).astype(BF), preferred_element_type=F32)
    return jnp.where(named, before, -1.0), gate


def moe_kernel(
    nx, nq, tok_ref, gout_ref, ids_ref, gates_ref, tiles_ref, wg_ref, wu_ref, wd_ref,
    mixed_ref, gtok_ref, rsc_ref, gwg_ref, gwu_ref, gwd_ref,
    tok, tabs, tabr, dyt, rows, xdy, pick, sg, wt, wg, wu, wd,
    gacc, uacc, dacc, hb, dgb, dub, scb,
    so, ob, rb, rv, tp, rsd, rsu, fin, fo, scr, st, rsc,
    tok_l, gout_l, w_l, row_l, back_l, out_l,
    tab_s, tab_r, gout_s, gout_r, x_s, x_r, up_s, down_s, ring_r,
    plane_s, plane_r, share_s, share_r, sib_s, sib_r, back_s, back_r,
    ring_s, down_r, up_r, fin_s, fin_r, dp_s, dp_r, ex_s, ex_r,
):
    me, zh, zl, c = place(nx)
    z = zh * 4 + zl
    e = lax.axis_index("expert")
    d = 2 * zl + c
    own = zh == c
    other = jnp.logical_not(own)
    r = lax.rem(z - 4 * c + 8, 8)
    ntok = tok_ref.shape[0]
    ch = gout_ref.shape[0]
    pair = 2 * ch
    ns = nq * SL
    ne = 2 * nq
    part = pair // PARTS
    up = device(nx, me, lax.rem(z + 1, 8), c)
    down = device(nx, me, lax.rem(z + 7, 8), c)
    across = device(nx, me, lax.rem(z + 4, 8), c)
    sibling = device(nx, me, z, 1 - c)
    outs = (mixed_ref, gtok_ref)
    mine = pl.ds(pl.multiple_of(c * ns, SL), ns)
    theirs = pl.ds(pl.multiple_of((1 - c) * ns, SL), ns)

    def slots(q):
        return pl.ds(pl.multiple_of(q * SL, SL), SL)

    weights = [
        pltpu.make_async_copy(a, b, w_l.at[i])
        for i, (a, b) in enumerate(((wg_ref, wg), (wu_ref, wu), (wd_ref, wd)))
    ]

    def tok_in(g):
        return pltpu.make_async_copy(tok_ref.at[:, pl.ds(g * pair, pair)], tok.at[g], tok_l.at[g])

    tab_out = remote(tabs.at[1 - zh], tabr, tab_s, tab_r, across)
    chunk = dyt.at[zl, pl.ds(pl.multiple_of(c * ch, SL), ch)]
    gout_in = pltpu.make_async_copy(gout_ref, chunk, gout_l)
    gout_out = remote(gout_ref, chunk, gout_s, gout_r, sibling)

    @pl.when(own)
    def _():
        for g in (0, 2, 1, 3):
            tok_in(g).start()
        gout_in.start()

    for w in weights:
        w.start()

    barrier = pltpu.get_barrier_semaphore()
    signal(barrier, up)
    signal(barrier, down)

    @pl.loop(1, 8)
    def _(i):
        signal(barrier, {"expert": e, "dp": lax.rem(d + i, 8)})

    @pl.loop(1, ne)
    def _(i):
        signal(barrier, {"expert": lax.rem(e + i, ne), "dp": d})

    row = lax.broadcasted_iota(jnp.int32, (nq, 1), 0)
    shift = nx.bit_length() - 1
    for h in range(2):
        names = lax.shift_right_logical(row, shift) * (2 * nx) + h * nx + jnp.bitwise_and(row, nx - 1)
        rank, gate = routing(ids_ref[...], gates_ref[...], tiles_ref[0:1, 0:1], names)
        tabs[h, 0:nq] = rank
        tabs[h, nq : 2 * nq] = gate

    @pl.when(own)
    def _():
        tabr[...] = tabs[zh]

    pl.semaphore_wait(barrier, 2 + 7 + ne - 1)

    def piece(h, i, who):
        step = ntok // ROWBLOCKS
        first = pl.multiple_of(lax.rem(i, ROWBLOCKS) * step, step)
        some = tok.at[2 * h + lax.div(i, ROWBLOCKS), pl.ds(first, step)]
        return remote(some, some, x_s.at[h, i], x_r.at[h, i], who)

    def ring(j, n, who, sems):
        some = dyt.at[j, pl.ds(pl.multiple_of(n * ch, SL), ch)]
        return remote(some, some, sems.at[j, n], ring_r.at[j, n], who)

    pieces = 2 * ROWBLOCKS

    @pl.when(own)
    def _():
        tab_out.start()
        for g in (0, 2, 1, 3):
            tok_in(g).wait()
            for i in range(ROWBLOCKS):
                n = (g % 2) * ROWBLOCKS + i
                if g < 2:

                    @pl.when(r == 3)
                    def _():
                        piece(0, n, up).start()
                else:

                    @pl.when(r == 0)
                    def _():
                        piece(1, n, down).start()

        gout_in.wait()
        ring(zl, c, up, up_s).start()
        ring(zl, c, down, down_s).start()
        gout_out.wait_recv()
        ring(zl, 1 - c, up, up_s).start()
        ring(zl, 1 - c, down, down_s).start()

    @pl.when(other)
    def _():
        gout_out.start()
        tab_out.wait_recv()

    rt = tabr[0:nq, :]
    gt = tabr[nq : 2 * nq, :]
    slot = lax.broadcasted_iota(jnp.int32, (nq, SL, ntok), 1).astype(F32)
    hit = jnp.where(jnp.broadcast_to(rt[:, None, :], (nq, SL, ntok)) == slot, 1.0, 0.0)
    heavy = (hit * jnp.broadcast_to(gt[:, None, :], (nq, SL, ntok))).reshape(ns, ntok)
    top = heavy.astype(BF)
    pick[...] = hit.reshape(ns, ntok).astype(BF)
    wt[0] = top
    wt[1] = (heavy - top.astype(F32)).astype(BF)
    sg[...] = jnp.broadcast_to(jnp.sum(heavy, axis=1, keepdims=True), sg.shape)

    def row_local(t, g):
        return pltpu.make_async_copy(
            rows.at[t, g, slots(me)], xdy.at[t, g, slots(c * nq + me)], row_l.at[t, g]
        )

    def send_rows(t, g):
        @pl.loop(1, nq)
        def _(i):
            q = lax.rem(me + i, nq)
            remote(
                rows.at[t, g, slots(q)], xdy.at[t, g, slots(c * nq + me)],
                plane_s.at[t, g], plane_r.at[t, g], device(nx, q, z, c),
            ).start()

        row_local(t, g).start()

    def x_group(g):
        rows[0, g] = jnp.dot(pick[...], tok[g], preferred_element_type=F32).astype(BF)
        send_rows(0, g)

    def dy_group(g):
        rows[1, g] = (dot_t(pick[...], dyt[g]) * sg[:, 0:1]).astype(BF)
        send_rows(1, g)

    def ring_step(k, m):
        n = lax.rem(c + m, 2)
        ju = lax.rem(r - k + 8, 8)
        jd = lax.rem(r + k, 8)
        from_below = ju < 4
        from_above = jnp.logical_and(jd < 4, k < 4)

        @pl.when(from_below)
        def _():
            ring(ju, n, up, up_s).wait_recv()

            @pl.when(k < 4)
            def _():
                ring(ju, n, up, up_s).start()

        @pl.when(from_above)
        def _():
            ring(jd, n, down, down_s).wait_recv()

            @pl.when(k < 3)
            def _():
                ring(jd, n, down, down_s).start()

        @pl.when(jnp.logical_and(from_below, m == 1))
        def _():
            dy_group(ju)

        @pl.when(jnp.logical_and(from_above, m == 1))
        def _():
            dy_group(jd)

    @pl.when(own)
    def _():
        @pl.loop(0, 11)
        def _(n):
            @pl.when(n < 2)
            def _():
                x_group(n)

            @pl.when(jnp.logical_and(n > 3, n < 6))
            def _():
                x_group(n - 2)

            @pl.when(n == 6)
            def _():
                dy_group(zl)

            @pl.when(jnp.logical_and(n > 1, n < 4))
            def _():
                ring_step(1, n - 2)

            @pl.when(n > 6)
            def _():
                ring_step(2 + lax.div(n - 7, 2), lax.rem(n - 7, 2))

    @pl.when(other)
    def _():
        @pl.loop(SKEW, pieces + 4 * SKEW)
        def _(n):
            for h, far, who in ((0, r - 3, up), (1, 8 - r, down)):
                i = n - far * SKEW

                @pl.when(jnp.logical_and(i >= 0, i < pieces))
                def _():
                    piece(h, i, who).wait_recv()

                    @pl.when(far < 4)
                    def _():
                        piece(h, i, who).start()

            for h, far in ((0, r - 3), (1, 8 - r)):
                i = n - far * SKEW
                whole = lax.rem(i + 4 * ROWBLOCKS, ROWBLOCKS) == ROWBLOCKS - 1

                @pl.when(jnp.logical_and(jnp.logical_and(i >= 0, i < pieces), whole))
                def _():
                    x_group(2 * h + lax.div(i, ROWBLOCKS))

            at = n - RING_FIRST

            @pl.when(jnp.logical_and(at >= 0, lax.rem(at + 8, 2) == 0))
            def _():
                ring_step(lax.div(at, 4) + 1, lax.div(lax.rem(at, 4), 2))

        ring_step(4, 1)

    def share(t, g):
        return remote(xdy.at[t, g, mine], xdy.at[t, g, mine], share_s.at[t, g], share_r.at[t, g], sibling)

    def arrived(t, g):
        some = pl.ds(0, ns - SL)
        return remote(rows.at[t, g, some], xdy.at[t, g, some], plane_s.at[t, g], plane_r.at[t, g], sibling)

    def take_in(t):
        @pl.loop(0, 4)
        def _(g):
            arrived(t, g).wait_recv()
            row_local(t, g).wait()
            share(t, g).start()

    def to_sibling(t, f):
        return remote(so.at[t, f], rb.at[t, f], sib_s.at[t, f], sib_r.at[t, f], sibling)

    def back_local(t, g):
        return pltpu.make_async_copy(ob.at[t, g, slots(me)], rv.at[t, g, slots(me)], back_l.at[t, g])

    def back_arrived(t, g):
        some = pl.ds(0, ns - SL)
        return remote(ob.at[t, g, some], rv.at[t, g, some], back_s.at[t, g], back_r.at[t, g], sibling)

    def send_back(t):
        @pl.loop(0, 4)
        def _(g):
            to_sibling(t, g).wait_recv()
            ob[t, g] = (ob[t, g].astype(F32) + rb[t, g].astype(F32)).astype(BF)

            @pl.loop(1, nq)
            def _(i):
                q = lax.rem(me + i, nq)
                remote(
                    ob.at[t, g, slots(q)], rv.at[t, g, slots(me)],
                    back_s.at[t, g], back_r.at[t, g], device(nx, q, z, c),
                ).start()

            back_local(t, g).start()

    def lanes(f):
        return slice(f * pair, (f + 1) * pair)

    take_in(0)
    weights[0].wait()
    weights[1].wait()
    gacc[...] = jnp.zeros_like(gacc)
    uacc[...] = jnp.zeros_like(uacc)

    @pl.loop(0, 4)
    def _(f):
        share(0, f).wait_recv()
        gacc[...] += jnp.dot(xdy[0, f], wg[f], preferred_element_type=F32)
        uacc[...] += jnp.dot(xdy[0, f], wu[f], preferred_element_type=F32)

    g = gacc[...]
    hb[...] = (g * jax.nn.sigmoid(g) * uacc[...]).astype(BF)
    weights[2].wait()
    for f in range(4):
        so[0, f] = jnp.dot(hb[theirs, :], wd[:, lanes(f)], preferred_element_type=F32).astype(BF)
        to_sibling(0, f).start()
        ob[0, f] = jnp.dot(hb[mine, :], wd[:, lanes(f)], preferred_element_type=F32).astype(BF)

    send_back(0)

    take_in(1)
    dacc[...] = jnp.zeros_like(dacc)
    for f in range(4):
        share(1, f).wait_recv()
        dacc[...] += dot_t(xdy[1, f], wd[:, lanes(f)])

    g = gacc[...]
    u = uacc[...]
    dh = dacc[...]
    sig = jax.nn.sigmoid(g)
    dgb[...] = (dh * u * sig * (1.0 + g * (1.0 - sig))).astype(BF)
    dub[...] = (dh * g * sig).astype(BF)
    prod = hb[...].astype(F32) * dh
    hi = prod.astype(BF)
    lo = (prod - hi.astype(F32)).astype(BF)
    ones = jnp.ones((8, prod.shape[1]), BF)
    scb[...] = (dot_t(ones, hi) + dot_t(ones, lo))[0:1, :]
    scr[pl.ds(d, 1)] = scb[...][None]

    @pl.loop(1, 8)
    def _(i):
        remote(scb, scr.at[d], dp_s, dp_r, {"expert": e, "dp": lax.rem(d + i, 8)}).start()

    @pl.loop(0, 4)
    def _(f):
        so[1, f] = (dot_t(dgb[theirs, :], wg[f]) + dot_t(dub[theirs, :], wu[f])).astype(BF)
        to_sibling(1, f).start()
        ob[1, f] = (dot_t(dgb[mine, :], wg[f]) + dot_t(dub[mine, :], wu[f])).astype(BF)

    send_back(1)

    seven = scr.at[pl.ds(0, 7)]
    dp_all = remote(seven, seven, dp_s, dp_r, sibling)
    dp_all.wait_recv()
    st[...] = jnp.sum(scr[...], axis=0)
    rsc[pl.ds(e, 1)] = st[...][None]

    @pl.loop(1, ne)
    def _(i):
        remote(st, rsc.at[e], ex_s, ex_r, {"expert": lax.rem(e + i, ne), "dp": d}).start()

    @pl.loop(0, 4)
    def _(f):
        wg[f] = tdot(xdy[0, f], dgb[...]).astype(BF)
        wu[f] = tdot(xdy[0, f], dub[...]).astype(BF)

    for f in range(4):
        wd[:, lanes(f)] = tdot(hb[...], xdy[1, f]).astype(BF)

    results = [
        pltpu.make_async_copy(a, b, out_l.at[i])
        for i, (a, b) in enumerate(((wg, gwg_ref), (wu, gwu_ref), (wd, gwd_ref)))
    ]
    for o in results:
        o.start()

    def rows_of(n):
        return pl.ds(pl.multiple_of(n * part, SL), part)

    def send_down(t, j, n):
        return remote(
            tp.at[t, j, rows_of(n)], rsd.at[t, j, rows_of(n)], ring_s.at[t, j, n], down_r.at[t, j, n], down
        )

    def send_up(t, j, n):
        return remote(
            tp.at[t, j, rows_of(n)], rsu.at[t, j, rows_of(n)], ring_s.at[t, j, n], up_r.at[t, j, n], up
        )

    def add_in(t, j, n, a):
        tp[t, j, rows_of(n)] = (
            tp[t, j, rows_of(n)].astype(F32) + a[t, j, rows_of(n)].astype(F32)
        ).astype(BF)

    def pass_on(t, g, m):
        above = lax.rem(r - g + 8, 8)
        below = lax.rem(g - r + 8, 8)

        @pl.when(above == 4 - m)
        def _():
            @pl.loop(0, PARTS)
            def _(n):
                if m > 0:
                    send_down(t, g, n).wait_recv()
                    add_in(t, g, n, rsd)
                send_down(t, g, n).start()

        if m < 3:

            @pl.when(below == 3 - m)
            def _():
                @pl.loop(0, PARTS)
                def _(n):
                    if m > 0:
                        send_up(t, g, n).wait_recv()
                        add_in(t, g, n, rsu)
                    send_up(t, g, n).start()

    def final(t):
        return remote(fin.at[t], fo.at[t], fin_s.at[t], fin_r.at[t], sibling)

    def finish_own(t):
        @pl.loop(0, PARTS)
        def _(n):
            send_down(t, zl, n).wait_recv()
            send_up(t, zl, n).wait_recv()

        def summed(core):
            some = pl.ds(pl.multiple_of(core * ch, SL), ch)
            total = tp[t, zl, some].astype(F32) + rsd[t, zl, some].astype(F32)
            return (total + rsu[t, zl, some].astype(F32)).astype(BF)

        fin[t] = summed(1 - c)
        final(t).start()
        outs[t][...] = summed(c)

    @pl.loop(0, 11)
    def _(n):
        for m in (3, 2, 1):
            at = n - m

            @pl.when(jnp.logical_and(at >= 0, at < 8))
            def _():
                pass_on(lax.div(at, 4), lax.rem(at, 4), m)

        @pl.when(n < 8)
        def _():
            t = lax.div(n, 4)
            g = lax.rem(n, 4)
            back_arrived(t, g).wait_recv()
            back_local(t, g).wait()

            @pl.when(t == 0)
            def _():
                tp[0, g] = (tdot(rv[0, g], wt[0]) + tdot(rv[0, g], wt[1])).astype(BF)

            @pl.when(t == 1)
            def _():
                tp[1, g] = tdot(rv[1, g], pick[...]).astype(BF)

            pass_on(t, g, 0)

        @pl.when(jnp.logical_and(n == 8, own))
        def _():
            finish_own(0)

    @pl.when(own)
    def _():
        finish_own(1)
        for t in range(2):
            final(t).wait_send()

        tab_out.wait_send()

    @pl.when(other)
    def _():
        for t in range(2):
            final(t).wait_recv()
            outs[t][...] = fo[t]

        gout_out.wait_send()

    some = pl.ds(0, ne - 1)
    ex_all = remote(rsc.at[some], rsc.at[some], ex_s, ex_r, sibling)
    ex_all.wait_recv()
    rsc_ref[...] = rsc[...].reshape(ne, 2 * ns)
    ex_all.wait_send()
    dp_all.wait_send()
    for o in results:
        o.wait()

    @pl.loop(0, pieces)
    def _(i):
        @pl.when(jnp.logical_and(r >= 3, r < 7))
        def _():
            piece(0, i, up).wait_send()

        @pl.when(jnp.logical_or(r == 0, r > 4))
        def _():
            piece(1, i, down).wait_send()

    for t in range(2):

        @pl.loop(0, 4)
        def _(g):
            arrived(t, g).wait_send()
            share(t, g).wait_send()
            to_sibling(t, g).wait_send()
            back_arrived(t, g).wait_send()

            @pl.when(g != r)
            def _():
                @pl.loop(0, PARTS)
                def _(n):
                    send_down(t, g, n).wait_send()

    @pl.loop(0, 4)
    def _(j):
        @pl.when(lax.rem(r - j + 8, 8) < 4)
        def _():
            for n in range(2):
                ring(j, n, up, up_s).wait_send()

        @pl.when(lax.rem(j - r + 8, 8) < 3)
        def _():
            for n in range(2):
                ring(j, n, down, down_s).wait_send()


def moe(nx, nq, tokens, gout, ids, gates, tiles, wg, wu, wd):
    ntok = tokens.shape[0]
    ch = gout.shape[0]
    pair = 2 * ch
    ns = nq * SL
    fh = wg.shape[2]
    hbm = pl.BlockSpec(memory_space=pl.ANY)
    vm = pl.BlockSpec(memory_space=pltpu.VMEM)
    dma = pltpu.SemaphoreType.DMA
    s = jax.ShapeDtypeStruct
    v = pltpu.VMEM
    wide = v((2, 4, ns, pair), BF)
    tall = v((2, 4, pair, ntok), BF)
    each = dma((2, 4))
    parts = dma((2, 4, PARTS))
    return pl.pallas_call(
        functools.partial(moe_kernel, nx, nq),
        out_shape=(
            s((ch, ntok), BF), s((ch, ntok), BF), s((2 * nq, 2 * ns), F32),
            s(wg.shape, BF), s(wu.shape, BF), s(wd.shape, BF),
        ),
        in_specs=[hbm, hbm, vm, vm, vm, hbm, hbm, hbm],
        out_specs=(vm, vm, vm, hbm, hbm, hbm),
        scratch_shapes=[
            v((4, ntok, pair), BF), v((2, 2 * nq, ntok), F32), v((2 * nq, ntok), F32), v((4, pair, ntok), BF), wide,
            v((2, 4, 2 * ns, pair), BF), v((ns, ntok), BF), v((ns, 128), F32), v((2, ns, ntok), BF),
            v(wg.shape, BF), v(wu.shape, BF), v(wd.shape, BF),
            v((2 * ns, fh), F32), v((2 * ns, fh), F32), v((2 * ns, fh), F32),
            v((2 * ns, fh), BF), v((2 * ns, fh), BF), v((2 * ns, fh), BF), v((1, 2 * ns), F32),
            wide, wide, wide, wide, tall, tall, tall, v((2, ch, ntok), BF), v((2, ch, ntok), BF),
            v((8, 1, 2 * ns), F32), v((1, 2 * ns), F32), v((2 * nq, 1, 2 * ns), F32),
            dma((4,)), dma, dma((3,)), each, each, dma((3,)),
            dma, dma, dma, dma, dma((2, 2 * ROWBLOCKS)), dma((2, 2 * ROWBLOCKS)), dma((4, 2)), dma((4, 2)), dma((4, 2)),
            each, each, each, each, each, each, each, each,
            parts, parts, parts, dma((2,)), dma((2,)), dma, dma, dma, dma,
        ],
        compiler_params=pltpu.CompilerParams(
            collective_id=1, has_side_effects=True, vmem_limit_bytes=VMEM_LIMIT
        ),
        name="moe",
    )(tokens, gout, ids, gates, tiles, wg, wu, wd)


def finish_kernel(nx, nq, rsc_ref, ids_ref, gates_ref, tiles_ref, *refs):
    count = (len(refs) - 2) // 2
    given, gg_ref, made, sems = refs[:count], refs[count], refs[count + 1 : -1], refs[-1]
    copies = []
    for i in range(count):
        step = given[i].shape[0] // 4
        for n in range(4):
            some = pl.ds(n * step, step)
            copies.append(pltpu.make_async_copy(given[i].at[some], made[i].at[some], sems.at[i, n]))
    for copy in copies:
        copy.start()
    me, zh, _, _ = place(nx)
    ne = 2 * nq
    ids = ids_ref[...]
    names = lax.broadcasted_iota(jnp.int32, (ne, 1), 0)
    rank, gate = routing(ids, gates_ref[...], tiles_ref[0:1, 0:1], names)
    lane = lax.broadcasted_iota(jnp.int32, rsc_ref.shape, 1) - (zh * nq + me) * SL
    at = jnp.zeros(rank.shape, F32)
    for n in range(SL):
        score = jnp.sum(jnp.where(lane == n, rsc_ref[...], 0.0), axis=1, keepdims=True)
        at = at + jnp.where(rank == float(n), score, 0.0)
    named = rank >= 0.0
    at = jnp.where(named, at / jnp.where(named, gate, 1.0), 0.0)
    for k in range(ids.shape[0]):
        gg_ref[k : k + 1, :] = jnp.sum(jnp.where(ids[k : k + 1, :] == names, at, 0.0), axis=0, keepdims=True)
    for copy in copies:
        copy.wait()


def finish(nx, nq, rsc, ids, gates, tiles, arrays):
    hbm = pl.BlockSpec(memory_space=pl.ANY)
    vm = pl.BlockSpec(memory_space=pltpu.VMEM)
    s = jax.ShapeDtypeStruct
    return pl.pallas_call(
        functools.partial(finish_kernel, nx, nq),
        out_shape=(s(ids.shape, F32), *(s(a.shape, a.dtype) for a in arrays)),
        in_specs=[vm] * 4 + [hbm] * len(arrays),
        out_specs=(vm, *([hbm] * len(arrays))),
        scratch_shapes=[pltpu.SemaphoreType.DMA((len(arrays), 4))],
        compiler_params=pltpu.CompilerParams(vmem_limit_bytes=16 * 1024 * 1024),
        name="finish",
    )(rsc, ids, gates, tiles, *arrays)


def on_device(nx, tokens, expert_ids, gate_values, tiles, w_gate, w_up, w_down, grad_out):
    nq = lax.axis_size("expert") // 2
    width = tokens.shape[1]
    pair = 2 * grad_out.shape[1]
    fh = w_gate.shape[2]
    ids = expert_ids.T
    gates = gate_values.T
    tiles = tiles.reshape(1, 1)
    wg = w_gate.reshape(4, pair, fh)
    wu = w_up.reshape(4, pair, fh)
    mixed, gtok, rsc, *grads = moe(nx, nq, tokens, grad_out.T, ids, gates, tiles, wg, wu, w_down[0])
    gg, mixed, gtok, gwg, gwu, gwd = finish(nx, nq, rsc, ids, gates, tiles, (mixed, gtok, *grads))
    return (
        mixed.T, gtok.T, gg.T,
        gwg.reshape(1, width, fh), gwu.reshape(1, width, fh), gwd[None],
    )


def build(mesh, nx):
    placed = (
        P("expert", None),
        P("expert", None),
        P("expert", None),
        P("expert"),
        P("expert", None, "dp"),
        P("expert", None, "dp"),
        P("expert", "dp", None),
        P("expert", "dp"),
    )
    return jax.shard_map(
        functools.partial(on_device, nx),
        mesh=mesh,
        in_specs=placed,
        out_specs=(
            P("expert", "dp"),
            P("expert", "dp"),
            P("expert", None),
            P("expert", None, "dp"),
            P("expert", None, "dp"),
            P("expert", "dp", None),
        ),
        check_vma=False,
    )


def solution(mesh):
    return build(mesh, 4)
```

```python
import functools

import jax
import jax.numpy as jnp
from jax import lax
from jax.experimental import pallas as pl
from jax.experimental.pallas import tpu as pltpu
from jax.sharding import PartitionSpec as P

TILE = 128
SL = 16
MESH = pl.DeviceIdType.MESH
VMEM_LIMIT = 60 * 1024 * 1024
BF = jnp.bfloat16
F32 = jnp.float32
ROWBLOCKS = 4
PARTS = 4
SKEW = 3
RING_FIRST = 6


def place(nx):
    e = lax.axis_index("expert")
    d = lax.axis_index("dp")
    x = lax.rem(e, nx)
    zh = lax.rem(lax.div(e, nx), 2)
    y = lax.div(e, 2 * nx)
    return y * nx + x, zh, lax.div(d, 2), lax.rem(d, 2)


def device(nx, q, z, core):
    e = (lax.div(q, nx) * 2 + lax.div(z, 4)) * nx + lax.rem(q, nx)
    return {"expert": e, "dp": lax.rem(z, 4) * 2 + core}


def signal(sem, who):
    pl.semaphore_signal(sem, inc=1, device_id=who, device_id_type=MESH)


def remote(src, dst, send, recv, who):
    return pltpu.make_async_remote_copy(
        src_ref=src, dst_ref=dst, send_sem=send, recv_sem=recv, device_id=who, device_id_type=MESH
    )


def tdot(a, b):
    return lax.dot_general(a, b, (((0,), (0,)), ((), ())), preferred_element_type=F32)


def dot_t(a, b):
    return lax.dot_general(a, b, (((1,), (1,)), ((), ())), preferred_element_type=F32)


def routing(ids, gates, tiles, names):
    top, ntok = ids.shape
    named = names < 0
    gate = jnp.zeros((names.shape[0], ntok), F32)
    named = jnp.broadcast_to(named, gate.shape)
    for k in range(top):
        chosen = ids[k : k + 1, :] == names
        named = jnp.logical_or(named, chosen)
        gate = gate + jnp.where(chosen, gates[k : k + 1, :], 0.0)
    live = lax.broadcasted_iota(jnp.int32, gate.shape, 1) < tiles * TILE
    named = jnp.logical_and(named, live)
    square = (ntok, ntok)
    earlier = lax.broadcasted_iota(jnp.int32, square, 0) < lax.broadcasted_iota(jnp.int32, square, 1)
    ones = jnp.where(named, 1.0, 0.0).astype(BF)
    before = jnp.dot(ones, jnp.where(earlier, 1.0, 0.0).astype(BF), preferred_element_type=F32)
    return jnp.where(named, before, -1.0), gate


def moe_kernel(
    nx, nq, tok_ref, gout_ref, ids_ref, gates_ref, tiles_ref, wg_ref, wu_ref, wd_ref,
    mixed_ref, gtok_ref, rsc_ref, gwg_ref, gwu_ref, gwd_ref,
    tok, tabs, tabr, dyt, rows, xdy, pick, sg, wt, wg, wu, wd,
    gacc, uacc, dacc, hb, dgb, dub, scb,
    so, ob, rb, rv, tp, rsd, rsu, fin, fo, scr, st, rsc,
    tok_l, gout_l, w_l, row_l, back_l, out_l,
    tab_s, tab_r, gout_s, gout_r, x_s, x_r, up_s, down_s, ring_r,
    plane_s, plane_r, share_s, share_r, sib_s, sib_r, back_s, back_r,
    ring_s, down_r, up_r, fin_s, fin_r, dp_s, dp_r, ex_s, ex_r,
):
    me, zh, zl, c = place(nx)
    z = zh * 4 + zl
    e = lax.axis_index("expert")
    d = 2 * zl + c
    own = zh == c
    other = jnp.logical_not(own)
    r = lax.rem(z - 4 * c + 8, 8)
    ntok = tok_ref.shape[0]
    ch = gout_ref.shape[0]
    pair = 2 * ch
    ns = nq * SL
    ne = 2 * nq
    part = pair // PARTS
    up = device(nx, me, lax.rem(z + 1, 8), c)
    down = device(nx, me, lax.rem(z + 7, 8), c)
    across = device(nx, me, lax.rem(z + 4, 8), c)
    sibling = device(nx, me, z, 1 - c)
    outs = (mixed_ref, gtok_ref)
    mine = pl.ds(pl.multiple_of(c * ns, SL), ns)
    theirs = pl.ds(pl.multiple_of((1 - c) * ns, SL), ns)

    def slots(q):
        return pl.ds(pl.multiple_of(q * SL, SL), SL)

    weights = [
        pltpu.make_async_copy(a, b, w_l.at[i])
        for i, (a, b) in enumerate(((wg_ref, wg), (wu_ref, wu), (wd_ref, wd)))
    ]

    def tok_in(g):
        return pltpu.make_async_copy(tok_ref.at[:, pl.ds(g * pair, pair)], tok.at[g], tok_l.at[g])

    tab_out = remote(tabs.at[1 - zh], tabr, tab_s, tab_r, across)
    chunk = dyt.at[zl, pl.ds(pl.multiple_of(c * ch, SL), ch)]
    gout_in = pltpu.make_async_copy(gout_ref, chunk, gout_l)
    gout_out = remote(gout_ref, chunk, gout_s, gout_r, sibling)

    @pl.when(own)
    def _():
        for g in (0, 2, 1, 3):
            tok_in(g).start()
        gout_in.start()

    for w in weights:
        w.start()

    barrier = pltpu.get_barrier_semaphore()
    signal(barrier, up)
    signal(barrier, down)

    @pl.loop(1, 8)
    def _(i):
        signal(barrier, {"expert": e, "dp": lax.rem(d + i, 8)})

    @pl.loop(1, ne)
    def _(i):
        signal(barrier, {"expert": lax.rem(e + i, ne), "dp": d})

    row = lax.broadcasted_iota(jnp.int32, (nq, 1), 0)
    shift = nx.bit_length() - 1
    for h in range(2):
        names = lax.shift_right_logical(row, shift) * (2 * nx) + h * nx + jnp.bitwise_and(row, nx - 1)
        rank, gate = routing(ids_ref[...], gates_ref[...], tiles_ref[0:1, 0:1], names)
        tabs[h, 0:nq] = rank
        tabs[h, nq : 2 * nq] = gate

    @pl.when(own)
    def _():
        tabr[...] = tabs[zh]

    pl.semaphore_wait(barrier, 2 + 7 + ne - 1)

    def piece(h, i, who):
        step = ntok // ROWBLOCKS
        first = pl.multiple_of(lax.rem(i, ROWBLOCKS) * step, step)
        some = tok.at[2 * h + lax.div(i, ROWBLOCKS), pl.ds(first, step)]
        return remote(some, some, x_s.at[h, i], x_r.at[h, i], who)

    def ring(j, n, who, sems):
        some = dyt.at[j, pl.ds(pl.multiple_of(n * ch, SL), ch)]
        return remote(some, some, sems.at[j, n], ring_r.at[j, n], who)

    pieces = 2 * ROWBLOCKS

    @pl.when(own)
    def _():
        tab_out.start()
        for g in (0, 2, 1, 3):
            tok_in(g).wait()
            for i in range(ROWBLOCKS):
                n = (g % 2) * ROWBLOCKS + i
                if g < 2:

                    @pl.when(r == 3)
                    def _():
                        piece(0, n, up).start()
                else:

                    @pl.when(r == 0)
                    def _():
                        piece(1, n, down).start()

        gout_in.wait()
        ring(zl, c, up, up_s).start()
        ring(zl, c, down, down_s).start()
        gout_out.wait_recv()
        ring(zl, 1 - c, up, up_s).start()
        ring(zl, 1 - c, down, down_s).start()

    @pl.when(other)
    def _():
        gout_out.start()
        tab_out.wait_recv()

    rt = tabr[0:nq, :]
    gt = tabr[nq : 2 * nq, :]
    slot = lax.broadcasted_iota(jnp.int32, (nq, SL, ntok), 1).astype(F32)
    hit = jnp.where(jnp.broadcast_to(rt[:, None, :], (nq, SL, ntok)) == slot, 1.0, 0.0)
    heavy = (hit * jnp.broadcast_to(gt[:, None, :], (nq, SL, ntok))).reshape(ns, ntok)
    top = heavy.astype(BF)
    pick[...] = hit.reshape(ns, ntok).astype(BF)
    wt[0] = top
    wt[1] = (heavy - top.astype(F32)).astype(BF)
    sg[...] = jnp.broadcast_to(jnp.sum(heavy, axis=1, keepdims=True), sg.shape)

    def row_local(t, g):
        return pltpu.make_async_copy(
            rows.at[t, g, slots(me)], xdy.at[t, g, slots(c * nq + me)], row_l.at[t, g]
        )

    def send_rows(t, g):
        @pl.loop(1, nq)
        def _(i):
            q = lax.rem(me + i, nq)
            remote(
                rows.at[t, g, slots(q)], xdy.at[t, g, slots(c * nq + me)],
                plane_s.at[t, g], plane_r.at[t, g], device(nx, q, z, c),
            ).start()

        row_local(t, g).start()

    def x_group(g):
        rows[0, g] = jnp.dot(pick[...], tok[g], preferred_element_type=F32).astype(BF)
        send_rows(0, g)

    def dy_group(g):
        rows[1, g] = (dot_t(pick[...], dyt[g]) * sg[:, 0:1]).astype(BF)
        send_rows(1, g)

    def ring_step(k, m):
        n = lax.rem(c + m, 2)
        ju = lax.rem(r - k + 8, 8)
        jd = lax.rem(r + k, 8)
        from_below = ju < 4
        from_above = jnp.logical_and(jd < 4, k < 4)

        @pl.when(from_below)
        def _():
            ring(ju, n, up, up_s).wait_recv()

            @pl.when(k < 4)
            def _():
                ring(ju, n, up, up_s).start()

        @pl.when(from_above)
        def _():
            ring(jd, n, down, down_s).wait_recv()

            @pl.when(k < 3)
            def _():
                ring(jd, n, down, down_s).start()

        @pl.when(jnp.logical_and(from_below, m == 1))
        def _():
            dy_group(ju)

        @pl.when(jnp.logical_and(from_above, m == 1))
        def _():
            dy_group(jd)

    @pl.when(own)
    def _():
        @pl.loop(0, 11)
        def _(n):
            @pl.when(n < 2)
            def _():
                x_group(n)

            @pl.when(jnp.logical_and(n > 3, n < 6))
            def _():
                x_group(n - 2)

            @pl.when(n == 6)
            def _():
                dy_group(zl)

            @pl.when(jnp.logical_and(n > 1, n < 4))
            def _():
                ring_step(1, n - 2)

            @pl.when(n > 6)
            def _():
                ring_step(2 + lax.div(n - 7, 2), lax.rem(n - 7, 2))

    @pl.when(other)
    def _():
        @pl.loop(SKEW, pieces + 4 * SKEW)
        def _(n):
            for h, far, who in ((0, r - 3, up), (1, 8 - r, down)):
                i = n - far * SKEW

                @pl.when(jnp.logical_and(i >= 0, i < pieces))
                def _():
                    piece(h, i, who).wait_recv()

                    @pl.when(far < 4)
                    def _():
                        piece(h, i, who).start()

            for h, far in ((0, r - 3), (1, 8 - r)):
                i = n - far * SKEW
                whole = lax.rem(i + 4 * ROWBLOCKS, ROWBLOCKS) == ROWBLOCKS - 1

                @pl.when(jnp.logical_and(jnp.logical_and(i >= 0, i < pieces), whole))
                def _():
                    x_group(2 * h + lax.div(i, ROWBLOCKS))

            at = n - RING_FIRST

            @pl.when(jnp.logical_and(at >= 0, lax.rem(at + 8, 2) == 0))
            def _():
                ring_step(lax.div(at, 4) + 1, lax.div(lax.rem(at, 4), 2))

        ring_step(4, 1)

    def share(t, g):
        return remote(xdy.at[t, g, mine], xdy.at[t, g, mine], share_s.at[t, g], share_r.at[t, g], sibling)

    def arrived(t, g):
        some = pl.ds(0, ns - SL)
        return remote(rows.at[t, g, some], xdy.at[t, g, some], plane_s.at[t, g], plane_r.at[t, g], sibling)

    def take_in(t):
        @pl.loop(0, 4)
        def _(g):
            arrived(t, g).wait_recv()
            row_local(t, g).wait()
            share(t, g).start()

    def to_sibling(t, f):
        return remote(so.at[t, f], rb.at[t, f], sib_s.at[t, f], sib_r.at[t, f], sibling)

    def back_local(t, g):
        return pltpu.make_async_copy(ob.at[t, g, slots(me)], rv.at[t, g, slots(me)], back_l.at[t, g])

    def back_arrived(t, g):
        some = pl.ds(0, ns - SL)
        return remote(ob.at[t, g, some], rv.at[t, g, some], back_s.at[t, g], back_r.at[t, g], sibling)

    def send_back(t):
        @pl.loop(0, 4)
        def _(g):
            to_sibling(t, g).wait_recv()
            ob[t, g] = (ob[t, g].astype(F32) + rb[t, g].astype(F32)).astype(BF)

            @pl.loop(1, nq)
            def _(i):
                q = lax.rem(me + i, nq)
                remote(
                    ob.at[t, g, slots(q)], rv.at[t, g, slots(me)],
                    back_s.at[t, g], back_r.at[t, g], device(nx, q, z, c),
                ).start()

            back_local(t, g).start()

    def lanes(f):
        return slice(f * pair, (f + 1) * pair)

    take_in(0)
    weights[0].wait()
    weights[1].wait()
    gacc[...] = jnp.zeros_like(gacc)
    uacc[...] = jnp.zeros_like(uacc)

    @pl.loop(0, 4)
    def _(f):
        share(0, f).wait_recv()
        gacc[...] += jnp.dot(xdy[0, f], wg[f], preferred_element_type=F32)
        uacc[...] += jnp.dot(xdy[0, f], wu[f], preferred_element_type=F32)

    g = gacc[...]
    hb[...] = (g * jax.nn.sigmoid(g) * uacc[...]).astype(BF)
    weights[2].wait()
    for f in range(4):
        so[0, f] = jnp.dot(hb[theirs, :], wd[:, lanes(f)], preferred_element_type=F32).astype(BF)
        to_sibling(0, f).start()
        ob[0, f] = jnp.dot(hb[mine, :], wd[:, lanes(f)], preferred_element_type=F32).astype(BF)

    send_back(0)

    def rows_of(n):
        return pl.ds(pl.multiple_of(n * part, SL), part)

    def send_down(t, j, n):
        return remote(
            tp.at[t, j, rows_of(n)], rsd.at[t, j, rows_of(n)], ring_s.at[t, j, n], down_r.at[t, j, n], down
        )

    def send_up(t, j, n):
        return remote(
            tp.at[t, j, rows_of(n)], rsu.at[t, j, rows_of(n)], ring_s.at[t, j, n], up_r.at[t, j, n], up
        )

    def add_in(t, j, n, a):
        tp[t, j, rows_of(n)] = (
            tp[t, j, rows_of(n)].astype(F32) + a[t, j, rows_of(n)].astype(F32)
        ).astype(BF)

    def pass_on(t, g, m):
        above = lax.rem(r - g + 8, 8)
        below = lax.rem(g - r + 8, 8)

        @pl.when(above == 4 - m)
        def _():
            @pl.loop(0, PARTS)
            def _(n):
                if m > 0:
                    send_down(t, g, n).wait_recv()
                    add_in(t, g, n, rsd)
                send_down(t, g, n).start()

        if m < 3:

            @pl.when(below == 3 - m)
            def _():
                @pl.loop(0, PARTS)
                def _(n):
                    if m > 0:
                        send_up(t, g, n).wait_recv()
                        add_in(t, g, n, rsu)
                    send_up(t, g, n).start()

    def return_step(n):
        for m in (3, 2, 1):
            at = n - m

            @pl.when(jnp.logical_and(at >= 0, at < 8))
            def _():
                pass_on(lax.div(at, 4), lax.rem(at, 4), m)

        @pl.when(n < 8)
        def _():
            t = lax.div(n, 4)
            g = lax.rem(n, 4)
            back_arrived(t, g).wait_recv()
            back_local(t, g).wait()

            @pl.when(t == 0)
            def _():
                tp[0, g] = (tdot(rv[0, g], wt[0]) + tdot(rv[0, g], wt[1])).astype(BF)

            @pl.when(t == 1)
            def _():
                tp[1, g] = tdot(rv[1, g], pick[...]).astype(BF)

            pass_on(t, g, 0)

    take_in(1)
    dacc[...] = jnp.zeros_like(dacc)
    for f in range(4):
        share(1, f).wait_recv()
        dacc[...] += dot_t(xdy[1, f], wd[:, lanes(f)])

    g = gacc[...]
    u = uacc[...]
    dh = dacc[...]
    sig = jax.nn.sigmoid(g)
    dgb[...] = (dh * u * sig * (1.0 + g * (1.0 - sig))).astype(BF)
    dub[...] = (dh * g * sig).astype(BF)
    prod = hb[...].astype(F32) * dh
    hi = prod.astype(BF)
    lo = (prod - hi.astype(F32)).astype(BF)
    ones = jnp.ones((8, prod.shape[1]), BF)
    scb[...] = (dot_t(ones, hi) + dot_t(ones, lo))[0:1, :]
    scr[pl.ds(d, 1)] = scb[...][None]

    @pl.loop(1, 8)
    def _(i):
        remote(scb, scr.at[d], dp_s, dp_r, {"expert": e, "dp": lax.rem(d + i, 8)}).start()

    @pl.loop(0, 4)
    def _(f):
        so[1, f] = (dot_t(dgb[theirs, :], wg[f]) + dot_t(dub[theirs, :], wu[f])).astype(BF)
        to_sibling(1, f).start()
        ob[1, f] = (dot_t(dgb[mine, :], wg[f]) + dot_t(dub[mine, :], wu[f])).astype(BF)
        return_step(f)

    send_back(1)

    seven = scr.at[pl.ds(0, 7)]
    dp_all = remote(seven, seven, dp_s, dp_r, sibling)
    dp_all.wait_recv()
    st[...] = jnp.sum(scr[...], axis=0)
    rsc[pl.ds(e, 1)] = st[...][None]

    @pl.loop(1, ne)
    def _(i):
        remote(st, rsc.at[e], ex_s, ex_r, {"expert": lax.rem(e + i, ne), "dp": d}).start()

    def final(t):
        return remote(fin.at[t], fo.at[t], fin_s.at[t], fin_r.at[t], sibling)

    def finish_own(t):
        @pl.loop(0, PARTS)
        def _(n):
            send_down(t, zl, n).wait_recv()
            send_up(t, zl, n).wait_recv()

        def summed(core):
            some = pl.ds(pl.multiple_of(core * ch, SL), ch)
            total = tp[t, zl, some].astype(F32) + rsd[t, zl, some].astype(F32)
            return (total + rsu[t, zl, some].astype(F32)).astype(BF)

        fin[t] = summed(1 - c)
        final(t).start()
        outs[t][...] = summed(c)

    results = [
        pltpu.make_async_copy(a, b, out_l.at[i])
        for i, (a, b) in enumerate(((wg, gwg_ref), (wu, gwu_ref), (wd, gwd_ref)))
    ]

    @pl.loop(4, 11)
    def _(n):
        return_step(n)

        @pl.when(n < 8)
        def _():
            f = n - 4
            some = pl.ds(pl.multiple_of(f * pair, 128), pair)
            wg[f] = tdot(xdy[0, f], dgb[...]).astype(BF)
            wu[f] = tdot(xdy[0, f], dub[...]).astype(BF)
            wd[:, some] = tdot(hb[...], xdy[1, f]).astype(BF)

        @pl.when(n == 8)
        def _():
            for o in results:
                o.start()

            @pl.when(own)
            def _():
                finish_own(0)

    @pl.when(own)
    def _():
        finish_own(1)
        for t in range(2):
            final(t).wait_send()

        tab_out.wait_send()

    @pl.when(other)
    def _():
        for t in range(2):
            final(t).wait_recv()
            outs[t][...] = fo[t]

        gout_out.wait_send()

    some = pl.ds(0, ne - 1)
    ex_all = remote(rsc.at[some], rsc.at[some], ex_s, ex_r, sibling)
    ex_all.wait_recv()
    rsc_ref[...] = rsc[...].reshape(ne, 2 * ns)
    ex_all.wait_send()
    dp_all.wait_send()
    for o in results:
        o.wait()

    @pl.loop(0, pieces)
    def _(i):
        @pl.when(jnp.logical_and(r >= 3, r < 7))
        def _():
            piece(0, i, up).wait_send()

        @pl.when(jnp.logical_or(r == 0, r > 4))
        def _():
            piece(1, i, down).wait_send()

    for t in range(2):

        @pl.loop(0, 4)
        def _(g):
            arrived(t, g).wait_send()
            share(t, g).wait_send()
            to_sibling(t, g).wait_send()
            back_arrived(t, g).wait_send()

            @pl.when(g != r)
            def _():
                @pl.loop(0, PARTS)
                def _(n):
                    send_down(t, g, n).wait_send()

    @pl.loop(0, 4)
    def _(j):
        @pl.when(lax.rem(r - j + 8, 8) < 4)
        def _():
            for n in range(2):
                ring(j, n, up, up_s).wait_send()

        @pl.when(lax.rem(j - r + 8, 8) < 3)
        def _():
            for n in range(2):
                ring(j, n, down, down_s).wait_send()


def moe(nx, nq, tokens, gout, ids, gates, tiles, wg, wu, wd):
    ntok = tokens.shape[0]
    ch = gout.shape[0]
    pair = 2 * ch
    ns = nq * SL
    fh = wg.shape[2]
    hbm = pl.BlockSpec(memory_space=pl.ANY)
    vm = pl.BlockSpec(memory_space=pltpu.VMEM)
    dma = pltpu.SemaphoreType.DMA
    s = jax.ShapeDtypeStruct
    v = pltpu.VMEM
    wide = v((2, 4, ns, pair), BF)
    tall = v((2, 4, pair, ntok), BF)
    each = dma((2, 4))
    parts = dma((2, 4, PARTS))
    return pl.pallas_call(
        functools.partial(moe_kernel, nx, nq),
        out_shape=(
            s((ch, ntok), BF), s((ch, ntok), BF), s((2 * nq, 2 * ns), F32),
            s(wg.shape, BF), s(wu.shape, BF), s(wd.shape, BF),
        ),
        in_specs=[hbm, hbm, vm, vm, vm, hbm, hbm, hbm],
        out_specs=(vm, vm, vm, hbm, hbm, hbm),
        scratch_shapes=[
            v((4, ntok, pair), BF), v((2, 2 * nq, ntok), F32), v((2 * nq, ntok), F32), v((4, pair, ntok), BF), wide,
            v((2, 4, 2 * ns, pair), BF), v((ns, ntok), BF), v((ns, 128), F32), v((2, ns, ntok), BF),
            v(wg.shape, BF), v(wu.shape, BF), v(wd.shape, BF),
            v((2 * ns, fh), F32), v((2 * ns, fh), F32), v((2 * ns, fh), F32),
            v((2 * ns, fh), BF), v((2 * ns, fh), BF), v((2 * ns, fh), BF), v((1, 2 * ns), F32),
            wide, wide, wide, wide, tall, tall, tall, v((2, ch, ntok), BF), v((2, ch, ntok), BF),
            v((8, 1, 2 * ns), F32), v((1, 2 * ns), F32), v((2 * nq, 1, 2 * ns), F32),
            dma((4,)), dma, dma((3,)), each, each, dma((3,)),
            dma, dma, dma, dma, dma((2, 2 * ROWBLOCKS)), dma((2, 2 * ROWBLOCKS)), dma((4, 2)), dma((4, 2)), dma((4, 2)),
            each, each, each, each, each, each, each, each,
            parts, parts, parts, dma((2,)), dma((2,)), dma, dma, dma, dma,
        ],
        compiler_params=pltpu.CompilerParams(
            collective_id=1, has_side_effects=True, vmem_limit_bytes=VMEM_LIMIT
        ),
        name="moe",
    )(tokens, gout, ids, gates, tiles, wg, wu, wd)


def finish_kernel(nx, nq, rsc_ref, ids_ref, gates_ref, tiles_ref, *refs):
    count = (len(refs) - 2) // 2
    given, gg_ref, made, sems = refs[:count], refs[count], refs[count + 1 : -1], refs[-1]
    copies = []
    for i in range(count):
        step = given[i].shape[0] // 4
        for n in range(4):
            some = pl.ds(n * step, step)
            copies.append(pltpu.make_async_copy(given[i].at[some], made[i].at[some], sems.at[i, n]))
    for copy in copies:
        copy.start()
    me, zh, _, _ = place(nx)
    ne = 2 * nq
    ids = ids_ref[...]
    names = lax.broadcasted_iota(jnp.int32, (ne, 1), 0)
    rank, gate = routing(ids, gates_ref[...], tiles_ref[0:1, 0:1], names)
    lane = lax.broadcasted_iota(jnp.int32, rsc_ref.shape, 1) - (zh * nq + me) * SL
    at = jnp.zeros(rank.shape, F32)
    for n in range(SL):
        score = jnp.sum(jnp.where(lane == n, rsc_ref[...], 0.0), axis=1, keepdims=True)
        at = at + jnp.where(rank == float(n), score, 0.0)
    named = rank >= 0.0
    at = jnp.where(named, at / jnp.where(named, gate, 1.0), 0.0)
    for k in range(ids.shape[0]):
        gg_ref[k : k + 1, :] = jnp.sum(jnp.where(ids[k : k + 1, :] == names, at, 0.0), axis=0, keepdims=True)
    for copy in copies:
        copy.wait()


def finish(nx, nq, rsc, ids, gates, tiles, arrays):
    hbm = pl.BlockSpec(memory_space=pl.ANY)
    vm = pl.BlockSpec(memory_space=pltpu.VMEM)
    s = jax.ShapeDtypeStruct
    return pl.pallas_call(
        functools.partial(finish_kernel, nx, nq),
        out_shape=(s(ids.shape, F32), *(s(a.shape, a.dtype) for a in arrays)),
        in_specs=[vm] * 4 + [hbm] * len(arrays),
        out_specs=(vm, *([hbm] * len(arrays))),
        scratch_shapes=[pltpu.SemaphoreType.DMA((len(arrays), 4))],
        compiler_params=pltpu.CompilerParams(vmem_limit_bytes=VMEM_LIMIT),
        name="finish",
    )(rsc, ids, gates, tiles, *arrays)


def on_device(nx, tokens, expert_ids, gate_values, tiles, w_gate, w_up, w_down, grad_out):
    nq = lax.axis_size("expert") // 2
    width = tokens.shape[1]
    pair = 2 * grad_out.shape[1]
    fh = w_gate.shape[2]
    ids = expert_ids.T
    gates = gate_values.T
    tiles = tiles.reshape(1, 1)
    wg = w_gate.reshape(4, pair, fh)
    wu = w_up.reshape(4, pair, fh)
    mixed, gtok, rsc, *grads = moe(nx, nq, tokens, grad_out.T, ids, gates, tiles, wg, wu, w_down[0])
    gg, mixed, gtok, gwg, gwu, gwd = finish(nx, nq, rsc, ids, gates, tiles, (mixed, gtok, *grads))
    return (
        mixed.T, gtok.T, gg.T,
        gwg.reshape(1, width, fh), gwu.reshape(1, width, fh), gwd[None],
    )


def build(mesh, nx):
    placed = (
        P("expert", None),
        P("expert", None),
        P("expert", None),
        P("expert"),
        P("expert", None, "dp"),
        P("expert", None, "dp"),
        P("expert", "dp", None),
        P("expert", "dp"),
    )
    return jax.shard_map(
        functools.partial(on_device, nx),
        mesh=mesh,
        in_specs=placed,
        out_specs=(
            P("expert", "dp"),
            P("expert", "dp"),
            P("expert", None),
            P("expert", None, "dp"),
            P("expert", None, "dp"),
            P("expert", "dp", None),
        ),
        check_vma=False,
    )


def solution(mesh):
    return build(mesh, 4)
```

```python
import functools

import jax
import jax.numpy as jnp
from jax import lax
from jax.experimental import pallas as pl
from jax.experimental.pallas import tpu as pltpu
from jax.sharding import PartitionSpec as P

TILE = 128
SL = 16
MESH = pl.DeviceIdType.MESH
VMEM_LIMIT = 60 * 1024 * 1024
BF = jnp.bfloat16
F32 = jnp.float32
ROWBLOCKS = 4
PARTS = 4
SKEW = 3
RING_FIRST = 6


def place(nx):
    e = lax.axis_index("expert")
    d = lax.axis_index("dp")
    x = lax.rem(e, nx)
    zh = lax.rem(lax.div(e, nx), 2)
    y = lax.div(e, 2 * nx)
    return y * nx + x, zh, lax.div(d, 2), lax.rem(d, 2)


def device(nx, q, z, core):
    e = (lax.div(q, nx) * 2 + lax.div(z, 4)) * nx + lax.rem(q, nx)
    return {"expert": e, "dp": lax.rem(z, 4) * 2 + core}


def signal(sem, who):
    pl.semaphore_signal(sem, inc=1, device_id=who, device_id_type=MESH)


def remote(src, dst, send, recv, who):
    return pltpu.make_async_remote_copy(
        src_ref=src, dst_ref=dst, send_sem=send, recv_sem=recv, device_id=who, device_id_type=MESH
    )


def tdot(a, b):
    return lax.dot_general(a, b, (((0,), (0,)), ((), ())), preferred_element_type=F32)


def dot_t(a, b):
    return lax.dot_general(a, b, (((1,), (1,)), ((), ())), preferred_element_type=F32)


def routing(ids, gates, tiles, names):
    top, ntok = ids.shape
    named = names < 0
    gate = jnp.zeros((names.shape[0], ntok), F32)
    named = jnp.broadcast_to(named, gate.shape)
    for k in range(top):
        chosen = ids[k : k + 1, :] == names
        named = jnp.logical_or(named, chosen)
        gate = gate + jnp.where(chosen, gates[k : k + 1, :], 0.0)
    live = lax.broadcasted_iota(jnp.int32, gate.shape, 1) < tiles * TILE
    named = jnp.logical_and(named, live)
    square = (ntok, ntok)
    earlier = lax.broadcasted_iota(jnp.int32, square, 0) < lax.broadcasted_iota(jnp.int32, square, 1)
    ones = jnp.where(named, 1.0, 0.0).astype(BF)
    before = jnp.dot(ones, jnp.where(earlier, 1.0, 0.0).astype(BF), preferred_element_type=F32)
    return jnp.where(named, before, -1.0), gate


def moe_kernel(
    nx, nq, tok_ref, gout_ref, ids_ref, gates_ref, tiles_ref, wg_ref, wu_ref, wd_ref,
    mixed_ref, gtok_ref, rsc_ref, gwg_ref, gwu_ref, gwd_ref,
    tok, tabs, tabr, dyt, rows, xdy, pick, sg, wt, wg, wu, wd,
    gacc, uacc, dacc, hb, dgb, dub, scb,
    so, ob, rb, rv, tp, rsd, rsu, fin, fo, scr, st, rsc,
    tok_l, gout_l, w_l, row_l, back_l, out_l,
    tab_s, tab_r, gout_s, gout_r, x_s, x_r, up_s, down_s, ring_r,
    plane_s, plane_r, share_s, share_r, sib_s, sib_r, back_s, back_r,
    ring_s, down_r, up_r, fin_s, fin_r, dp_s, dp_r, ex_s, ex_r,
):
    me, zh, zl, c = place(nx)
    z = zh * 4 + zl
    e = lax.axis_index("expert")
    d = 2 * zl + c
    own = zh == c
    other = jnp.logical_not(own)
    r = lax.rem(z - 4 * c + 8, 8)
    ntok = tok_ref.shape[0]
    ch = gout_ref.shape[0]
    pair = 2 * ch
    ns = nq * SL
    ne = 2 * nq
    part = pair // PARTS
    up = device(nx, me, lax.rem(z + 1, 8), c)
    down = device(nx, me, lax.rem(z + 7, 8), c)
    across = device(nx, me, lax.rem(z + 4, 8), c)
    sibling = device(nx, me, z, 1 - c)
    outs = (mixed_ref, gtok_ref)
    mine = pl.ds(pl.multiple_of(c * ns, SL), ns)
    theirs = pl.ds(pl.multiple_of((1 - c) * ns, SL), ns)

    def slots(q):
        return pl.ds(pl.multiple_of(q * SL, SL), SL)

    weights = [
        pltpu.make_async_copy(a, b, w_l.at[i])
        for i, (a, b) in enumerate(((wg_ref, wg), (wu_ref, wu), (wd_ref, wd)))
    ]

    def tok_in(g):
        return pltpu.make_async_copy(tok_ref.at[:, pl.ds(g * pair, pair)], tok.at[g], tok_l.at[g])

    tab_out = remote(tabs.at[1 - zh], tabr, tab_s, tab_r, across)
    chunk = dyt.at[zl, pl.ds(pl.multiple_of(c * ch, SL), ch)]
    gout_in = pltpu.make_async_copy(gout_ref, chunk, gout_l)
    gout_out = remote(gout_ref, chunk, gout_s, gout_r, sibling)

    @pl.when(own)
    def _():
        for g in (0, 2, 1, 3):
            tok_in(g).start()
        gout_in.start()

    for w in weights:
        w.start()

    barrier = pltpu.get_barrier_semaphore()
    signal(barrier, up)
    signal(barrier, down)

    @pl.loop(1, 8)
    def _(i):
        signal(barrier, {"expert": e, "dp": lax.rem(d + i, 8)})

    @pl.loop(1, ne)
    def _(i):
        signal(barrier, {"expert": lax.rem(e + i, ne), "dp": d})

    row = lax.broadcasted_iota(jnp.int32, (nq, 1), 0)
    shift = nx.bit_length() - 1
    for h in range(2):
        names = lax.shift_right_logical(row, shift) * (2 * nx) + h * nx + jnp.bitwise_and(row, nx - 1)
        rank, gate = routing(ids_ref[...], gates_ref[...], tiles_ref[0:1, 0:1], names)
        tabs[h, 0:nq] = rank
        tabs[h, nq : 2 * nq] = gate

    @pl.when(own)
    def _():
        tabr[...] = tabs[zh]

    pl.semaphore_wait(barrier, 2 + 7 + ne - 1)

    def piece(h, i, who):
        step = ntok // ROWBLOCKS
        first = pl.multiple_of(lax.rem(i, ROWBLOCKS) * step, step)
        some = tok.at[2 * h + lax.div(i, ROWBLOCKS), pl.ds(first, step)]
        return remote(some, some, x_s.at[h, i], x_r.at[h, i], who)

    def ring(j, n, who, sems):
        some = dyt.at[j, pl.ds(pl.multiple_of(n * ch, SL), ch)]
        return remote(some, some, sems.at[j, n], ring_r.at[j, n], who)

    pieces = 2 * ROWBLOCKS

    @pl.when(own)
    def _():
        tab_out.start()
        for g in (0, 2, 1, 3):
            tok_in(g).wait()
            for i in range(ROWBLOCKS):
                n = (g % 2) * ROWBLOCKS + i
                if g < 2:

                    @pl.when(r == 3)
                    def _():
                        piece(0, n, up).start()
                else:

                    @pl.when(r == 0)
                    def _():
                        piece(1, n, down).start()

        gout_in.wait()
        ring(zl, c, up, up_s).start()
        ring(zl, c, down, down_s).start()
        gout_out.wait_recv()
        ring(zl, 1 - c, up, up_s).start()
        ring(zl, 1 - c, down, down_s).start()

    @pl.when(other)
    def _():
        gout_out.start()
        tab_out.wait_recv()

    rt = tabr[0:nq, :]
    gt = tabr[nq : 2 * nq, :]
    slot = lax.broadcasted_iota(jnp.int32, (nq, SL, ntok), 1).astype(F32)
    hit = jnp.where(jnp.broadcast_to(rt[:, None, :], (nq, SL, ntok)) == slot, 1.0, 0.0)
    heavy = (hit * jnp.broadcast_to(gt[:, None, :], (nq, SL, ntok))).reshape(ns, ntok)
    top = heavy.astype(BF)
    pick[...] = hit.reshape(ns, ntok).astype(BF)
    wt[0] = top
    wt[1] = (heavy - top.astype(F32)).astype(BF)
    sg[...] = jnp.broadcast_to(jnp.sum(heavy, axis=1, keepdims=True), sg.shape)

    def row_local(t, g):
        return pltpu.make_async_copy(
            rows.at[t, g, slots(me)], xdy.at[t, g, slots(c * nq + me)], row_l.at[t, g]
        )

    def send_rows(t, g):
        @pl.loop(1, nq)
        def _(i):
            q = lax.rem(me + i, nq)
            remote(
                rows.at[t, g, slots(q)], xdy.at[t, g, slots(c * nq + me)],
                plane_s.at[t, g], plane_r.at[t, g], device(nx, q, z, c),
            ).start()

        row_local(t, g).start()

    def x_group(g):
        rows[0, g] = jnp.dot(pick[...], tok[g], preferred_element_type=F32).astype(BF)
        send_rows(0, g)

    def dy_group(g):
        rows[1, g] = (dot_t(pick[...], dyt[g]) * sg[:, 0:1]).astype(BF)
        send_rows(1, g)

    def ring_step(k, m):
        n = lax.rem(c + m, 2)
        ju = lax.rem(r - k + 8, 8)
        jd = lax.rem(r + k, 8)
        from_below = ju < 4
        from_above = jnp.logical_and(jd < 4, k < 4)

        @pl.when(from_below)
        def _():
            ring(ju, n, up, up_s).wait_recv()

            @pl.when(k < 4)
            def _():
                ring(ju, n, up, up_s).start()

        @pl.when(from_above)
        def _():
            ring(jd, n, down, down_s).wait_recv()

            @pl.when(k < 3)
            def _():
                ring(jd, n, down, down_s).start()

        @pl.when(jnp.logical_and(from_below, m == 1))
        def _():
            dy_group(ju)

        @pl.when(jnp.logical_and(from_above, m == 1))
        def _():
            dy_group(jd)

    @pl.when(own)
    def _():
        @pl.loop(0, 11)
        def _(n):
            @pl.when(n < 2)
            def _():
                x_group(n)

            @pl.when(jnp.logical_and(n > 3, n < 6))
            def _():
                x_group(n - 2)

            @pl.when(n == 6)
            def _():
                dy_group(zl)

            @pl.when(jnp.logical_and(n > 1, n < 4))
            def _():
                ring_step(1, n - 2)

            @pl.when(n > 6)
            def _():
                ring_step(2 + lax.div(n - 7, 2), lax.rem(n - 7, 2))

    @pl.when(other)
    def _():
        @pl.loop(SKEW, pieces + 4 * SKEW)
        def _(n):
            for h, far, who in ((0, r - 3, up), (1, 8 - r, down)):
                i = n - far * SKEW

                @pl.when(jnp.logical_and(i >= 0, i < pieces))
                def _():
                    piece(h, i, who).wait_recv()

                    @pl.when(far < 4)
                    def _():
                        piece(h, i, who).start()

            for h, far in ((0, r - 3), (1, 8 - r)):
                i = n - far * SKEW
                whole = lax.rem(i + 4 * ROWBLOCKS, ROWBLOCKS) == ROWBLOCKS - 1

                @pl.when(jnp.logical_and(jnp.logical_and(i >= 0, i < pieces), whole))
                def _():
                    x_group(2 * h + lax.div(i, ROWBLOCKS))

            at = n - RING_FIRST

            @pl.when(jnp.logical_and(at >= 0, lax.rem(at + 8, 2) == 0))
            def _():
                ring_step(lax.div(at, 4) + 1, lax.div(lax.rem(at, 4), 2))

        ring_step(4, 1)

    def share(t, g):
        return remote(xdy.at[t, g, mine], xdy.at[t, g, mine], share_s.at[t, g], share_r.at[t, g], sibling)

    def arrived(t, g):
        some = pl.ds(0, ns - SL)
        return remote(rows.at[t, g, some], xdy.at[t, g, some], plane_s.at[t, g], plane_r.at[t, g], sibling)

    def take_in(t):
        @pl.loop(0, 4)
        def _(g):
            arrived(t, g).wait_recv()
            row_local(t, g).wait()
            share(t, g).start()

    def to_sibling(t, f):
        return remote(so.at[t, f], rb.at[t, f], sib_s.at[t, f], sib_r.at[t, f], sibling)

    def back_local(t, g):
        return pltpu.make_async_copy(ob.at[t, g, slots(me)], rv.at[t, g, slots(me)], back_l.at[t, g])

    def back_arrived(t, g):
        some = pl.ds(0, ns - SL)
        return remote(ob.at[t, g, some], rv.at[t, g, some], back_s.at[t, g], back_r.at[t, g], sibling)

    def send_back(t, g):
        to_sibling(t, g).wait_recv()
        ob[t, g] = (ob[t, g].astype(F32) + rb[t, g].astype(F32)).astype(BF)

        @pl.loop(1, nq)
        def _(i):
            q = lax.rem(me + i, nq)
            remote(
                ob.at[t, g, slots(q)], rv.at[t, g, slots(me)],
                back_s.at[t, g], back_r.at[t, g], device(nx, q, z, c),
            ).start()

        back_local(t, g).start()

    def lanes(f):
        return slice(f * pair, (f + 1) * pair)

    take_in(0)
    weights[0].wait()
    weights[1].wait()
    gacc[...] = jnp.zeros_like(gacc)
    uacc[...] = jnp.zeros_like(uacc)

    @pl.loop(0, 4)
    def _(f):
        share(0, f).wait_recv()
        gacc[...] += jnp.dot(xdy[0, f], wg[f], preferred_element_type=F32)
        uacc[...] += jnp.dot(xdy[0, f], wu[f], preferred_element_type=F32)

    g = gacc[...]
    hb[...] = (g * jax.nn.sigmoid(g) * uacc[...]).astype(BF)
    weights[2].wait()
    for f in range(4):
        so[0, f] = jnp.dot(hb[theirs, :], wd[:, lanes(f)], preferred_element_type=F32).astype(BF)
        to_sibling(0, f).start()
        ob[0, f] = jnp.dot(hb[mine, :], wd[:, lanes(f)], preferred_element_type=F32).astype(BF)

    @pl.loop(0, 4)
    def _(f):
        send_back(0, f)

    def rows_of(n):
        return pl.ds(pl.multiple_of(n * part, SL), part)

    def send_down(t, j, n):
        return remote(
            tp.at[t, j, rows_of(n)], rsd.at[t, j, rows_of(n)], ring_s.at[t, j, n], down_r.at[t, j, n], down
        )

    def send_up(t, j, n):
        return remote(
            tp.at[t, j, rows_of(n)], rsu.at[t, j, rows_of(n)], ring_s.at[t, j, n], up_r.at[t, j, n], up
        )

    def add_in(t, j, n, a):
        tp[t, j, rows_of(n)] = (
            tp[t, j, rows_of(n)].astype(F32) + a[t, j, rows_of(n)].astype(F32)
        ).astype(BF)

    def pass_on(t, g, m):
        above = lax.rem(r - g + 8, 8)
        below = lax.rem(g - r + 8, 8)

        @pl.when(above == 4 - m)
        def _():
            @pl.loop(0, PARTS)
            def _(n):
                if m > 0:
                    send_down(t, g, n).wait_recv()
                    add_in(t, g, n, rsd)
                send_down(t, g, n).start()

        if m < 3:

            @pl.when(below == 3 - m)
            def _():
                @pl.loop(0, PARTS)
                def _(n):
                    if m > 0:
                        send_up(t, g, n).wait_recv()
                        add_in(t, g, n, rsu)
                    send_up(t, g, n).start()

    def return_step(n):
        for m in (3, 2, 1):
            at = n - m

            @pl.when(jnp.logical_and(at >= 0, at < 8))
            def _():
                pass_on(lax.div(at, 4), lax.rem(at, 4), m)

        @pl.when(n < 8)
        def _():
            t = lax.div(n, 4)
            g = lax.rem(n, 4)
            back_arrived(t, g).wait_recv()
            back_local(t, g).wait()

            @pl.when(t == 0)
            def _():
                tp[0, g] = (tdot(rv[0, g], wt[0]) + tdot(rv[0, g], wt[1])).astype(BF)

            @pl.when(t == 1)
            def _():
                tp[1, g] = tdot(rv[1, g], pick[...]).astype(BF)

            pass_on(t, g, 0)

    take_in(1)
    dacc[...] = jnp.zeros_like(dacc)
    for f in range(4):
        share(1, f).wait_recv()
        dacc[...] += dot_t(xdy[1, f], wd[:, lanes(f)])

    g = gacc[...]
    u = uacc[...]
    dh = dacc[...]
    sig = jax.nn.sigmoid(g)
    dgb[...] = (dh * u * sig * (1.0 + g * (1.0 - sig))).astype(BF)
    dub[...] = (dh * g * sig).astype(BF)
    prod = hb[...].astype(F32) * dh
    hi = prod.astype(BF)
    lo = (prod - hi.astype(F32)).astype(BF)
    ones = jnp.ones((8, prod.shape[1]), BF)
    scb[...] = (dot_t(ones, hi) + dot_t(ones, lo))[0:1, :]
    scr[pl.ds(d, 1)] = scb[...][None]

    @pl.loop(1, 8)
    def _(i):
        remote(scb, scr.at[d], dp_s, dp_r, {"expert": e, "dp": lax.rem(d + i, 8)}).start()

    @pl.loop(0, 4)
    def _(f):
        so[1, f] = (dot_t(dgb[theirs, :], wg[f]) + dot_t(dub[theirs, :], wu[f])).astype(BF)
        to_sibling(1, f).start()
        ob[1, f] = (dot_t(dgb[mine, :], wg[f]) + dot_t(dub[mine, :], wu[f])).astype(BF)

        @pl.when(f > 0)
        def _():
            send_back(1, f - 1)

        return_step(f)

    send_back(1, 3)

    seven = scr.at[pl.ds(0, 7)]
    dp_all = remote(seven, seven, dp_s, dp_r, sibling)
    dp_all.wait_recv()
    st[...] = jnp.sum(scr[...], axis=0)
    rsc[pl.ds(e, 1)] = st[...][None]

    @pl.loop(1, ne)
    def _(i):
        remote(st, rsc.at[e], ex_s, ex_r, {"expert": lax.rem(e + i, ne), "dp": d}).start()

    def final(t):
        return remote(fin.at[t], fo.at[t], fin_s.at[t], fin_r.at[t], sibling)

    def finish_own(t):
        @pl.loop(0, PARTS)
        def _(n):
            send_down(t, zl, n).wait_recv()
            send_up(t, zl, n).wait_recv()

        def summed(core):
            some = pl.ds(pl.multiple_of(core * ch, SL), ch)
            total = tp[t, zl, some].astype(F32) + rsd[t, zl, some].astype(F32)
            return (total + rsu[t, zl, some].astype(F32)).astype(BF)

        fin[t] = summed(1 - c)
        final(t).start()
        outs[t][...] = summed(c)

    results = [
        pltpu.make_async_copy(a, b, out_l.at[i])
        for i, (a, b) in enumerate(((wg, gwg_ref), (wu, gwu_ref), (wd, gwd_ref)))
    ]

    @pl.loop(4, 11)
    def _(n):
        return_step(n)

        @pl.when(n < 8)
        def _():
            f = n - 4
            some = pl.ds(pl.multiple_of(f * pair, 128), pair)
            wg[f] = tdot(xdy[0, f], dgb[...]).astype(BF)
            wu[f] = tdot(xdy[0, f], dub[...]).astype(BF)
            wd[:, some] = tdot(hb[...], xdy[1, f]).astype(BF)

        @pl.when(n == 8)
        def _():
            for o in results:
                o.start()

            @pl.when(own)
            def _():
                finish_own(0)

    @pl.when(own)
    def _():
        finish_own(1)
        for t in range(2):
            final(t).wait_send()

        tab_out.wait_send()

    @pl.when(other)
    def _():
        for t in range(2):
            final(t).wait_recv()
            outs[t][...] = fo[t]

        gout_out.wait_send()

    some = pl.ds(0, ne - 1)
    ex_all = remote(rsc.at[some], rsc.at[some], ex_s, ex_r, sibling)
    ex_all.wait_recv()
    rsc_ref[...] = rsc[...].reshape(ne, 2 * ns)
    ex_all.wait_send()
    dp_all.wait_send()
    for o in results:
        o.wait()

    @pl.loop(0, pieces)
    def _(i):
        @pl.when(jnp.logical_and(r >= 3, r < 7))
        def _():
            piece(0, i, up).wait_send()

        @pl.when(jnp.logical_or(r == 0, r > 4))
        def _():
            piece(1, i, down).wait_send()

    for t in range(2):

        @pl.loop(0, 4)
        def _(g):
            arrived(t, g).wait_send()
            share(t, g).wait_send()
            to_sibling(t, g).wait_send()
            back_arrived(t, g).wait_send()

            @pl.when(g != r)
            def _():
                @pl.loop(0, PARTS)
                def _(n):
                    send_down(t, g, n).wait_send()

    @pl.loop(0, 4)
    def _(j):
        @pl.when(lax.rem(r - j + 8, 8) < 4)
        def _():
            for n in range(2):
                ring(j, n, up, up_s).wait_send()

        @pl.when(lax.rem(j - r + 8, 8) < 3)
        def _():
            for n in range(2):
                ring(j, n, down, down_s).wait_send()


def moe(nx, nq, tokens, gout, ids, gates, tiles, wg, wu, wd):
    ntok = tokens.shape[0]
    ch = gout.shape[0]
    pair = 2 * ch
    ns = nq * SL
    fh = wg.shape[2]
    hbm = pl.BlockSpec(memory_space=pl.ANY)
    vm = pl.BlockSpec(memory_space=pltpu.VMEM)
    dma = pltpu.SemaphoreType.DMA
    s = jax.ShapeDtypeStruct
    v = pltpu.VMEM
    wide = v((2, 4, ns, pair), BF)
    tall = v((2, 4, pair, ntok), BF)
    each = dma((2, 4))
    parts = dma((2, 4, PARTS))
    return pl.pallas_call(
        functools.partial(moe_kernel, nx, nq),
        out_shape=(
            s((ch, ntok), BF), s((ch, ntok), BF), s((2 * nq, 2 * ns), F32),
            s(wg.shape, BF), s(wu.shape, BF), s(wd.shape, BF),
        ),
        in_specs=[hbm, hbm, vm, vm, vm, hbm, hbm, hbm],
        out_specs=(vm, vm, vm, hbm, hbm, hbm),
        scratch_shapes=[
            v((4, ntok, pair), BF), v((2, 2 * nq, ntok), F32), v((2 * nq, ntok), F32), v((4, pair, ntok), BF), wide,
            v((2, 4, 2 * ns, pair), BF), v((ns, ntok), BF), v((ns, 128), F32), v((2, ns, ntok), BF),
            v(wg.shape, BF), v(wu.shape, BF), v(wd.shape, BF),
            v((2 * ns, fh), F32), v((2 * ns, fh), F32), v((2 * ns, fh), F32),
            v((2 * ns, fh), BF), v((2 * ns, fh), BF), v((2 * ns, fh), BF), v((1, 2 * ns), F32),
            wide, wide, wide, wide, tall, tall, tall, v((2, ch, ntok), BF), v((2, ch, ntok), BF),
            v((8, 1, 2 * ns), F32), v((1, 2 * ns), F32), v((2 * nq, 1, 2 * ns), F32),
            dma((4,)), dma, dma((3,)), each, each, dma((3,)),
            dma, dma, dma, dma, dma((2, 2 * ROWBLOCKS)), dma((2, 2 * ROWBLOCKS)), dma((4, 2)), dma((4, 2)), dma((4, 2)),
            each, each, each, each, each, each, each, each,
            parts, parts, parts, dma((2,)), dma((2,)), dma, dma, dma, dma,
        ],
        compiler_params=pltpu.CompilerParams(
            collective_id=1, has_side_effects=True, vmem_limit_bytes=VMEM_LIMIT
        ),
        name="moe",
    )(tokens, gout, ids, gates, tiles, wg, wu, wd)


def finish_kernel(nx, nq, rsc_ref, ids_ref, gates_ref, tiles_ref, *refs):
    count = (len(refs) - 3) // 3
    given, gg_ref, made = refs[:count], refs[count], refs[count + 1 : 2 * count + 1]
    held, got, put = refs[2 * count + 1 : -2], refs[-2], refs[-1]
    loads, stores = [], []
    for i in range(count):
        step = given[i].shape[0] // 4
        for n in range(4):
            some = pl.ds(n * step, step)
            loads.append(pltpu.make_async_copy(given[i].at[some], held[i].at[some], got.at[i, n]))
            stores.append(pltpu.make_async_copy(held[i].at[some], made[i].at[some], put.at[i, n]))
    for copy in loads:
        copy.start()
    for load, store in zip(loads, stores):
        load.wait()
        store.start()
    me, zh, _, _ = place(nx)
    ne = 2 * nq
    ids = ids_ref[...]
    names = lax.broadcasted_iota(jnp.int32, (ne, 1), 0)
    rank, gate = routing(ids, gates_ref[...], tiles_ref[0:1, 0:1], names)
    lane = lax.broadcasted_iota(jnp.int32, rsc_ref.shape, 1) - (zh * nq + me) * SL
    at = jnp.zeros(rank.shape, F32)
    for n in range(SL):
        score = jnp.sum(jnp.where(lane == n, rsc_ref[...], 0.0), axis=1, keepdims=True)
        at = at + jnp.where(rank == float(n), score, 0.0)
    named = rank >= 0.0
    at = jnp.where(named, at / jnp.where(named, gate, 1.0), 0.0)
    for k in range(ids.shape[0]):
        gg_ref[k : k + 1, :] = jnp.sum(jnp.where(ids[k : k + 1, :] == names, at, 0.0), axis=0, keepdims=True)
    for store in stores:
        store.wait()


def finish(nx, nq, rsc, ids, gates, tiles, arrays):
    hbm = pl.BlockSpec(memory_space=pl.ANY)
    vm = pl.BlockSpec(memory_space=pltpu.VMEM)
    s = jax.ShapeDtypeStruct
    return pl.pallas_call(
        functools.partial(finish_kernel, nx, nq),
        out_shape=(s(ids.shape, F32), *(s(a.shape, a.dtype) for a in arrays)),
        in_specs=[vm] * 4 + [hbm] * len(arrays),
        out_specs=(vm, *([hbm] * len(arrays))),
        scratch_shapes=[
            *(pltpu.VMEM(a.shape, a.dtype) for a in arrays),
            pltpu.SemaphoreType.DMA((len(arrays), 4)), pltpu.SemaphoreType.DMA((len(arrays), 4)),
        ],
        compiler_params=pltpu.CompilerParams(vmem_limit_bytes=VMEM_LIMIT),
        name="finish",
    )(rsc, ids, gates, tiles, *arrays)


def on_device(nx, tokens, expert_ids, gate_values, tiles, w_gate, w_up, w_down, grad_out):
    nq = lax.axis_size("expert") // 2
    width = tokens.shape[1]
    pair = 2 * grad_out.shape[1]
    fh = w_gate.shape[2]
    ids = expert_ids.T
    gates = gate_values.T
    tiles = tiles.reshape(1, 1)
    wg = w_gate.reshape(4, pair, fh)
    wu = w_up.reshape(4, pair, fh)
    mixed, gtok, rsc, *grads = moe(nx, nq, tokens, grad_out.T, ids, gates, tiles, wg, wu, w_down[0])
    gg, mixed, gtok, gwg, gwu, gwd = finish(nx, nq, rsc, ids, gates, tiles, (mixed, gtok, *grads))
    return (
        mixed.T, gtok.T, gg.T,
        gwg.reshape(1, width, fh), gwu.reshape(1, width, fh), gwd[None],
    )


def build(mesh, nx):
    placed = (
        P("expert", None),
        P("expert", None),
        P("expert", None),
        P("expert"),
        P("expert", None, "dp"),
        P("expert", None, "dp"),
        P("expert", "dp", None),
        P("expert", "dp"),
    )
    return jax.shard_map(
        functools.partial(on_device, nx),
        mesh=mesh,
        in_specs=placed,
        out_specs=(
            P("expert", "dp"),
            P("expert", "dp"),
            P("expert", None),
            P("expert", None, "dp"),
            P("expert", None, "dp"),
            P("expert", "dp", None),
        ),
        check_vma=False,
    )


def solution(mesh):
    return build(mesh, 4)
```

```python
import functools

import jax
import jax.numpy as jnp
from jax import lax
from jax.experimental import pallas as pl
from jax.experimental.pallas import tpu as pltpu
from jax.sharding import PartitionSpec as P

TILE = 128
SL = 16
MESH = pl.DeviceIdType.MESH
VMEM_LIMIT = 60 * 1024 * 1024
BF = jnp.bfloat16
F32 = jnp.float32
ROWBLOCKS = 4
PARTS = 4
SKEW = 3
RING_FIRST = 9
RING_GAP = 2


def place(nx):
    e = lax.axis_index("expert")
    d = lax.axis_index("dp")
    x = lax.rem(e, nx)
    zh = lax.rem(lax.div(e, nx), 2)
    y = lax.div(e, 2 * nx)
    return y * nx + x, zh, lax.div(d, 2), lax.rem(d, 2)


def device(nx, q, z, core):
    e = (lax.div(q, nx) * 2 + lax.div(z, 4)) * nx + lax.rem(q, nx)
    return {"expert": e, "dp": lax.rem(z, 4) * 2 + core}


def signal(sem, who):
    pl.semaphore_signal(sem, inc=1, device_id=who, device_id_type=MESH)


def remote(src, dst, send, recv, who):
    return pltpu.make_async_remote_copy(
        src_ref=src, dst_ref=dst, send_sem=send, recv_sem=recv, device_id=who, device_id_type=MESH
    )


def tdot(a, b):
    return lax.dot_general(a, b, (((0,), (0,)), ((), ())), preferred_element_type=F32)


def dot_t(a, b):
    return lax.dot_general(a, b, (((1,), (1,)), ((), ())), preferred_element_type=F32)


def routing(ids, gates, tiles, names):
    top, ntok = ids.shape
    named = names < 0
    gate = jnp.zeros((names.shape[0], ntok), F32)
    named = jnp.broadcast_to(named, gate.shape)
    for k in range(top):
        chosen = ids[k : k + 1, :] == names
        named = jnp.logical_or(named, chosen)
        gate = gate + jnp.where(chosen, gates[k : k + 1, :], 0.0)
    live = lax.broadcasted_iota(jnp.int32, gate.shape, 1) < tiles * TILE
    named = jnp.logical_and(named, live)
    square = (ntok, ntok)
    earlier = lax.broadcasted_iota(jnp.int32, square, 0) < lax.broadcasted_iota(jnp.int32, square, 1)
    ones = jnp.where(named, 1.0, 0.0).astype(BF)
    before = jnp.dot(ones, jnp.where(earlier, 1.0, 0.0).astype(BF), preferred_element_type=F32)
    return jnp.where(named, before, -1.0), gate


def moe_kernel(
    nx, nq, tok_ref, gout_ref, ids_ref, gates_ref, tiles_ref, wg_ref, wu_ref, wd_ref,
    mixed_ref, gtok_ref, rsc_ref, gwg_ref, gwu_ref, gwd_ref,
    tok, tabs, tabr, dyt, rows, xdy, pick, sg, wt, wg, wu, wd,
    gacc, uacc, dacc, hb, dgb, dub, scb,
    so, ob, rb, rv, tp, rsd, rsu, fin, fo, scr, st, rsc,
    tok_l, gout_l, w_l, row_l, back_l, out_l,
    tab_s, tab_r, gout_s, gout_r, x_s, x_r, up_s, down_s, ring_r,
    plane_s, plane_r, share_s, share_r, sib_s, sib_r, back_s, back_r,
    ring_s, down_r, up_r, fin_s, fin_r, dp_s, dp_r, ex_s, ex_r,
):
    me, zh, zl, c = place(nx)
    z = zh * 4 + zl
    e = lax.axis_index("expert")
    d = 2 * zl + c
    own = zh == c
    other = jnp.logical_not(own)
    r = lax.rem(z - 4 * c + 8, 8)
    ntok = tok_ref.shape[0]
    ch = gout_ref.shape[0]
    pair = 2 * ch
    ns = nq * SL
    ne = 2 * nq
    part = pair // PARTS
    up = device(nx, me, lax.rem(z + 1, 8), c)
    down = device(nx, me, lax.rem(z + 7, 8), c)
    across = device(nx, me, lax.rem(z + 4, 8), c)
    sibling = device(nx, me, z, 1 - c)
    outs = (mixed_ref, gtok_ref)
    mine = pl.ds(pl.multiple_of(c * ns, SL), ns)
    theirs = pl.ds(pl.multiple_of((1 - c) * ns, SL), ns)

    def slots(q):
        return pl.ds(pl.multiple_of(q * SL, SL), SL)

    weights = [
        pltpu.make_async_copy(a, b, w_l.at[i])
        for i, (a, b) in enumerate(((wg_ref, wg), (wu_ref, wu), (wd_ref, wd)))
    ]

    def tok_in(g):
        return pltpu.make_async_copy(tok_ref.at[:, pl.ds(g * pair, pair)], tok.at[g], tok_l.at[g])

    tab_out = remote(tabs.at[1 - zh], tabr, tab_s, tab_r, across)
    chunk = dyt.at[zl, pl.ds(pl.multiple_of(c * ch, SL), ch)]
    gout_in = pltpu.make_async_copy(gout_ref, chunk, gout_l)
    gout_out = remote(gout_ref, chunk, gout_s, gout_r, sibling)

    @pl.when(own)
    def _():
        for g in (0, 2, 1, 3):
            tok_in(g).start()
        gout_in.start()

    for w in weights:
        w.start()

    barrier = pltpu.get_barrier_semaphore()
    signal(barrier, up)
    signal(barrier, down)

    @pl.loop(1, 8)
    def _(i):
        signal(barrier, {"expert": e, "dp": lax.rem(d + i, 8)})

    @pl.loop(1, ne)
    def _(i):
        signal(barrier, {"expert": lax.rem(e + i, ne), "dp": d})

    row = lax.broadcasted_iota(jnp.int32, (nq, 1), 0)
    shift = nx.bit_length() - 1
    for h in range(2):
        names = lax.shift_right_logical(row, shift) * (2 * nx) + h * nx + jnp.bitwise_and(row, nx - 1)
        rank, gate = routing(ids_ref[...], gates_ref[...], tiles_ref[0:1, 0:1], names)
        tabs[h, 0:nq] = rank
        tabs[h, nq : 2 * nq] = gate

    @pl.when(own)
    def _():
        tabr[...] = tabs[zh]

    pl.semaphore_wait(barrier, 2 + 7 + ne - 1)

    def piece(h, i, who):
        step = ntok // ROWBLOCKS
        first = pl.multiple_of(lax.rem(i, ROWBLOCKS) * step, step)
        some = tok.at[2 * h + lax.div(i, ROWBLOCKS), pl.ds(first, step)]
        return remote(some, some, x_s.at[h, i], x_r.at[h, i], who)

    def ring(j, n, who, sems):
        some = dyt.at[j, pl.ds(pl.multiple_of(n * ch, SL), ch)]
        return remote(some, some, sems.at[j, n], ring_r.at[j, n], who)

    pieces = 2 * ROWBLOCKS

    @pl.when(own)
    def _():
        tab_out.start()
        for g in (0, 2, 1, 3):
            tok_in(g).wait()
            for i in range(ROWBLOCKS):
                n = (g % 2) * ROWBLOCKS + i
                if g < 2:

                    @pl.when(r == 3)
                    def _():
                        piece(0, n, up).start()
                else:

                    @pl.when(r == 0)
                    def _():
                        piece(1, n, down).start()

        gout_in.wait()
        ring(zl, c, up, up_s).start()
        ring(zl, c, down, down_s).start()
        gout_out.wait_recv()
        ring(zl, 1 - c, up, up_s).start()
        ring(zl, 1 - c, down, down_s).start()

    @pl.when(other)
    def _():
        gout_out.start()
        tab_out.wait_recv()

    rt = tabr[0:nq, :]
    gt = tabr[nq : 2 * nq, :]
    slot = lax.broadcasted_iota(jnp.int32, (nq, SL, ntok), 1).astype(F32)
    hit = jnp.where(jnp.broadcast_to(rt[:, None, :], (nq, SL, ntok)) == slot, 1.0, 0.0)
    heavy = (hit * jnp.broadcast_to(gt[:, None, :], (nq, SL, ntok))).reshape(ns, ntok)
    top = heavy.astype(BF)
    pick[...] = hit.reshape(ns, ntok).astype(BF)
    wt[0] = top
    wt[1] = (heavy - top.astype(F32)).astype(BF)
    sg[...] = jnp.broadcast_to(jnp.sum(heavy, axis=1, keepdims=True), sg.shape)

    def row_local(t, g):
        return pltpu.make_async_copy(
            rows.at[t, g, slots(me)], xdy.at[t, g, slots(c * nq + me)], row_l.at[t, g]
        )

    def send_rows(t, g):
        @pl.loop(1, nq)
        def _(i):
            q = lax.rem(me + i, nq)
            remote(
                rows.at[t, g, slots(q)], xdy.at[t, g, slots(c * nq + me)],
                plane_s.at[t, g], plane_r.at[t, g], device(nx, q, z, c),
            ).start()

        row_local(t, g).start()

    def x_group(g):
        rows[0, g] = jnp.dot(pick[...], tok[g], preferred_element_type=F32).astype(BF)
        send_rows(0, g)

    def dy_group(g):
        rows[1, g] = (dot_t(pick[...], dyt[g]) * sg[:, 0:1]).astype(BF)
        send_rows(1, g)

    def ring_step(k, m):
        n = lax.rem(c + m, 2)
        ju = lax.rem(r - k + 8, 8)
        jd = lax.rem(r + k, 8)
        from_below = ju < 4
        from_above = jnp.logical_and(jd < 4, k < 4)

        @pl.when(from_below)
        def _():
            ring(ju, n, up, up_s).wait_recv()

            @pl.when(k < 4)
            def _():
                ring(ju, n, up, up_s).start()

        @pl.when(from_above)
        def _():
            ring(jd, n, down, down_s).wait_recv()

            @pl.when(k < 3)
            def _():
                ring(jd, n, down, down_s).start()

        @pl.when(jnp.logical_and(from_below, m == 1))
        def _():
            dy_group(ju)

        @pl.when(jnp.logical_and(from_above, m == 1))
        def _():
            dy_group(jd)

    @pl.when(own)
    def _():
        @pl.loop(0, 11)
        def _(n):
            @pl.when(n < 2)
            def _():
                x_group(n)

            @pl.when(jnp.logical_and(n > 3, n < 6))
            def _():
                x_group(n - 2)

            @pl.when(n == 6)
            def _():
                dy_group(zl)

            @pl.when(jnp.logical_and(n > 1, n < 4))
            def _():
                ring_step(1, n - 2)

            @pl.when(n > 6)
            def _():
                ring_step(2 + lax.div(n - 7, 2), lax.rem(n - 7, 2))

    @pl.when(other)
    def _():
        inside = min(7, -(-(pieces + 4 * SKEW - RING_FIRST) // RING_GAP))

        @pl.loop(SKEW, pieces + 4 * SKEW)
        def _(n):
            for h, far, who in ((0, r - 3, up), (1, 8 - r, down)):
                i = n - far * SKEW

                @pl.when(jnp.logical_and(i >= 0, i < pieces))
                def _():
                    piece(h, i, who).wait_recv()

                    @pl.when(far < 4)
                    def _():
                        piece(h, i, who).start()

            for h, far in ((0, r - 3), (1, 8 - r)):
                i = n - far * SKEW
                whole = lax.rem(i + 4 * ROWBLOCKS, ROWBLOCKS) == ROWBLOCKS - 1

                @pl.when(jnp.logical_and(jnp.logical_and(i >= 0, i < pieces), whole))
                def _():
                    x_group(2 * h + lax.div(i, ROWBLOCKS))

            at = n - RING_FIRST
            turn = lax.div(at, RING_GAP)

            @pl.when(jnp.logical_and(at >= 0, jnp.logical_and(turn < inside, lax.rem(at + 8 * RING_GAP, RING_GAP) == 0)))
            def _():
                ring_step(lax.div(turn, 2) + 1, lax.rem(turn, 2))

        @pl.loop(inside, 8)
        def _(turn):
            ring_step(lax.div(turn, 2) + 1, lax.rem(turn, 2))

    def share(t, g):
        return remote(xdy.at[t, g, mine], xdy.at[t, g, mine], share_s.at[t, g], share_r.at[t, g], sibling)

    def arrived(t, g):
        some = pl.ds(0, ns - SL)
        return remote(rows.at[t, g, some], xdy.at[t, g, some], plane_s.at[t, g], plane_r.at[t, g], sibling)

    def take_in(t):
        @pl.loop(0, 4)
        def _(g):
            arrived(t, g).wait_recv()
            row_local(t, g).wait()
            share(t, g).start()

    def to_sibling(t, f):
        return remote(so.at[t, f], rb.at[t, f], sib_s.at[t, f], sib_r.at[t, f], sibling)

    def back_local(t, g):
        return pltpu.make_async_copy(ob.at[t, g, slots(me)], rv.at[t, g, slots(me)], back_l.at[t, g])

    def back_arrived(t, g):
        some = pl.ds(0, ns - SL)
        return remote(ob.at[t, g, some], rv.at[t, g, some], back_s.at[t, g], back_r.at[t, g], sibling)

    def send_back(t, g):
        to_sibling(t, g).wait_recv()
        ob[t, g] = (ob[t, g].astype(F32) + rb[t, g].astype(F32)).astype(BF)

        @pl.loop(1, nq)
        def _(i):
            q = lax.rem(me + i, nq)
            remote(
                ob.at[t, g, slots(q)], rv.at[t, g, slots(me)],
                back_s.at[t, g], back_r.at[t, g], device(nx, q, z, c),
            ).start()

        back_local(t, g).start()

    def lanes(f):
        return slice(f * pair, (f + 1) * pair)

    take_in(0)
    weights[0].wait()
    weights[1].wait()
    gacc[...] = jnp.zeros_like(gacc)
    uacc[...] = jnp.zeros_like(uacc)

    @pl.loop(0, 4)
    def _(f):
        share(0, f).wait_recv()
        gacc[...] += jnp.dot(xdy[0, f], wg[f], preferred_element_type=F32)
        uacc[...] += jnp.dot(xdy[0, f], wu[f], preferred_element_type=F32)

    g = gacc[...]
    hb[...] = (g * jax.nn.sigmoid(g) * uacc[...]).astype(BF)
    weights[2].wait()
    for f in range(4):
        so[0, f] = jnp.dot(hb[theirs, :], wd[:, lanes(f)], preferred_element_type=F32).astype(BF)
        to_sibling(0, f).start()
        ob[0, f] = jnp.dot(hb[mine, :], wd[:, lanes(f)], preferred_element_type=F32).astype(BF)

    @pl.loop(0, 4)
    def _(f):
        send_back(0, f)

    def rows_of(n):
        return pl.ds(pl.multiple_of(n * part, SL), part)

    def send_down(t, j, n):
        return remote(
            tp.at[t, j, rows_of(n)], rsd.at[t, j, rows_of(n)], ring_s.at[t, j, n], down_r.at[t, j, n], down
        )

    def send_up(t, j, n):
        return remote(
            tp.at[t, j, rows_of(n)], rsu.at[t, j, rows_of(n)], ring_s.at[t, j, n], up_r.at[t, j, n], up
        )

    def add_in(t, j, n, a):
        tp[t, j, rows_of(n)] = (
            tp[t, j, rows_of(n)].astype(F32) + a[t, j, rows_of(n)].astype(F32)
        ).astype(BF)

    def pass_on(t, g, m):
        above = lax.rem(r - g + 8, 8)
        below = lax.rem(g - r + 8, 8)

        @pl.when(above == 4 - m)
        def _():
            @pl.loop(0, PARTS)
            def _(n):
                if m > 0:
                    send_down(t, g, n).wait_recv()
                    add_in(t, g, n, rsd)
                send_down(t, g, n).start()

        if m < 3:

            @pl.when(below == 3 - m)
            def _():
                @pl.loop(0, PARTS)
                def _(n):
                    if m > 0:
                        send_up(t, g, n).wait_recv()
                        add_in(t, g, n, rsu)
                    send_up(t, g, n).start()

    def return_step(n):
        for m in (3, 2, 1):
            at = n - m

            @pl.when(jnp.logical_and(at >= 0, at < 8))
            def _():
                pass_on(lax.div(at, 4), lax.rem(at, 4), m)

        @pl.when(n < 8)
        def _():
            t = lax.div(n, 4)
            g = lax.rem(n, 4)
            back_arrived(t, g).wait_recv()
            back_local(t, g).wait()

            @pl.when(t == 0)
            def _():
                tp[0, g] = (tdot(rv[0, g], wt[0]) + tdot(rv[0, g], wt[1])).astype(BF)

            @pl.when(t == 1)
            def _():
                tp[1, g] = tdot(rv[1, g], pick[...]).astype(BF)

            pass_on(t, g, 0)

    take_in(1)
    dacc[...] = jnp.zeros_like(dacc)
    for f in range(4):
        share(1, f).wait_recv()
        dacc[...] += dot_t(xdy[1, f], wd[:, lanes(f)])

    g = gacc[...]
    u = uacc[...]
    dh = dacc[...]
    sig = jax.nn.sigmoid(g)
    dgb[...] = (dh * u * sig * (1.0 + g * (1.0 - sig))).astype(BF)
    dub[...] = (dh * g * sig).astype(BF)
    prod = hb[...].astype(F32) * dh
    hi = prod.astype(BF)
    lo = (prod - hi.astype(F32)).astype(BF)
    ones = jnp.ones((8, prod.shape[1]), BF)
    scb[...] = (dot_t(ones, hi) + dot_t(ones, lo))[0:1, :]
    scr[pl.ds(d, 1)] = scb[...][None]

    @pl.loop(1, 8)
    def _(i):
        remote(scb, scr.at[d], dp_s, dp_r, {"expert": e, "dp": lax.rem(d + i, 8)}).start()

    @pl.loop(0, 4)
    def _(f):
        so[1, f] = (dot_t(dgb[theirs, :], wg[f]) + dot_t(dub[theirs, :], wu[f])).astype(BF)
        to_sibling(1, f).start()
        ob[1, f] = (dot_t(dgb[mine, :], wg[f]) + dot_t(dub[mine, :], wu[f])).astype(BF)

        @pl.when(f > 0)
        def _():
            send_back(1, f - 1)

        return_step(f)

    send_back(1, 3)

    seven = scr.at[pl.ds(0, 7)]
    dp_all = remote(seven, seven, dp_s, dp_r, sibling)
    dp_all.wait_recv()
    st[...] = jnp.sum(scr[...], axis=0)
    rsc[pl.ds(e, 1)] = st[...][None]

    @pl.loop(1, ne)
    def _(i):
        remote(st, rsc.at[e], ex_s, ex_r, {"expert": lax.rem(e + i, ne), "dp": d}).start()

    def final(t):
        return remote(fin.at[t], fo.at[t], fin_s.at[t], fin_r.at[t], sibling)

    def finish_own(t):
        @pl.loop(0, PARTS)
        def _(n):
            send_down(t, zl, n).wait_recv()
            send_up(t, zl, n).wait_recv()

        def summed(core):
            some = pl.ds(pl.multiple_of(core * ch, SL), ch)
            total = tp[t, zl, some].astype(F32) + rsd[t, zl, some].astype(F32)
            return (total + rsu[t, zl, some].astype(F32)).astype(BF)

        fin[t] = summed(1 - c)
        final(t).start()
        outs[t][...] = summed(c)

    results = [
        pltpu.make_async_copy(a, b, out_l.at[i])
        for i, (a, b) in enumerate(((wg, gwg_ref), (wu, gwu_ref), (wd, gwd_ref)))
    ]

    @pl.loop(4, 11)
    def _(n):
        return_step(n)

        @pl.when(n < 8)
        def _():
            f = n - 4
            some = pl.ds(pl.multiple_of(f * pair, 128), pair)
            wg[f] = tdot(xdy[0, f], dgb[...]).astype(BF)
            wu[f] = tdot(xdy[0, f], dub[...]).astype(BF)
            wd[:, some] = tdot(hb[...], xdy[1, f]).astype(BF)

        @pl.when(n == 8)
        def _():
            for o in results:
                o.start()

            @pl.when(own)
            def _():
                finish_own(0)

    @pl.when(own)
    def _():
        finish_own(1)
        for t in range(2):
            final(t).wait_send()

        tab_out.wait_send()

    @pl.when(other)
    def _():
        for t in range(2):
            final(t).wait_recv()
            outs[t][...] = fo[t]

        gout_out.wait_send()

    some = pl.ds(0, ne - 1)
    ex_all = remote(rsc.at[some], rsc.at[some], ex_s, ex_r, sibling)
    ex_all.wait_recv()
    rsc_ref[...] = rsc[...].reshape(ne, 2 * ns)
    ex_all.wait_send()
    dp_all.wait_send()
    for o in results:
        o.wait()

    @pl.loop(0, pieces)
    def _(i):
        @pl.when(jnp.logical_and(r >= 3, r < 7))
        def _():
            piece(0, i, up).wait_send()

        @pl.when(jnp.logical_or(r == 0, r > 4))
        def _():
            piece(1, i, down).wait_send()

    for t in range(2):

        @pl.loop(0, 4)
        def _(g):
            arrived(t, g).wait_send()
            share(t, g).wait_send()
            to_sibling(t, g).wait_send()
            back_arrived(t, g).wait_send()

            @pl.when(g != r)
            def _():
                @pl.loop(0, PARTS)
                def _(n):
                    send_down(t, g, n).wait_send()

    @pl.loop(0, 4)
    def _(j):
        @pl.when(lax.rem(r - j + 8, 8) < 4)
        def _():
            for n in range(2):
                ring(j, n, up, up_s).wait_send()

        @pl.when(lax.rem(j - r + 8, 8) < 3)
        def _():
            for n in range(2):
                ring(j, n, down, down_s).wait_send()


def moe(nx, nq, tokens, gout, ids, gates, tiles, wg, wu, wd):
    ntok = tokens.shape[0]
    ch = gout.shape[0]
    pair = 2 * ch
    ns = nq * SL
    fh = wg.shape[2]
    hbm = pl.BlockSpec(memory_space=pl.ANY)
    vm = pl.BlockSpec(memory_space=pltpu.VMEM)
    dma = pltpu.SemaphoreType.DMA
    s = jax.ShapeDtypeStruct
    v = pltpu.VMEM
    wide = v((2, 4, ns, pair), BF)
    tall = v((2, 4, pair, ntok), BF)
    each = dma((2, 4))
    parts = dma((2, 4, PARTS))
    return pl.pallas_call(
        functools.partial(moe_kernel, nx, nq),
        out_shape=(
            s((ch, ntok), BF), s((ch, ntok), BF), s((2 * nq, 2 * ns), F32),
            s(wg.shape, BF), s(wu.shape, BF), s(wd.shape, BF),
        ),
        in_specs=[hbm, hbm, vm, vm, vm, hbm, hbm, hbm],
        out_specs=(vm, vm, vm, hbm, hbm, hbm),
        scratch_shapes=[
            v((4, ntok, pair), BF), v((2, 2 * nq, ntok), F32), v((2 * nq, ntok), F32), v((4, pair, ntok), BF), wide,
            v((2, 4, 2 * ns, pair), BF), v((ns, ntok), BF), v((ns, 128), F32), v((2, ns, ntok), BF),
            v(wg.shape, BF), v(wu.shape, BF), v(wd.shape, BF),
            v((2 * ns, fh), F32), v((2 * ns, fh), F32), v((2 * ns, fh), F32),
            v((2 * ns, fh), BF), v((2 * ns, fh), BF), v((2 * ns, fh), BF), v((1, 2 * ns), F32),
            wide, wide, wide, wide, tall, tall, tall, v((2, ch, ntok), BF), v((2, ch, ntok), BF),
            v((8, 1, 2 * ns), F32), v((1, 2 * ns), F32), v((2 * nq, 1, 2 * ns), F32),
            dma((4,)), dma, dma((3,)), each, each, dma((3,)),
            dma, dma, dma, dma, dma((2, 2 * ROWBLOCKS)), dma((2, 2 * ROWBLOCKS)), dma((4, 2)), dma((4, 2)), dma((4, 2)),
            each, each, each, each, each, each, each, each,
            parts, parts, parts, dma((2,)), dma((2,)), dma, dma, dma, dma,
        ],
        compiler_params=pltpu.CompilerParams(
            collective_id=1, has_side_effects=True, vmem_limit_bytes=VMEM_LIMIT
        ),
        name="moe",
    )(tokens, gout, ids, gates, tiles, wg, wu, wd)


def finish_kernel(nx, nq, rsc_ref, ids_ref, gates_ref, tiles_ref, *refs):
    count = (len(refs) - 3) // 3
    given, gg_ref, made = refs[:count], refs[count], refs[count + 1 : 2 * count + 1]
    held, got, put = refs[2 * count + 1 : -2], refs[-2], refs[-1]
    loads, stores = [], []
    for i in range(count):
        step = given[i].shape[0] // 4
        for n in range(4):
            some = pl.ds(n * step, step)
            loads.append(pltpu.make_async_copy(given[i].at[some], held[i].at[some], got.at[i, n]))
            stores.append(pltpu.make_async_copy(held[i].at[some], made[i].at[some], put.at[i, n]))
    for copy in loads:
        copy.start()
    me, zh, _, _ = place(nx)
    ne = 2 * nq
    ids = ids_ref[...]
    names = lax.broadcasted_iota(jnp.int32, (ne, 1), 0)
    rank, gate = routing(ids, gates_ref[...], tiles_ref[0:1, 0:1], names)
    lane = lax.broadcasted_iota(jnp.int32, rsc_ref.shape, 1) - (zh * nq + me) * SL
    at = jnp.zeros(rank.shape, F32)
    for n in range(SL):
        score = jnp.sum(jnp.where(lane == n, rsc_ref[...], 0.0), axis=1, keepdims=True)
        at = at + jnp.where(rank == float(n), score, 0.0)
    named = rank >= 0.0
    at = jnp.where(named, at / jnp.where(named, gate, 1.0), 0.0)
    for k in range(ids.shape[0]):
        gg_ref[k : k + 1, :] = jnp.sum(jnp.where(ids[k : k + 1, :] == names, at, 0.0), axis=0, keepdims=True)
    for load, store in zip(loads, stores):
        load.wait()
        store.start()
    for store in stores:
        store.wait()


def finish(nx, nq, rsc, ids, gates, tiles, arrays):
    hbm = pl.BlockSpec(memory_space=pl.ANY)
    vm = pl.BlockSpec(memory_space=pltpu.VMEM)
    s = jax.ShapeDtypeStruct
    return pl.pallas_call(
        functools.partial(finish_kernel, nx, nq),
        out_shape=(s(ids.shape, F32), *(s(a.shape, a.dtype) for a in arrays)),
        in_specs=[vm] * 4 + [hbm] * len(arrays),
        out_specs=(vm, *([hbm] * len(arrays))),
        scratch_shapes=[
            *(pltpu.VMEM(a.shape, a.dtype) for a in arrays),
            pltpu.SemaphoreType.DMA((len(arrays), 4)), pltpu.SemaphoreType.DMA((len(arrays), 4)),
        ],
        compiler_params=pltpu.CompilerParams(vmem_limit_bytes=VMEM_LIMIT),
        name="finish",
    )(rsc, ids, gates, tiles, *arrays)


def on_device(nx, tokens, expert_ids, gate_values, tiles, w_gate, w_up, w_down, grad_out):
    nq = lax.axis_size("expert") // 2
    width = tokens.shape[1]
    pair = 2 * grad_out.shape[1]
    fh = w_gate.shape[2]
    ids = expert_ids.T
    gates = gate_values.T
    tiles = tiles.reshape(1, 1)
    wg = w_gate.reshape(4, pair, fh)
    wu = w_up.reshape(4, pair, fh)
    mixed, gtok, rsc, *grads = moe(nx, nq, tokens, grad_out.T, ids, gates, tiles, wg, wu, w_down[0])
    gg, mixed, gtok, gwg, gwu, gwd = finish(nx, nq, rsc, ids, gates, tiles, (mixed, gtok, *grads))
    return (
        mixed.T, gtok.T, gg.T,
        gwg.reshape(1, width, fh), gwu.reshape(1, width, fh), gwd[None],
    )


def build(mesh, nx):
    placed = (
        P("expert", None),
        P("expert", None),
        P("expert", None),
        P("expert"),
        P("expert", None, "dp"),
        P("expert", None, "dp"),
        P("expert", "dp", None),
        P("expert", "dp"),
    )
    return jax.shard_map(
        functools.partial(on_device, nx),
        mesh=mesh,
        in_specs=placed,
        out_specs=(
            P("expert", "dp"),
            P("expert", "dp"),
            P("expert", None),
            P("expert", None, "dp"),
            P("expert", None, "dp"),
            P("expert", "dp", None),
        ),
        check_vma=False,
    )


def solution(mesh):
    return build(mesh, 4)
```

```python
import functools

import jax
import jax.numpy as jnp
from jax import lax
from jax.experimental import pallas as pl
from jax.experimental.pallas import tpu as pltpu
from jax.sharding import PartitionSpec as P

TILE = 128
SL = 16
MESH = pl.DeviceIdType.MESH
VMEM_LIMIT = 60 * 1024 * 1024
BF = jnp.bfloat16
F32 = jnp.float32
ROWBLOCKS = 4
PARTS = 8
SKEW = 3
RING_FIRST = 9
RING_GAP = 2


def place(nx):
    e = lax.axis_index("expert")
    d = lax.axis_index("dp")
    x = lax.rem(e, nx)
    zh = lax.rem(lax.div(e, nx), 2)
    y = lax.div(e, 2 * nx)
    return y * nx + x, zh, lax.div(d, 2), lax.rem(d, 2)


def device(nx, q, z, core):
    e = (lax.div(q, nx) * 2 + lax.div(z, 4)) * nx + lax.rem(q, nx)
    return {"expert": e, "dp": lax.rem(z, 4) * 2 + core}


def signal(sem, who):
    pl.semaphore_signal(sem, inc=1, device_id=who, device_id_type=MESH)


def remote(src, dst, send, recv, who):
    return pltpu.make_async_remote_copy(
        src_ref=src, dst_ref=dst, send_sem=send, recv_sem=recv, device_id=who, device_id_type=MESH
    )


def tdot(a, b):
    return lax.dot_general(a, b, (((0,), (0,)), ((), ())), preferred_element_type=F32)


def dot_t(a, b):
    return lax.dot_general(a, b, (((1,), (1,)), ((), ())), preferred_element_type=F32)


def routing(ids, gates, tiles, names):
    top, ntok = ids.shape
    named = names < 0
    gate = jnp.zeros((names.shape[0], ntok), F32)
    named = jnp.broadcast_to(named, gate.shape)
    for k in range(top):
        chosen = ids[k : k + 1, :] == names
        named = jnp.logical_or(named, chosen)
        gate = gate + jnp.where(chosen, gates[k : k + 1, :], 0.0)
    live = lax.broadcasted_iota(jnp.int32, gate.shape, 1) < tiles * TILE
    named = jnp.logical_and(named, live)
    square = (ntok, ntok)
    earlier = lax.broadcasted_iota(jnp.int32, square, 0) < lax.broadcasted_iota(jnp.int32, square, 1)
    ones = jnp.where(named, 1.0, 0.0).astype(BF)
    before = jnp.dot(ones, jnp.where(earlier, 1.0, 0.0).astype(BF), preferred_element_type=F32)
    return jnp.where(named, before, -1.0), gate


def moe_kernel(
    nx, nq, tok_ref, gout_ref, ids_ref, gates_ref, tiles_ref, wg_ref, wu_ref, wd_ref,
    mixed_ref, gtok_ref, rsc_ref, gwg_ref, gwu_ref, gwd_ref,
    tok, tabs, tabr, dyt, rows, xdy, pick, sg, wt, wg, wu, wd,
    gacc, uacc, dacc, hb, dgb, dub, scb,
    so, ob, rb, rv, tp, rsd, rsu, fin, fo, scr, st, rsc,
    tok_l, gout_l, w_l, row_l, back_l, out_l,
    tab_s, tab_r, gout_s, gout_r, x_s, x_r, up_s, down_s, ring_r,
    plane_s, plane_r, share_s, share_r, sib_s, sib_r, back_s, back_r,
    ring_s, down_r, up_r, fin_s, fin_r, dp_s, dp_r, ex_s, ex_r,
):
    me, zh, zl, c = place(nx)
    z = zh * 4 + zl
    e = lax.axis_index("expert")
    d = 2 * zl + c
    own = zh == c
    other = jnp.logical_not(own)
    r = lax.rem(z - 4 * c + 8, 8)
    ntok = tok_ref.shape[0]
    ch = gout_ref.shape[0]
    pair = 2 * ch
    ns = nq * SL
    ne = 2 * nq
    part = pair // PARTS
    up = device(nx, me, lax.rem(z + 1, 8), c)
    down = device(nx, me, lax.rem(z + 7, 8), c)
    across = device(nx, me, lax.rem(z + 4, 8), c)
    sibling = device(nx, me, z, 1 - c)
    outs = (mixed_ref, gtok_ref)
    mine = pl.ds(pl.multiple_of(c * ns, SL), ns)
    theirs = pl.ds(pl.multiple_of((1 - c) * ns, SL), ns)

    def slots(q):
        return pl.ds(pl.multiple_of(q * SL, SL), SL)

    weights = [
        pltpu.make_async_copy(a, b, w_l.at[i])
        for i, (a, b) in enumerate(((wg_ref, wg), (wu_ref, wu), (wd_ref, wd)))
    ]

    def tok_in(g):
        return pltpu.make_async_copy(tok_ref.at[:, pl.ds(g * pair, pair)], tok.at[g], tok_l.at[g])

    tab_out = remote(tabs.at[1 - zh], tabr, tab_s, tab_r, across)
    chunk = dyt.at[zl, pl.ds(pl.multiple_of(c * ch, SL), ch)]
    gout_in = pltpu.make_async_copy(gout_ref, chunk, gout_l)
    gout_out = remote(gout_ref, chunk, gout_s, gout_r, sibling)

    @pl.when(own)
    def _():
        for g in (0, 2, 1, 3):
            tok_in(g).start()
        gout_in.start()

    for w in weights:
        w.start()

    barrier = pltpu.get_barrier_semaphore()
    signal(barrier, up)
    signal(barrier, down)

    @pl.loop(1, 8)
    def _(i):
        signal(barrier, {"expert": e, "dp": lax.rem(d + i, 8)})

    @pl.loop(1, ne)
    def _(i):
        signal(barrier, {"expert": lax.rem(e + i, ne), "dp": d})

    row = lax.broadcasted_iota(jnp.int32, (nq, 1), 0)
    shift = nx.bit_length() - 1
    for h in range(2):
        names = lax.shift_right_logical(row, shift) * (2 * nx) + h * nx + jnp.bitwise_and(row, nx - 1)
        rank, gate = routing(ids_ref[...], gates_ref[...], tiles_ref[0:1, 0:1], names)
        tabs[h, 0:nq] = rank
        tabs[h, nq : 2 * nq] = gate

    @pl.when(own)
    def _():
        tabr[...] = tabs[zh]

    pl.semaphore_wait(barrier, 2 + 7 + ne - 1)

    def piece(h, i, who):
        step = ntok // ROWBLOCKS
        first = pl.multiple_of(lax.rem(i, ROWBLOCKS) * step, step)
        some = tok.at[2 * h + lax.div(i, ROWBLOCKS), pl.ds(first, step)]
        return remote(some, some, x_s.at[h, i], x_r.at[h, i], who)

    def ring(j, n, who, sems):
        some = dyt.at[j, pl.ds(pl.multiple_of(n * ch, SL), ch)]
        return remote(some, some, sems.at[j, n], ring_r.at[j, n], who)

    pieces = 2 * ROWBLOCKS

    @pl.when(own)
    def _():
        tab_out.start()
        for g in (0, 2, 1, 3):
            tok_in(g).wait()
            for i in range(ROWBLOCKS):
                n = (g % 2) * ROWBLOCKS + i
                if g < 2:

                    @pl.when(r == 3)
                    def _():
                        piece(0, n, up).start()
                else:

                    @pl.when(r == 0)
                    def _():
                        piece(1, n, down).start()

        gout_in.wait()
        ring(zl, c, up, up_s).start()
        ring(zl, c, down, down_s).start()
        gout_out.wait_recv()
        ring(zl, 1 - c, up, up_s).start()
        ring(zl, 1 - c, down, down_s).start()

    @pl.when(other)
    def _():
        gout_out.start()
        tab_out.wait_recv()

    rt = tabr[0:nq, :]
    gt = tabr[nq : 2 * nq, :]
    slot = lax.broadcasted_iota(jnp.int32, (nq, SL, ntok), 1).astype(F32)
    hit = jnp.where(jnp.broadcast_to(rt[:, None, :], (nq, SL, ntok)) == slot, 1.0, 0.0)
    heavy = (hit * jnp.broadcast_to(gt[:, None, :], (nq, SL, ntok))).reshape(ns, ntok)
    top = heavy.astype(BF)
    pick[...] = hit.reshape(ns, ntok).astype(BF)
    wt[0] = top
    wt[1] = (heavy - top.astype(F32)).astype(BF)
    sg[...] = jnp.broadcast_to(jnp.sum(heavy, axis=1, keepdims=True), sg.shape)

    def row_local(t, g):
        return pltpu.make_async_copy(
            rows.at[t, g, slots(me)], xdy.at[t, g, slots(c * nq + me)], row_l.at[t, g]
        )

    def send_rows(t, g):
        @pl.loop(1, nq)
        def _(i):
            q = lax.rem(me + i, nq)
            remote(
                rows.at[t, g, slots(q)], xdy.at[t, g, slots(c * nq + me)],
                plane_s.at[t, g], plane_r.at[t, g], device(nx, q, z, c),
            ).start()

        row_local(t, g).start()

    def x_group(g):
        rows[0, g] = jnp.dot(pick[...], tok[g], preferred_element_type=F32).astype(BF)
        send_rows(0, g)

    def dy_group(g):
        rows[1, g] = (dot_t(pick[...], dyt[g]) * sg[:, 0:1]).astype(BF)
        send_rows(1, g)

    def ring_step(k, m):
        n = lax.rem(c + m, 2)
        ju = lax.rem(r - k + 8, 8)
        jd = lax.rem(r + k, 8)
        from_below = ju < 4
        from_above = jnp.logical_and(jd < 4, k < 4)

        @pl.when(from_below)
        def _():
            ring(ju, n, up, up_s).wait_recv()

            @pl.when(k < 4)
            def _():
                ring(ju, n, up, up_s).start()

        @pl.when(from_above)
        def _():
            ring(jd, n, down, down_s).wait_recv()

            @pl.when(k < 3)
            def _():
                ring(jd, n, down, down_s).start()

        @pl.when(jnp.logical_and(from_below, m == 1))
        def _():
            dy_group(ju)

        @pl.when(jnp.logical_and(from_above, m == 1))
        def _():
            dy_group(jd)

    @pl.when(own)
    def _():
        @pl.loop(0, 11)
        def _(n):
            @pl.when(n < 2)
            def _():
                x_group(n)

            @pl.when(jnp.logical_and(n > 3, n < 6))
            def _():
                x_group(n - 2)

            @pl.when(n == 6)
            def _():
                dy_group(zl)

            @pl.when(jnp.logical_and(n > 1, n < 4))
            def _():
                ring_step(1, n - 2)

            @pl.when(n > 6)
            def _():
                ring_step(2 + lax.div(n - 7, 2), lax.rem(n - 7, 2))

    @pl.when(other)
    def _():
        inside = min(7, -(-(pieces + 4 * SKEW - RING_FIRST) // RING_GAP))

        @pl.loop(SKEW, pieces + 4 * SKEW)
        def _(n):
            for h, far, who in ((0, r - 3, up), (1, 8 - r, down)):
                i = n - far * SKEW

                @pl.when(jnp.logical_and(i >= 0, i < pieces))
                def _():
                    piece(h, i, who).wait_recv()

                    @pl.when(far < 4)
                    def _():
                        piece(h, i, who).start()

            for h, far in ((0, r - 3), (1, 8 - r)):
                i = n - far * SKEW
                whole = lax.rem(i + 4 * ROWBLOCKS, ROWBLOCKS) == ROWBLOCKS - 1

                @pl.when(jnp.logical_and(jnp.logical_and(i >= 0, i < pieces), whole))
                def _():
                    x_group(2 * h + lax.div(i, ROWBLOCKS))

            at = n - RING_FIRST
            turn = lax.div(at, RING_GAP)

            @pl.when(jnp.logical_and(at >= 0, jnp.logical_and(turn < inside, lax.rem(at + 8 * RING_GAP, RING_GAP) == 0)))
            def _():
                ring_step(lax.div(turn, 2) + 1, lax.rem(turn, 2))

        @pl.loop(inside, 8)
        def _(turn):
            ring_step(lax.div(turn, 2) + 1, lax.rem(turn, 2))

    def share(t, g):
        return remote(xdy.at[t, g, mine], xdy.at[t, g, mine], share_s.at[t, g], share_r.at[t, g], sibling)

    def arrived(t, g):
        some = pl.ds(0, ns - SL)
        return remote(rows.at[t, g, some], xdy.at[t, g, some], plane_s.at[t, g], plane_r.at[t, g], sibling)

    def take_in(t):
        @pl.loop(0, 4)
        def _(g):
            arrived(t, g).wait_recv()
            row_local(t, g).wait()
            share(t, g).start()

    def to_sibling(t, f):
        return remote(so.at[t, f], rb.at[t, f], sib_s.at[t, f], sib_r.at[t, f], sibling)

    def back_local(t, g):
        return pltpu.make_async_copy(ob.at[t, g, slots(me)], rv.at[t, g, slots(me)], back_l.at[t, g])

    def back_arrived(t, g):
        some = pl.ds(0, ns - SL)
        return remote(ob.at[t, g, some], rv.at[t, g, some], back_s.at[t, g], back_r.at[t, g], sibling)

    def send_back(t, g):
        to_sibling(t, g).wait_recv()
        ob[t, g] = (ob[t, g].astype(F32) + rb[t, g].astype(F32)).astype(BF)

        @pl.loop(1, nq)
        def _(i):
            q = lax.rem(me + i, nq)
            remote(
                ob.at[t, g, slots(q)], rv.at[t, g, slots(me)],
                back_s.at[t, g], back_r.at[t, g], device(nx, q, z, c),
            ).start()

        back_local(t, g).start()

    def lanes(f):
        return slice(f * pair, (f + 1) * pair)

    take_in(0)
    weights[0].wait()
    weights[1].wait()
    gacc[...] = jnp.zeros_like(gacc)
    uacc[...] = jnp.zeros_like(uacc)

    @pl.loop(0, 4)
    def _(f):
        share(0, f).wait_recv()
        gacc[...] += jnp.dot(xdy[0, f], wg[f], preferred_element_type=F32)
        uacc[...] += jnp.dot(xdy[0, f], wu[f], preferred_element_type=F32)

    g = gacc[...]
    hb[...] = (g * jax.nn.sigmoid(g) * uacc[...]).astype(BF)
    weights[2].wait()
    for f in range(4):
        so[0, f] = jnp.dot(hb[theirs, :], wd[:, lanes(f)], preferred_element_type=F32).astype(BF)
        to_sibling(0, f).start()
        ob[0, f] = jnp.dot(hb[mine, :], wd[:, lanes(f)], preferred_element_type=F32).astype(BF)

    @pl.loop(0, 4)
    def _(f):
        send_back(0, f)

    def rows_of(n):
        return pl.ds(pl.multiple_of(n * part, SL), part)

    def send_down(t, j, n):
        return remote(
            tp.at[t, j, rows_of(n)], rsd.at[t, j, rows_of(n)], ring_s.at[t, j, n], down_r.at[t, j, n], down
        )

    def send_up(t, j, n):
        return remote(
            tp.at[t, j, rows_of(n)], rsu.at[t, j, rows_of(n)], ring_s.at[t, j, n], up_r.at[t, j, n], up
        )

    def add_in(t, j, n, a):
        tp[t, j, rows_of(n)] = (
            tp[t, j, rows_of(n)].astype(F32) + a[t, j, rows_of(n)].astype(F32)
        ).astype(BF)

    def pass_on(t, g, m):
        above = lax.rem(r - g + 8, 8)
        below = lax.rem(g - r + 8, 8)

        @pl.when(above == 4 - m)
        def _():
            @pl.loop(0, PARTS)
            def _(n):
                if m > 0:
                    send_down(t, g, n).wait_recv()
                    add_in(t, g, n, rsd)
                send_down(t, g, n).start()

        if m < 3:

            @pl.when(below == 3 - m)
            def _():
                @pl.loop(0, PARTS)
                def _(n):
                    if m > 0:
                        send_up(t, g, n).wait_recv()
                        add_in(t, g, n, rsu)
                    send_up(t, g, n).start()

    def return_step(n):
        for m in (3, 2, 1):
            at = n - m

            @pl.when(jnp.logical_and(at >= 0, at < 8))
            def _():
                pass_on(lax.div(at, 4), lax.rem(at, 4), m)

        @pl.when(n < 8)
        def _():
            t = lax.div(n, 4)
            g = lax.rem(n, 4)
            back_arrived(t, g).wait_recv()
            back_local(t, g).wait()

            @pl.when(t == 0)
            def _():
                tp[0, g] = (tdot(rv[0, g], wt[0]) + tdot(rv[0, g], wt[1])).astype(BF)

            @pl.when(t == 1)
            def _():
                tp[1, g] = tdot(rv[1, g], pick[...]).astype(BF)

            pass_on(t, g, 0)

    take_in(1)
    dacc[...] = jnp.zeros_like(dacc)
    for f in range(4):
        share(1, f).wait_recv()
        dacc[...] += dot_t(xdy[1, f], wd[:, lanes(f)])

    g = gacc[...]
    u = uacc[...]
    dh = dacc[...]
    sig = jax.nn.sigmoid(g)
    dgb[...] = (dh * u * sig * (1.0 + g * (1.0 - sig))).astype(BF)
    dub[...] = (dh * g * sig).astype(BF)
    prod = hb[...].astype(F32) * dh
    hi = prod.astype(BF)
    lo = (prod - hi.astype(F32)).astype(BF)
    ones = jnp.ones((8, prod.shape[1]), BF)
    scb[...] = (dot_t(ones, hi) + dot_t(ones, lo))[0:1, :]
    scr[pl.ds(d, 1)] = scb[...][None]

    @pl.loop(1, 8)
    def _(i):
        remote(scb, scr.at[d], dp_s, dp_r, {"expert": e, "dp": lax.rem(d + i, 8)}).start()

    @pl.loop(0, 4)
    def _(f):
        so[1, f] = (dot_t(dgb[theirs, :], wg[f]) + dot_t(dub[theirs, :], wu[f])).astype(BF)
        to_sibling(1, f).start()
        ob[1, f] = (dot_t(dgb[mine, :], wg[f]) + dot_t(dub[mine, :], wu[f])).astype(BF)

        @pl.when(f > 0)
        def _():
            send_back(1, f - 1)

        return_step(f)

    send_back(1, 3)

    seven = scr.at[pl.ds(0, 7)]
    dp_all = remote(seven, seven, dp_s, dp_r, sibling)
    dp_all.wait_recv()
    st[...] = jnp.sum(scr[...], axis=0)
    rsc[pl.ds(e, 1)] = st[...][None]

    @pl.loop(1, ne)
    def _(i):
        remote(st, rsc.at[e], ex_s, ex_r, {"expert": lax.rem(e + i, ne), "dp": d}).start()

    def final(t):
        return remote(fin.at[t], fo.at[t], fin_s.at[t], fin_r.at[t], sibling)

    def finish_own(t):
        @pl.loop(0, PARTS)
        def _(n):
            send_down(t, zl, n).wait_recv()
            send_up(t, zl, n).wait_recv()

        def summed(core):
            some = pl.ds(pl.multiple_of(core * ch, SL), ch)
            total = tp[t, zl, some].astype(F32) + rsd[t, zl, some].astype(F32)
            return (total + rsu[t, zl, some].astype(F32)).astype(BF)

        fin[t] = summed(1 - c)
        final(t).start()
        outs[t][...] = summed(c)

    results = [
        pltpu.make_async_copy(a, b, out_l.at[i])
        for i, (a, b) in enumerate(((wg, gwg_ref), (wu, gwu_ref), (wd, gwd_ref)))
    ]

    @pl.loop(4, 11)
    def _(n):
        return_step(n)

        @pl.when(n < 8)
        def _():
            f = n - 4
            some = pl.ds(pl.multiple_of(f * pair, 128), pair)
            wg[f] = tdot(xdy[0, f], dgb[...]).astype(BF)
            wu[f] = tdot(xdy[0, f], dub[...]).astype(BF)
            wd[:, some] = tdot(hb[...], xdy[1, f]).astype(BF)

        @pl.when(n == 8)
        def _():
            for o in results:
                o.start()

            @pl.when(own)
            def _():
                finish_own(0)

    @pl.when(own)
    def _():
        finish_own(1)
        for t in range(2):
            final(t).wait_send()

        tab_out.wait_send()

    @pl.when(other)
    def _():
        for t in range(2):
            final(t).wait_recv()
            outs[t][...] = fo[t]

        gout_out.wait_send()

    some = pl.ds(0, ne - 1)
    ex_all = remote(rsc.at[some], rsc.at[some], ex_s, ex_r, sibling)
    ex_all.wait_recv()
    rsc_ref[...] = rsc[...].reshape(ne, 2 * ns)
    ex_all.wait_send()
    dp_all.wait_send()
    for o in results:
        o.wait()

    @pl.loop(0, pieces)
    def _(i):
        @pl.when(jnp.logical_and(r >= 3, r < 7))
        def _():
            piece(0, i, up).wait_send()

        @pl.when(jnp.logical_or(r == 0, r > 4))
        def _():
            piece(1, i, down).wait_send()

    for t in range(2):

        @pl.loop(0, 4)
        def _(g):
            arrived(t, g).wait_send()
            share(t, g).wait_send()
            to_sibling(t, g).wait_send()
            back_arrived(t, g).wait_send()

            @pl.when(g != r)
            def _():
                @pl.loop(0, PARTS)
                def _(n):
                    send_down(t, g, n).wait_send()

    @pl.loop(0, 4)
    def _(j):
        @pl.when(lax.rem(r - j + 8, 8) < 4)
        def _():
            for n in range(2):
                ring(j, n, up, up_s).wait_send()

        @pl.when(lax.rem(j - r + 8, 8) < 3)
        def _():
            for n in range(2):
                ring(j, n, down, down_s).wait_send()


def moe(nx, nq, tokens, gout, ids, gates, tiles, wg, wu, wd):
    ntok = tokens.shape[0]
    ch = gout.shape[0]
    pair = 2 * ch
    ns = nq * SL
    fh = wg.shape[2]
    hbm = pl.BlockSpec(memory_space=pl.ANY)
    vm = pl.BlockSpec(memory_space=pltpu.VMEM)
    dma = pltpu.SemaphoreType.DMA
    s = jax.ShapeDtypeStruct
    v = pltpu.VMEM
    wide = v((2, 4, ns, pair), BF)
    tall = v((2, 4, pair, ntok), BF)
    each = dma((2, 4))
    parts = dma((2, 4, PARTS))
    return pl.pallas_call(
        functools.partial(moe_kernel, nx, nq),
        out_shape=(
            s((ch, ntok), BF), s((ch, ntok), BF), s((2 * nq, 2 * ns), F32),
            s(wg.shape, BF), s(wu.shape, BF), s(wd.shape, BF),
        ),
        in_specs=[hbm, hbm, vm, vm, vm, hbm, hbm, hbm],
        out_specs=(vm, vm, vm, hbm, hbm, hbm),
        scratch_shapes=[
            v((4, ntok, pair), BF), v((2, 2 * nq, ntok), F32), v((2 * nq, ntok), F32), v((4, pair, ntok), BF), wide,
            v((2, 4, 2 * ns, pair), BF), v((ns, ntok), BF), v((ns, 128), F32), v((2, ns, ntok), BF),
            v(wg.shape, BF), v(wu.shape, BF), v(wd.shape, BF),
            v((2 * ns, fh), F32), v((2 * ns, fh), F32), v((2 * ns, fh), F32),
            v((2 * ns, fh), BF), v((2 * ns, fh), BF), v((2 * ns, fh), BF), v((1, 2 * ns), F32),
            wide, wide, wide, wide, tall, tall, tall, v((2, ch, ntok), BF), v((2, ch, ntok), BF),
            v((8, 1, 2 * ns), F32), v((1, 2 * ns), F32), v((2 * nq, 1, 2 * ns), F32),
            dma((4,)), dma, dma((3,)), each, each, dma((3,)),
            dma, dma, dma, dma, dma((2, 2 * ROWBLOCKS)), dma((2, 2 * ROWBLOCKS)), dma((4, 2)), dma((4, 2)), dma((4, 2)),
            each, each, each, each, each, each, each, each,
            parts, parts, parts, dma((2,)), dma((2,)), dma, dma, dma, dma,
        ],
        compiler_params=pltpu.CompilerParams(
            collective_id=1, has_side_effects=True, vmem_limit_bytes=VMEM_LIMIT
        ),
        name="moe",
    )(tokens, gout, ids, gates, tiles, wg, wu, wd)


def finish_kernel(nx, nq, rsc_ref, ids_ref, gates_ref, tiles_ref, *refs):
    count = (len(refs) - 3) // 3
    given, gg_ref, made = refs[:count], refs[count], refs[count + 1 : 2 * count + 1]
    held, got, put = refs[2 * count + 1 : -2], refs[-2], refs[-1]
    loads, stores = [], []
    for i in range(count):
        step = given[i].shape[0] // 4
        for n in range(4):
            some = pl.ds(n * step, step)
            loads.append(pltpu.make_async_copy(given[i].at[some], held[i].at[some], got.at[i, n]))
            stores.append(pltpu.make_async_copy(held[i].at[some], made[i].at[some], put.at[i, n]))
    for copy in loads:
        copy.start()
    me, zh, _, _ = place(nx)
    ne = 2 * nq
    ids = ids_ref[...]
    names = lax.broadcasted_iota(jnp.int32, (ne, 1), 0)
    rank, gate = routing(ids, gates_ref[...], tiles_ref[0:1, 0:1], names)
    lane = lax.broadcasted_iota(jnp.int32, rsc_ref.shape, 1) - (zh * nq + me) * SL
    at = jnp.zeros(rank.shape, F32)
    for n in range(SL):
        score = jnp.sum(jnp.where(lane == n, rsc_ref[...], 0.0), axis=1, keepdims=True)
        at = at + jnp.where(rank == float(n), score, 0.0)
    named = rank >= 0.0
    at = jnp.where(named, at / jnp.where(named, gate, 1.0), 0.0)
    for k in range(ids.shape[0]):
        gg_ref[k : k + 1, :] = jnp.sum(jnp.where(ids[k : k + 1, :] == names, at, 0.0), axis=0, keepdims=True)
    for load, store in zip(loads, stores):
        load.wait()
        store.start()
    for store in stores:
        store.wait()


def finish(nx, nq, rsc, ids, gates, tiles, arrays):
    hbm = pl.BlockSpec(memory_space=pl.ANY)
    vm = pl.BlockSpec(memory_space=pltpu.VMEM)
    s = jax.ShapeDtypeStruct
    return pl.pallas_call(
        functools.partial(finish_kernel, nx, nq),
        out_shape=(s(ids.shape, F32), *(s(a.shape, a.dtype) for a in arrays)),
        in_specs=[vm] * 4 + [hbm] * len(arrays),
        out_specs=(vm, *([hbm] * len(arrays))),
        scratch_shapes=[
            *(pltpu.VMEM(a.shape, a.dtype) for a in arrays),
            pltpu.SemaphoreType.DMA((len(arrays), 4)), pltpu.SemaphoreType.DMA((len(arrays), 4)),
        ],
        compiler_params=pltpu.CompilerParams(vmem_limit_bytes=VMEM_LIMIT),
        name="finish",
    )(rsc, ids, gates, tiles, *arrays)


def on_device(nx, tokens, expert_ids, gate_values, tiles, w_gate, w_up, w_down, grad_out):
    nq = lax.axis_size("expert") // 2
    width = tokens.shape[1]
    pair = 2 * grad_out.shape[1]
    fh = w_gate.shape[2]
    ids = expert_ids.T
    gates = gate_values.T
    tiles = tiles.reshape(1, 1)
    wg = w_gate.reshape(4, pair, fh)
    wu = w_up.reshape(4, pair, fh)
    mixed, gtok, rsc, *grads = moe(nx, nq, tokens, grad_out.T, ids, gates, tiles, wg, wu, w_down[0])
    gg, mixed, gtok, gwg, gwu, gwd = finish(nx, nq, rsc, ids, gates, tiles, (mixed, gtok, *grads))
    return (
        mixed.T, gtok.T, gg.T,
        gwg.reshape(1, width, fh), gwu.reshape(1, width, fh), gwd[None],
    )


def build(mesh, nx):
    placed = (
        P("expert", None),
        P("expert", None),
        P("expert", None),
        P("expert"),
        P("expert", None, "dp"),
        P("expert", None, "dp"),
        P("expert", "dp", None),
        P("expert", "dp"),
    )
    return jax.shard_map(
        functools.partial(on_device, nx),
        mesh=mesh,
        in_specs=placed,
        out_specs=(
            P("expert", "dp"),
            P("expert", "dp"),
            P("expert", None),
            P("expert", None, "dp"),
            P("expert", None, "dp"),
            P("expert", "dp", None),
        ),
        check_vma=False,
    )


def solution(mesh):
    return build(mesh, 4)
```
